32 devices in a mesh: grp: 4 (over y, x), sub: 8 (over z, core).
Axes of the slice: x: 2, y: 2, z: 4, core: 2. Of those that a mesh axis runs over, the one named last changes fastest.
Arguments:
- right_side: float32 [24576, 160], P(('grp', 'sub')), may hold values from -6 to 6
- iterate_in: float32 [24576, 160], P(('grp', 'sub')), may hold values from -6 to 6
- diagonal: float32 [24576], P(('grp', 'sub')), may hold values from 1.5 to 4
- block_values: bfloat16 [32, 6, 3, 128, 128], P(('grp', 'sub')), may hold values from -0.125 to 0.125
- block_cols: int32 [32, 6, 3], P(('grp', 'sub')), may hold values from 0 to 5, as said below
- couple_left: bfloat16 [24576, 128], P(('grp', 'sub')), may hold values from -0.125 to 0.125
- couple_right: bfloat16 [24576, 128], P(('grp', 'sub')), may hold values from -0.125 to 0.125
- send_rows: int32 [32, 2, 128], P(('grp', 'sub')), may hold values from 0 to 767, as said below
- local_inverse: bfloat16 [32, 1024, 1024], P(('grp', 'sub')), may hold values from -0.3 to 2.3, as said below
- coarse_basis: bfloat16 [32, 1024, 32], P(('grp', 'sub')), may hold values from -0.1875 to 0.1875
- coarse_diag: float32 [32, 32, 32], P(('grp', 'sub')), may hold values from -54 to 59.5, as said below
- coarse_up: float32 [32, 32, 32], P(('grp', 'sub')), may hold values from -29.7 to 27
Outputs:
- iterate: float32 [24576, 160], P(('grp', 'sub'))
- residual: float32 [24576, 160], P(('grp', 'sub'))
The draws below stay inside these ranges and needn't reach their ends.
Inputs may be any that keep to these rules, and one draw needn't show every extreme that they name: `block_cols`: the 3 column blocks of one row block are distinct. `send_rows`: the 256 rows listed for one subdomain are distinct. `local_inverse`: each block is symmetric positive definite. `coarse_diag`: each block is symmetric; with coarse_up the coarse operator is symmetric positive definite.
All inputs are finite; a program needn't handle non-finite values.
Results may differ from the reference program's by a relative error of at most 0.0032.
Values may be sent and summed in bfloat16 or wider, within the bound.
No kernel may reach another device: no remote copies, remote signals or barrier semaphores. Data moves between devices by JAX's collectives and lax.ppermute only.
A program may use at most 64 MiB of HBM per device.

```python
import math
import jax
import jax.numpy as jnp
from jax import lax

ROWS = 768
CASES = 160
INTERSECTION = 128
BLOCK = 128
NONZEROS = 3
MODES = 32
ROW_BLOCKS = 6
EXTENDED = 1024
SUBDOMAINS = 32
UNKNOWNS = 24576


def draw_block_cols(key, part):
    keys = jax.random.split(jax.random.fold_in(key, 3), SUBDOMAINS * ROW_BLOCKS)

    def one_row(row_key):
        return jax.random.permutation(row_key, ROW_BLOCKS)[:NONZEROS]
    return jax.vmap(one_row)(keys).reshape(SUBDOMAINS, ROW_BLOCKS, NONZEROS).astype(jnp.int32)


def draw_send_rows(key, part):
    keys = jax.random.split(jax.random.fold_in(key, 5), SUBDOMAINS)

    def one_domain(domain_key):
        return jax.random.permutation(domain_key, ROWS)[:2 * INTERSECTION]
    return jax.vmap(one_domain)(keys).reshape(SUBDOMAINS, 2, INTERSECTION).astype(jnp.int32)


def draw_local_inverse(key, part):
    noise_key, diag_key = jax.random.split(jax.random.fold_in(key, 7))
    noise = jnp.clip(jax.random.normal(noise_key, (SUBDOMAINS, EXTENDED, EXTENDED), jnp.float32), -4.0, 4.0) * (0.25 / math.sqrt(EXTENDED))
    symmetric = noise + jnp.swapaxes(noise, 1, 2)
    low_end = 1.0
    diag_values = jax.random.uniform(diag_key, (SUBDOMAINS, EXTENDED, 1), jnp.float32, low_end, 2.0)
    return (symmetric + diag_values * jnp.eye(EXTENDED, dtype=jnp.float32)).astype(jnp.bfloat16)


def edge_couplings(key):
    strength_key, factor_key = jax.random.split(jax.random.fold_in(key, 11))
    root_three = math.sqrt(3.0)
    factor = jax.random.uniform(factor_key, (SUBDOMAINS, MODES, MODES), jnp.float32, -root_three, root_three)
    product = jnp.einsum('kab,kcb->kac', factor, factor, precision=jax.lax.Precision.HIGHEST) / MODES
    product = 0.5 * (product + jnp.swapaxes(product, 1, 2))
    strength = jnp.exp(jax.random.uniform(strength_key, (SUBDOMAINS, 1, 1), jnp.float32, math.log(3.0), math.log(9.0)))
    return strength * (0.3 * jnp.eye(MODES, dtype=jnp.float32) + product)


def draw_coarse_diag(key, part):
    coupling = edge_couplings(key)
    shift_key = jax.random.fold_in(key, 17)
    shift_low = 0.005
    shift_high = 0.02
    shifts = jnp.exp(jax.random.uniform(shift_key, (SUBDOMAINS, MODES, 1), jnp.float32, math.log(shift_low), math.log(shift_high)))
    inside = (jnp.arange(SUBDOMAINS) < SUBDOMAINS - 1).astype(jnp.float32)[:, None, None]
    own = coupling * inside
    previous = jnp.concatenate([jnp.zeros_like(coupling[:1]), own[:-1]], axis=0)
    return own + previous + shifts * jnp.eye(MODES, dtype=jnp.float32)


def draw_coarse_up(key, part):
    return -edge_couplings(key)


def levels(rng, extent, pieces, least, high):
    def one(dim, parts):
        heights = jax.random.uniform(jax.random.fold_in(jax.random.fold_in(rng, 6), dim), (parts,), jnp.float32, least / len(pieces), high / len(pieces))
        return jnp.repeat(jnp.exp(heights), extent[dim] // parts).reshape((-1,) + (1,) * (len(extent) - dim - 1))

    factor_of = one(*pieces[0])
    for cut in pieces[1:]:
        factor_of = factor_of * one(*cut)
    return factor_of


def centred(key, extent, deviation, limit, pieces=(), kind=jnp.bfloat16):
    entries = deviation * jax.random.normal(key, extent, jnp.float32)
    if pieces:
        entries = entries * levels(key, extent, pieces, -0.22, 0.18)
    return jnp.clip(entries, -limit, limit).astype(kind)


def setup_inputs(seed: int = 0) -> dict:
    splits = jax.random.split(jax.random.key(seed), 13)
    return {
        "right_side": centred(splits[0], (UNKNOWNS, CASES), 1.0, 6.0, ((0, 32),), jnp.float32),
        "iterate_in": centred(splits[1], (UNKNOWNS, CASES), 1.0, 6.0, ((0, 32),), jnp.float32),
        "diagonal": jnp.clip(jnp.exp(math.log(4.0) - 0.98082925 * jax.random.uniform(splits[2], (UNKNOWNS,), jnp.float32) ** levels(splits[2], (UNKNOWNS,), ((0, 32),), -0.2, 0.2)), 1.5, 4.0),
        "block_values": centred(splits[3], (SUBDOMAINS, ROW_BLOCKS, NONZEROS, BLOCK, BLOCK), (4 * (NONZEROS * BLOCK + 2 * INTERSECTION)) ** -0.5, 0.125, ((0, 32),)),
        "block_cols": draw_block_cols(jax.random.fold_in(splits[12], 71), 0),
        "couple_left": centred(splits[5], (UNKNOWNS, INTERSECTION), (4 * (NONZEROS * BLOCK + 2 * INTERSECTION)) ** -0.5, 0.125, ((0, 32),)),
        "couple_right": centred(splits[6], (UNKNOWNS, INTERSECTION), (4 * (NONZEROS * BLOCK + 2 * INTERSECTION)) ** -0.5, 0.125, ((0, 32),)),
        "send_rows": draw_send_rows(jax.random.fold_in(splits[12], 71), 0),
        "local_inverse": draw_local_inverse(jax.random.fold_in(splits[12], 71), 0),
        "coarse_basis": centred(splits[9], (SUBDOMAINS, EXTENDED, MODES), EXTENDED ** -0.5, 0.1875, ((0, 32),)),
        "coarse_diag": draw_coarse_diag(jax.random.fold_in(splits[12], 71), 0),
        "coarse_up": draw_coarse_up(jax.random.fold_in(splits[12], 71), 0),
    }


def chol_solve(factor, values):
    halfway = lax.linalg.triangular_solve(factor, values, left_side=True, lower=True)
    return lax.linalg.triangular_solve(factor, halfway, left_side=True, lower=True, transpose_a=True)

def solve_chain(diagonal_blocks, upper, values):
    highest = lax.Precision.HIGHEST
    width_up = upper.shape[2]
    first = jnp.linalg.cholesky(diagonal_blocks[0])

    def forward(state, entry):
        factor, reduced, coupling = state
        block_diag, block_up, block_rhs = entry
        through = chol_solve(factor, jnp.concatenate([coupling, reduced], axis=1))
        schur = block_diag - jnp.dot(coupling.T, through[:, :width_up], precision=highest)
        carried = block_rhs - jnp.dot(coupling.T, through[:, width_up:], precision=highest)
        new_factor = jnp.linalg.cholesky(schur)
        return ((new_factor, carried, block_up), (new_factor, carried))
    _, (factors, carried_all) = lax.scan(forward, (first, values[0], upper[0]), (diagonal_blocks[1:], upper[1:], values[1:]))
    factors = jnp.concatenate([first[None], factors], axis=0)
    carried_all = jnp.concatenate([values[0][None], carried_all], axis=0)
    final = chol_solve(factors[-1], carried_all[-1])

    def backward(later, entry):
        factor, reduced, coupling = entry
        current = chol_solve(factor, reduced - jnp.dot(coupling, later, precision=highest))
        return (current, current)
    _, earlier = lax.scan(backward, final, (factors[:-1], carried_all[:-1], upper[:-1]), reverse=True)
    return jnp.concatenate([earlier, final[None]], axis=0)

def pick_rows(values, indices):

    def chosen(source, index):
        return source[index]
    return jax.vmap(chosen)(values, indices)

def add_rows(values, indices, addend):

    def placed(source, index, extra):
        return source.at[index].add(extra)
    return jax.vmap(placed)(values, indices, addend)

def reference(right_side, iterate_in, diagonal, block_values, block_cols, couple_left, couple_right, send_rows, local_inverse, coarse_basis, coarse_diag, coarse_up):
    bf16 = jnp.bfloat16
    f32 = jnp.float32
    left_all = couple_left.reshape(SUBDOMAINS, ROWS, INTERSECTION)
    right_all = couple_right.reshape(SUBDOMAINS, ROWS, INTERSECTION)
    diag_all = diagonal.reshape(SUBDOMAINS, ROWS, 1)

    def neighbours(rounded):
        sent_right = pick_rows(rounded, send_rows[:, 1])
        sent_left = pick_rows(rounded, send_rows[:, 0])
        nothing = jnp.zeros_like(sent_right[:1])
        from_left = jnp.concatenate([nothing, sent_right[:-1]], axis=0)
        from_right = jnp.concatenate([sent_left[1:], nothing], axis=0)
        return (from_left, from_right)

    def apply_operator(vector):
        rounded = vector.astype(bf16)
        from_left, from_right = neighbours(rounded)

        def one_domain(entry):
            values_here, cols_here, rows_here, left_here, right_here, left_coupling, right_coupling = entry
            blocks = rows_here.reshape(ROW_BLOCKS, BLOCK, CASES)
            picked = blocks[cols_here]
            sparse = jnp.einsum('itab,itbn->ian', values_here.astype(f32), picked.astype(f32)).reshape(ROWS, CASES)
            coupled = jnp.dot(left_coupling, left_here, preferred_element_type=f32) + jnp.dot(right_coupling, right_here, preferred_element_type=f32)
            return sparse + coupled
        offdiag = lax.map(one_domain, (block_values, block_cols, rounded, from_left, from_right, left_all, right_all))
        return diag_all * vector + offdiag

    def precondition(residual_in):
        rounded = residual_in.astype(bf16)
        from_left, from_right = neighbours(rounded)
        extended = jnp.concatenate([from_left, rounded, from_right], axis=1)

        def local_step(entry):
            inverse, basis, margin = entry
            return (jnp.dot(inverse, margin, preferred_element_type=f32), jnp.dot(basis.T, margin, preferred_element_type=f32))
        local_part, coarse_in = lax.map(local_step, (local_inverse, coarse_basis, extended))
        coarse_sol = solve_chain(coarse_diag, coarse_up, coarse_in)

        def lift(entry):
            basis, solution = entry
            return jnp.dot(basis, solution.astype(bf16), preferred_element_type=f32)
        correction = local_part + lax.map(lift, (coarse_basis, coarse_sol))
        owned = correction[:, INTERSECTION:INTERSECTION + ROWS]
        nothing = jnp.zeros_like(correction[:1, :INTERSECTION])
        from_next = jnp.concatenate([correction[1:, :INTERSECTION], nothing], axis=0)
        from_prev = jnp.concatenate([nothing, correction[:-1, INTERSECTION + ROWS:]], axis=0)
        owned = add_rows(owned, send_rows[:, 1], from_next)
        owned = add_rows(owned, send_rows[:, 0], from_prev)
        return owned
    loads = right_side.reshape(SUBDOMAINS, ROWS, CASES)
    start = iterate_in.reshape(SUBDOMAINS, ROWS, CASES)
    residual_start = loads - apply_operator(start)
    precond = precondition(residual_start)
    inner = jnp.sum(residual_start * precond, axis=(0, 1))
    image = apply_operator(precond)
    curvature = jnp.sum(precond * image, axis=(0, 1))
    step_size = inner / curvature
    iterate = start + step_size * precond
    residual = residual_start - step_size * image
    return (iterate.reshape(UNKNOWNS, CASES), residual.reshape(UNKNOWNS, CASES))
```

```python
import functools

import jax
import jax.numpy as jnp
from jax import lax
from jax.experimental import pallas as pl
from jax.experimental.pallas import tpu as pltpu
from jax.sharding import PartitionSpec as P

AXES = ("grp", "sub")
BF16 = jnp.bfloat16
F32 = jnp.float32
VMEM = pl.BlockSpec(memory_space=pltpu.VMEM)
SMEM = pl.BlockSpec(memory_space=pltpu.SMEM)


def mm(a, b):
    return jnp.dot(a, b, preferred_element_type=F32)


def mm_t(a, b, **kw):
    return lax.dot_general(a, b, (((0,), (0,)), ((), ())), preferred_element_type=F32, **kw)


def position():
    return lax.axis_index("grp") * lax.axis_size("sub") + lax.axis_index("sub")


def is_even():
    return position() % 2 == 0


def column_index(row):
    return jnp.transpose(jnp.broadcast_to(row, (row.shape[1], row.shape[1])))


def pick_matrix(row, total):
    column = column_index(row)
    width = column.shape[1]
    lane = lax.broadcasted_iota(jnp.int32, column.shape, 1)
    parts = [(column == lane + c * width).astype(F32).astype(BF16) for c in range(total // width)]
    return jnp.concatenate(parts, axis=1)


def place_matrix(row, total):
    place = lax.broadcasted_iota(jnp.int32, (total, row.shape[1]), 0)
    return (place == row).astype(F32).astype(BF16)


def gather_kernel(x_ref, rows_ref, to_pair_ref, to_other_ref):
    values = x_ref[...].astype(BF16)
    left, right = rows_ref[0, 0:1, :], rows_ref[0, 1:2, :]
    even = is_even()
    pair_rows = jnp.where(even, right, left)
    other_rows = jnp.where(even, left, right)
    to_pair_ref[...] = mm(pick_matrix(pair_rows, values.shape[0]), values).astype(BF16)
    to_other_ref[...] = mm(pick_matrix(other_rows, values.shape[0]), values).astype(BF16)


def times_operator(x, rounded_ref, left, right, diag_ref, values_ref, cols_ref, cl_ref, cr_ref, finish):
    blocks, nonzeros, size = values_ref.shape[1], values_ref.shape[2], values_ref.shape[3]
    for i in range(blocks):
        span = slice(i * size, (i + 1) * size)
        total = mm(cl_ref[span, :], left) + mm(cr_ref[span, :], right)
        for t in range(nonzeros):
            start = pl.multiple_of(cols_ref[0, i, t] * size, size)
            total = total + mm(values_ref[0, i, t], rounded_ref[pl.ds(start, size), :])
        column = jnp.transpose(jnp.broadcast_to(diag_ref[0:1, span], (size, size)))
        cases = x.shape[1]
        wide = jnp.concatenate([column] * pl.cdiv(cases, size), axis=1)[:, :cases]
        finish(span, wide * x[span, :] + total)


def residual_kernel(b_ref, x_ref, diag_ref, values_ref, cols_ref, cl_ref, cr_ref, rows_ref, pair_ref, other_ref,
                    r_ref, rb_ref, to_pair_ref, to_other_ref, xb_ref):
    x = x_ref[...]
    xb_ref[...] = x.astype(BF16)
    even = is_even()
    left = jnp.where(even, other_ref[...], pair_ref[...])
    right = jnp.where(even, pair_ref[...], other_ref[...])

    def finish(span, image):
        r = b_ref[span, :] - image
        r_ref[span, :] = r
        rb_ref[span, :] = r.astype(BF16)

    times_operator(x, xb_ref, left, right, diag_ref, values_ref, cols_ref, cl_ref, cr_ref, finish)
    values = rb_ref[...]
    row_left, row_right = rows_ref[0, 0:1, :], rows_ref[0, 1:2, :]
    pair_rows = jnp.where(even, row_right, row_left)
    other_rows = jnp.where(even, row_left, row_right)
    to_pair_ref[...] = mm(pick_matrix(pair_rows, values.shape[0]), values).astype(BF16)
    to_other_ref[...] = mm(pick_matrix(other_rows, values.shape[0]), values).astype(BF16)


def local_kernel(inverse_ref, basis_ref, diag_ref, up_ref, rb_ref, pair_ref, other_ref, local_ref, message_ref):
    even = is_even()
    left = jnp.where(even, other_ref[...], pair_ref[...])
    right = jnp.where(even, pair_ref[...], other_ref[...])
    extended = jnp.concatenate([left, rb_ref[...], right], axis=0)
    local_ref[...] = mm(inverse_ref[0], extended)
    coarse_in = mm_t(basis_ref[0], extended)
    last = position() == lax.axis_size("grp") * lax.axis_size("sub") - 1
    up = jnp.where(last, 0.0, up_ref[0])
    message = jnp.concatenate([diag_ref[0], jnp.transpose(up), up, coarse_in], axis=1)
    for slot in range(message_ref.shape[0]):
        message_ref[slot] = message


def reduce_rows(blocks):
    size = blocks[0].shape[0]
    here = lax.broadcasted_iota(jnp.int32, (size, 1), 0)
    for p in range(size):
        done = []
        for block in blocks:
            row = block[p:p + 1, :] / block[p:p + 1, p:p + 1]
            done.append(jnp.where(here == p, row, block - block[:, p:p + 1] * row))
        blocks = done
    return blocks


def schur(block, solved, size):
    width = solved.shape[1]
    product = -mm_t(block[:, :4 * size], solved, precision=lax.Precision.HIGHEST)
    top, bottom = product[size:2 * size], product[2 * size:3 * size]
    zero = jnp.zeros((size, size), F32)
    to_left = jnp.concatenate([top[:, size:2 * size], zero, top[:, 2 * size:]], axis=1)
    to_right = jnp.concatenate([bottom[:, 2 * size:3 * size], bottom[:, size:2 * size], zero, bottom[:, 3 * size:]], axis=1)
    return to_left, to_right


def own_part(block, size):
    lane = lax.broadcasted_iota(jnp.int32, block.shape, 1)
    return jnp.where((lane >= size) & (lane < 3 * size), 0.0, block)


def eliminate(chain, size, keep):
    count = len(chain) - 1
    step = 1
    while step < count:
        inner = list(range(step, count, 2 * step))
        solved = dict(zip(inner, reduce_rows([chain[j] for j in inner])))
        parts = {j: schur(chain[j], solved[j], size) for j in inner}
        for j in inner:
            keep(j, solved[j])
        for i in range(0, count + 1, 2 * step):
            total = own_part(chain[i], size)
            if i + step in parts:
                total = total + parts[i + step][0]
            if i - step in parts:
                total = total + parts[i - step][1]
            chain[i] = total
        step = 2 * step
    return chain[0], chain[count]


def back(solved, left, right, size):
    zero = jnp.zeros_like(left)
    stacked = jnp.concatenate([zero, left, right, zero], axis=0)
    return solved[:, 3 * size:] - jnp.dot(
        solved[:, :4 * size], stacked, precision=lax.Precision.HIGHEST, preferred_element_type=F32)


def padded(count):
    total = 1
    while total < count:
        total = 2 * total
    return total


def chain_of(blocks, size):
    width = blocks[0].shape[1]
    lane = lax.broadcasted_iota(jnp.int32, (size, width), 1)
    row = lax.broadcasted_iota(jnp.int32, (size, width), 0)
    from_previous = (lane >= size) & (lane < 2 * size)
    own = [jnp.where(from_previous, 0.0, block) for block in blocks]
    chain = [own[0]]
    for j in range(1, len(blocks)):
        chain.append(jnp.where(from_previous, blocks[j - 1], blocks[j]))
    return chain, from_previous, (lane == row).astype(F32)


def group_kernel(gathered_ref, solved_ref, message_ref):
    members, size, width = gathered_ref.shape
    blocks = [gathered_ref[j] for j in range(members)]
    chain, from_previous, identity = chain_of(blocks, size)
    tail = jnp.where(from_previous, blocks[members - 1], 0.0)
    total = padded(members)
    if total > members:
        raise NotImplementedError("members")
    chain.append(tail)

    def keep(j, solved):
        solved_ref[j] = solved

    head, tail = eliminate(chain, size, keep)
    message_ref[:size, :] = head
    message_ref[size:, :] = tail


def solve_kernel(reduced_ref, solved_ref, local_ref, basis_ref, rows_ref,
                 corr_ref, to_pair_ref, to_other_ref, sep_ref, x_ref, own_ref):
    groups, two_size, width = reduced_ref.shape
    size = two_size // 2
    members = solved_ref.shape[0]
    chain = []
    for g in range(groups):
        total = reduced_ref[g, :size, :]
        if g:
            total = total + reduced_ref[g - 1, size:, :]
        chain.append(total)
    count = padded(groups)
    row = lax.broadcasted_iota(jnp.int32, (size, width), 0)
    lane = lax.broadcasted_iota(jnp.int32, (size, width), 1)
    while len(chain) < count:
        chain.append((row == lane).astype(F32))
    chain.append(jnp.zeros((size, width), F32))
    factors = {}
    head, _ = eliminate(chain, size, factors.__setitem__)
    solution = {count: jnp.zeros((size, width - 3 * size), F32)}
    solution[0] = reduce_rows([head])[0][:, 3 * size:]
    step = count // 2
    while step >= 1:
        for j in range(step, count, 2 * step):
            solution[j] = back(factors[j], solution[j - step], solution[j + step], size)
        step = step // 2
    for g in range(groups):
        sep_ref[g] = solution[g]
    sep_ref[groups] = jnp.zeros((size, width - 3 * size), F32)
    group, member = lax.axis_index("grp"), lax.axis_index("sub")
    x_ref[0] = sep_ref[group]
    x_ref[members] = sep_ref[group + 1]
    step = members // 2
    while step >= 2:
        for j in range(step, members, 2 * step):
            x_ref[j] = back(solved_ref[j], x_ref[j - step], x_ref[j + step], size)
        step = step // 2
    odd = member // 2 * 2 + 1
    x_ref[odd] = back(solved_ref[odd], x_ref[odd - 1], x_ref[odd + 1], size)
    coarse = x_ref[member].astype(BF16)
    correction = local_ref[...] + mm(basis_ref[0], coarse)
    corr_ref[...] = correction
    margin = rows_ref.shape[2]
    owned = correction.shape[0] - 2 * margin
    rounded = correction.astype(BF16)
    even = is_even()
    head, tail = rounded[:margin], rounded[margin + owned:]
    values = rounded[margin:margin + owned]
    row_left, row_right = rows_ref[0, 0:1, :], rows_ref[0, 1:2, :]
    pair_rows = jnp.where(even, row_right, row_left)
    other_rows = jnp.where(even, row_left, row_right)
    to_pair_ref[:margin, :] = jnp.where(even, tail, head)
    to_other_ref[:margin, :] = jnp.where(even, head, tail)
    to_pair_ref[margin:, :] = mm(pick_matrix(pair_rows, owned), values).astype(BF16)
    to_other_ref[margin:, :] = mm(pick_matrix(other_rows, owned), values).astype(BF16)


def image_kernel(corr_ref, r_ref, diag_ref, values_ref, cols_ref, cl_ref, cr_ref, rows_ref, pair_ref, other_ref,
                 p_ref, image_ref, sums_ref, pb_ref):
    margin = rows_ref.shape[2]
    owned = p_ref.shape[0]
    even = is_even()
    from_left = jnp.where(even, other_ref[...], pair_ref[...])
    from_right = jnp.where(even, pair_ref[...], other_ref[...])
    place = jnp.concatenate(
        [place_matrix(rows_ref[0, 0:1, :], owned), place_matrix(rows_ref[0, 1:2, :], owned)], axis=1)
    tails = jnp.concatenate([from_left[:margin], from_right[:margin]], axis=0)
    p = corr_ref[margin:margin + owned, :] + mm(place, tails)
    p_ref[...] = p
    pb_ref[...] = p.astype(BF16)
    me = position()
    last = lax.axis_size("grp") * lax.axis_size("sub") - 1
    left = from_left[margin:].astype(F32) + corr_ref[:margin, :]
    right = from_right[margin:].astype(F32) + corr_ref[margin + owned:, :]
    left = jnp.where(me == 0, 0.0, left).astype(BF16)
    right = jnp.where(me == last, 0.0, right).astype(BF16)

    def finish(span, image):
        image_ref[span, :] = image

    times_operator(p, pb_ref, left, right, diag_ref, values_ref, cols_ref, cl_ref, cr_ref, finish)
    inner = jnp.sum(r_ref[...] * p, axis=0, keepdims=True)
    curvature = jnp.sum(p * image_ref[...], axis=0, keepdims=True)
    sums = jnp.concatenate([inner, curvature], axis=0)
    for slot in range(sums_ref.shape[0]):
        sums_ref[slot] = sums


def finish_kernel(x_ref, p_ref, r_ref, image_ref, sums_ref, out_x_ref, out_r_ref):
    sums = jnp.sum(sums_ref[...], axis=0)
    step = sums[0:1, :] / sums[1:2, :]
    out_x_ref[...] = x_ref[...] + step * p_ref[...]
    out_r_ref[...] = r_ref[...] - step * image_ref[...]


def call(kernel, out, in_specs, scratch=()):
    many = isinstance(out, (list, tuple))
    return pl.pallas_call(
        kernel,
        out_shape=out,
        in_specs=in_specs,
        out_specs=[VMEM] * len(out) if many else VMEM,
        scratch_shapes=list(scratch),
        name=kernel.__name__,
    )


def struct(shape, dtype):
    return jax.ShapeDtypeStruct(shape, dtype)


def shards(right_side, iterate_in, diagonal, block_values, block_cols, couple_left, couple_right, send_rows,
           local_inverse, coarse_basis, coarse_diag, coarse_up):
    groups, members = lax.axis_size("grp"), lax.axis_size("sub")
    total = groups * members
    rows, cases = right_side.shape
    margin = send_rows.shape[2]
    extended = local_inverse.shape[1]
    modes = coarse_basis.shape[2]
    width = 3 * modes + cases
    pairs = [(i, i ^ 1) for i in range(total)]
    others = [(i, i + 1 if i % 2 else i - 1) for i in range(1, total - 1)]
    diag = diagonal.reshape(1, rows)

    def swap(to_pair, to_other):
        return lax.ppermute(to_pair, AXES, pairs), lax.ppermute(to_other, AXES, others)

    halo = struct((margin, cases), BF16)
    full = struct((rows, cases), F32)
    operator = (diag, block_values, block_cols, couple_left, couple_right, send_rows)
    operator_specs = [VMEM, VMEM, SMEM, VMEM, VMEM, VMEM]
    sent = call(gather_kernel, [halo, halo], [VMEM] * 2)(iterate_in, send_rows)
    got = swap(*sent)
    residual, rounded, *sent = call(
        residual_kernel,
        [full, struct((rows, cases), BF16), halo, halo],
        [VMEM, VMEM] + operator_specs + [VMEM, VMEM],
        [pltpu.VMEM((rows, cases), BF16)],
    )(right_side, iterate_in, *operator, *got)
    got = swap(*sent)
    local, message = call(
        local_kernel, [struct((extended, cases), F32), struct((members, modes, width), F32)], [VMEM] * 7
    )(local_inverse, coarse_basis, coarse_diag, coarse_up, rounded, *got)
    gathered = lax.all_to_all(message, "sub", 0, 0, tiled=True)
    solved, reduced = call(
        group_kernel, [struct((members, modes, width), F32), struct((2 * modes, width), F32)], [VMEM]
    )(gathered)
    reduced = lax.all_gather(reduced, "grp", axis=0)
    correction, *sent = call(
        solve_kernel,
        [struct((extended, cases), F32)] + [struct((2 * margin, cases), BF16)] * 2,
        [VMEM] * 5,
        [
            pltpu.VMEM((groups + 1, modes, cases), F32),
            pltpu.VMEM((members + 1, modes, cases), F32),
            pltpu.VMEM((8, 128), F32),
        ],
    )(reduced, solved, local, coarse_basis, send_rows)
    got = swap(*sent)
    direction, image, sums = call(
        image_kernel,
        [full, full, struct((total, 2, cases), F32)],
        [VMEM, VMEM] + operator_specs + [VMEM, VMEM],
        [pltpu.VMEM((rows, cases), BF16)],
    )(correction, residual, *operator, *got)
    sums = lax.all_to_all(sums, AXES, 0, 0, tiled=True)
    return tuple(
        call(finish_kernel, [full, full], [VMEM] * 5)(iterate_in, direction, residual, image, sums)
    )


def solution(mesh):
    whole = P(AXES)

    def spec(rank):
        return P(AXES, *([None] * (rank - 1)))

    return jax.shard_map(
        shards,
        mesh=mesh,
        in_specs=tuple(spec(rank) for rank in (2, 2, 1, 5, 3, 2, 2, 3, 3, 3, 3, 3)),
        out_specs=(spec(2), spec(2)),
        check_vma=False,
    )
```

```python
import functools

import jax
import jax.numpy as jnp
from jax import lax
from jax.experimental import pallas as pl
from jax.experimental.pallas import tpu as pltpu
from jax.sharding import PartitionSpec as P

AXES = ("grp", "sub")
BF16 = jnp.bfloat16
F32 = jnp.float32
VMEM = pl.BlockSpec(memory_space=pltpu.VMEM)
SMEM = pl.BlockSpec(memory_space=pltpu.SMEM)


def mm(a, b):
    return jnp.dot(a, b, preferred_element_type=F32)


def mm_t(a, b, **kw):
    return lax.dot_general(a, b, (((0,), (0,)), ((), ())), preferred_element_type=F32, **kw)


def mm_nt(a, b, **kw):
    return lax.dot_general(a, b, (((1,), (1,)), ((), ())), preferred_element_type=F32, **kw)


def position():
    return lax.axis_index("grp") * lax.axis_size("sub") + lax.axis_index("sub")


def is_even():
    return position() % 2 == 0


def place_matrix(row, total):
    place = lax.broadcasted_iota(jnp.int32, (total, row.shape[1]), 0)
    return (place == row).astype(F32).astype(BF16)


def send_matrix(rows_ref, total):
    left, right = rows_ref[0, 0:1, :], rows_ref[0, 1:2, :]
    even = is_even()
    rows = jnp.concatenate([jnp.where(even, right, left), jnp.where(even, left, right)], axis=1)
    return place_matrix(rows, total)


def from_sides(pair_ref, other_ref):
    even = is_even()
    pair, other = pair_ref[...], other_ref[...]
    return jnp.where(even, other, pair), jnp.where(even, pair, other)


def gather_kernel(x_ref, rows_ref, to_pair_ref, to_other_ref):
    values = x_ref[...].astype(BF16)
    margin = rows_ref.shape[2]
    sent = mm(values, send_matrix(rows_ref, values.shape[1])).astype(BF16)
    to_pair_ref[...] = sent[:, :margin]
    to_other_ref[...] = sent[:, margin:]


def times_operator(x, rounded_ref, left, right, diag_ref, values_ref, cols_ref, cl_ref, cr_ref, finish):
    blocks, nonzeros, size = values_ref.shape[1], values_ref.shape[2], values_ref.shape[3]
    diag = diag_ref[...].reshape(1, x.shape[1])
    for i in range(blocks):
        span = slice(i * size, (i + 1) * size)
        total = mm_nt(left, cl_ref[span, :]) + mm_nt(right, cr_ref[span, :])
        for t in range(nonzeros):
            start = pl.multiple_of(cols_ref[t, 0, i] * size, size)
            total = total + mm_nt(rounded_ref[:, pl.ds(start, size)], values_ref[0, i, t])
        finish(span, diag[:, span] * x[:, span] + total)


def residual_kernel(b_ref, x_ref, diag_ref, values_ref, cols_ref, cl_ref, cr_ref, rows_ref, pair_ref, other_ref,
                    r_ref, rb_ref, to_pair_ref, to_other_ref, xb_ref):
    x = x_ref[...]
    xb_ref[...] = x.astype(BF16)
    left, right = from_sides(pair_ref, other_ref)

    def finish(span, image):
        r = b_ref[:, span] - image
        r_ref[:, span] = r
        rb_ref[:, span] = r.astype(BF16)

    times_operator(x, xb_ref, left, right, diag_ref, values_ref, cols_ref, cl_ref, cr_ref, finish)
    margin = rows_ref.shape[2]
    sent = mm(rb_ref[...], send_matrix(rows_ref, x.shape[1])).astype(BF16)
    to_pair_ref[...] = sent[:, :margin]
    to_other_ref[...] = sent[:, margin:]


def local_kernel(inverse_ref, basis_ref, diag_ref, up_ref, rb_ref, pair_ref, other_ref, local_ref, message_ref):
    left, right = from_sides(pair_ref, other_ref)
    extended = jnp.concatenate([left, rb_ref[...], right], axis=1)
    local_ref[...] = mm(extended, inverse_ref[0])
    coarse_in = mm_nt(basis_ref[0], extended)
    last = position() == lax.axis_size("grp") * lax.axis_size("sub") - 1
    up = jnp.where(last, 0.0, up_ref[0])
    message = jnp.concatenate([diag_ref[0], jnp.transpose(up), up, coarse_in], axis=1)
    for slot in range(message_ref.shape[0]):
        message_ref[slot] = message


def reduce_rows(blocks):
    size, width = blocks[0].shape
    panel = 8 if len(blocks) <= 2 else 4
    lanes = 128
    here = lax.broadcasted_iota(jnp.int32, (size, 1), 0)

    def wide(value):
        return jnp.concatenate([value] * (width // lanes), axis=1)

    for first in range(0, size, panel):
        panels = [
            [jnp.broadcast_to(block[:, q:q + 1], (size, lanes)) for q in range(first, first + panel)] for block in blocks
        ]
        for a in range(panel):
            p = first + a
            done = []
            for block, columns in zip(blocks, panels):
                column = columns[a]
                inverse = 1.0 / column[p:p + 1, :]
                for b in range(a + 1, panel):
                    entry = columns[b][p:p + 1, :] * inverse
                    columns[b] = jnp.where(here == p, entry, columns[b] - column * entry)
                row = block[p:p + 1, :] * wide(inverse)
                done.append(jnp.where(here == p, row, block - wide(column) * row))
            blocks = done
    return blocks


def schur(block, solved, size):
    width = solved.shape[1]
    product = -mm_t(block[:, :4 * size], solved, precision=lax.Precision.HIGHEST)
    top, bottom = product[size:2 * size], product[2 * size:3 * size]
    zero = jnp.zeros((size, size), F32)
    to_left = jnp.concatenate([top[:, size:2 * size], zero, top[:, 2 * size:]], axis=1)
    to_right = jnp.concatenate([bottom[:, 2 * size:3 * size], bottom[:, size:2 * size], zero, bottom[:, 3 * size:]], axis=1)
    return to_left, to_right


def own_part(block, size):
    lane = lax.broadcasted_iota(jnp.int32, block.shape, 1)
    return jnp.where((lane >= size) & (lane < 3 * size), 0.0, block)


def eliminate(chain, size, keep):
    count = len(chain) - 1
    step = 1
    while step < count:
        inner = list(range(step, count, 2 * step))
        solved = dict(zip(inner, reduce_rows([chain[j] for j in inner])))
        parts = {j: schur(chain[j], solved[j], size) for j in inner}
        for j in inner:
            keep(j, solved[j])
        for i in range(0, count + 1, 2 * step):
            total = own_part(chain[i], size)
            if i + step in parts:
                total = total + parts[i + step][0]
            if i - step in parts:
                total = total + parts[i - step][1]
            chain[i] = total
        step = 2 * step
    return chain[0], chain[count]


def back(solved, left, right, size):
    zero = jnp.zeros_like(left)
    stacked = jnp.concatenate([zero, left, right, zero], axis=0)
    return solved[:, 3 * size:] - jnp.dot(
        solved[:, :4 * size], stacked, precision=lax.Precision.HIGHEST, preferred_element_type=F32)


def padded(count):
    total = 1
    while total < count:
        total = 2 * total
    return total


def chain_of(blocks, size):
    width = blocks[0].shape[1]
    lane = lax.broadcasted_iota(jnp.int32, (size, width), 1)
    row = lax.broadcasted_iota(jnp.int32, (size, width), 0)
    from_previous = (lane >= size) & (lane < 2 * size)
    own = [jnp.where(from_previous, 0.0, block) for block in blocks]
    chain = [own[0]]
    for j in range(1, len(blocks)):
        chain.append(jnp.where(from_previous, blocks[j - 1], blocks[j]))
    return chain, from_previous, (lane == row).astype(F32)


def group_kernel(gathered_ref, solved_ref, message_ref):
    members, size, width = gathered_ref.shape
    blocks = [gathered_ref[j] for j in range(members)]
    chain, from_previous, identity = chain_of(blocks, size)
    tail = jnp.where(from_previous, blocks[members - 1], 0.0)
    total = padded(members)
    if total > members:
        raise NotImplementedError("members")
    chain.append(tail)

    def keep(j, solved):
        solved_ref[j] = solved

    head, tail = eliminate(chain, size, keep)
    message_ref[:size, :] = head
    message_ref[size:, :] = tail


def solve_kernel(reduced_ref, solved_ref, local_ref, basis_ref, rows_ref,
                 corr_ref, to_pair_ref, to_other_ref, sep_ref, x_ref, own_ref):
    groups, two_size, width = reduced_ref.shape
    size = two_size // 2
    members = solved_ref.shape[0]
    chain = []
    for g in range(groups):
        total = reduced_ref[g, :size, :]
        if g:
            total = total + reduced_ref[g - 1, size:, :]
        chain.append(total)
    count = padded(groups)
    row = lax.broadcasted_iota(jnp.int32, (size, width), 0)
    lane = lax.broadcasted_iota(jnp.int32, (size, width), 1)
    while len(chain) < count:
        chain.append((row == lane).astype(F32))
    chain.append(jnp.zeros((size, width), F32))
    factors = {}
    head, _ = eliminate(chain, size, factors.__setitem__)
    solution = {count: jnp.zeros((size, width - 3 * size), F32)}
    solution[0] = reduce_rows([head])[0][:, 3 * size:]
    step = count // 2
    while step >= 1:
        for j in range(step, count, 2 * step):
            solution[j] = back(factors[j], solution[j - step], solution[j + step], size)
        step = step // 2
    for g in range(groups):
        sep_ref[g] = solution[g]
    sep_ref[groups] = jnp.zeros((size, width - 3 * size), F32)
    group, member = lax.axis_index("grp"), lax.axis_index("sub")
    x_ref[0] = sep_ref[group]
    x_ref[members] = sep_ref[group + 1]
    step = members // 2
    while step >= 2:
        for j in range(step, members, 2 * step):
            x_ref[j] = back(solved_ref[j], x_ref[j - step], x_ref[j + step], size)
        step = step // 2
    odd = member // 2 * 2 + 1
    x_ref[odd] = back(solved_ref[odd], x_ref[odd - 1], x_ref[odd + 1], size)
    coarse = x_ref[member].astype(BF16)
    correction = local_ref[...] + mm_t(coarse, basis_ref[0])
    corr_ref[...] = correction
    margin = rows_ref.shape[2]
    owned = correction.shape[1] - 2 * margin
    rounded = correction.astype(BF16)
    even = is_even()
    head, tail = rounded[:, :margin], rounded[:, margin + owned:]
    sent = mm(rounded[:, margin:margin + owned], send_matrix(rows_ref, owned)).astype(BF16)
    to_pair_ref[:, :margin] = jnp.where(even, tail, head)
    to_other_ref[:, :margin] = jnp.where(even, head, tail)
    to_pair_ref[:, margin:] = sent[:, :margin]
    to_other_ref[:, margin:] = sent[:, margin:]


def image_kernel(corr_ref, r_ref, diag_ref, values_ref, cols_ref, cl_ref, cr_ref, rows_ref, pair_ref, other_ref,
                 p_ref, image_ref, sums_ref, pb_ref):
    margin = rows_ref.shape[2]
    owned = p_ref.shape[1]
    from_left, from_right = from_sides(pair_ref, other_ref)
    place = place_matrix(jnp.concatenate([rows_ref[0, 0:1, :], rows_ref[0, 1:2, :]], axis=1), owned)
    tails = jnp.concatenate([from_left[:, :margin], from_right[:, :margin]], axis=1)
    p = corr_ref[:, margin:margin + owned] + mm_nt(tails, place)
    p_ref[...] = p
    pb_ref[...] = p.astype(BF16)
    me = position()
    last = lax.axis_size("grp") * lax.axis_size("sub") - 1
    left = from_left[:, margin:].astype(F32) + corr_ref[:, :margin]
    right = from_right[:, margin:].astype(F32) + corr_ref[:, margin + owned:]
    left = jnp.where(me == 0, 0.0, left).astype(BF16)
    right = jnp.where(me == last, 0.0, right).astype(BF16)

    def finish(span, image):
        image_ref[:, span] = image

    times_operator(p, pb_ref, left, right, diag_ref, values_ref, cols_ref, cl_ref, cr_ref, finish)
    ones = jnp.ones((8, owned), F32)
    inner = mm_nt(ones, r_ref[...] * p, precision=lax.Precision.HIGHEST)
    curvature = mm_nt(ones, p * image_ref[...], precision=lax.Precision.HIGHEST)
    sums = jnp.concatenate([inner[0:1], curvature[0:1]], axis=0)
    for slot in range(sums_ref.shape[0]):
        sums_ref[slot] = sums


def finish_kernel(x_ref, p_ref, r_ref, image_ref, sums_ref, out_x_ref, out_r_ref):
    sums = jnp.sum(sums_ref[...], axis=0)
    row = sums[0:1, :] / sums[1:2, :]
    lanes = 128
    step = jnp.transpose(jnp.broadcast_to(row, (lanes, row.shape[1])))
    for start in range(0, x_ref.shape[1], lanes):
        span = slice(start, start + lanes)
        out_x_ref[:, span] = x_ref[:, span] + step * p_ref[:, span]
        out_r_ref[:, span] = r_ref[:, span] - step * image_ref[:, span]


def call(kernel, out, in_specs, scratch=()):
    return pl.pallas_call(
        kernel,
        out_shape=out,
        in_specs=in_specs,
        out_specs=[VMEM] * len(out),
        scratch_shapes=list(scratch),
        name=kernel.__name__,
        compiler_params=pltpu.CompilerParams(vmem_limit_bytes=16 * 2**20),
    )


def struct(shape, dtype):
    return jax.ShapeDtypeStruct(shape, dtype)


def shards(right_side, iterate_in, diagonal, block_values, block_cols, couple_left, couple_right, send_rows,
           local_inverse, coarse_basis, coarse_diag, coarse_up):
    groups, members = lax.axis_size("grp"), lax.axis_size("sub")
    total = groups * members
    rows, cases = right_side.shape
    margin = send_rows.shape[2]
    extended = local_inverse.shape[1]
    modes = coarse_basis.shape[2]
    width = 3 * modes + cases
    pairs = [(i, i ^ 1) for i in range(total)]
    others = [(i, i + 1 if i % 2 else i - 1) for i in range(1, total - 1)]
    right_side, iterate_in = right_side.T, iterate_in.T
    basis = jnp.swapaxes(coarse_basis, 1, 2)
    block_cols = jnp.transpose(block_cols, (2, 0, 1))

    def swap(to_pair, to_other):
        return lax.ppermute(to_pair, AXES, pairs), lax.ppermute(to_other, AXES, others)

    halo = struct((cases, margin), BF16)
    full = struct((cases, rows), F32)
    operator = (diagonal, block_values, block_cols, couple_left, couple_right, send_rows)
    operator_specs = [VMEM, VMEM, SMEM, VMEM, VMEM, VMEM]
    sent = call(gather_kernel, [halo, halo], [VMEM] * 2)(iterate_in, send_rows)
    got = swap(*sent)
    residual, rounded, *sent = call(
        residual_kernel,
        [full, struct((cases, rows), BF16), halo, halo],
        [VMEM, VMEM] + operator_specs + [VMEM, VMEM],
        [pltpu.VMEM((cases, rows), BF16)],
    )(right_side, iterate_in, *operator, *got)
    got = swap(*sent)
    local, message = call(
        local_kernel, [struct((cases, extended), F32), struct((members, modes, width), F32)], [VMEM] * 7
    )(local_inverse, basis, coarse_diag, coarse_up, rounded, *got)
    gathered = lax.all_to_all(message, "sub", 0, 0, tiled=True)
    solved, reduced = call(
        group_kernel, [struct((members, modes, width), F32), struct((2 * modes, width), F32)], [VMEM]
    )(gathered)
    reduced = lax.all_gather(reduced, "grp", axis=0)
    correction, *sent = call(
        solve_kernel,
        [struct((cases, extended), F32)] + [struct((cases, 2 * margin), BF16)] * 2,
        [VMEM] * 5,
        [
            pltpu.VMEM((groups + 1, modes, cases), F32),
            pltpu.VMEM((members + 1, modes, cases), F32),
            pltpu.VMEM((8, 128), F32),
        ],
    )(reduced, solved, local, basis, send_rows)
    got = swap(*sent)
    direction, image, sums = call(
        image_kernel,
        [full, full, struct((total, 2, cases), F32)],
        [VMEM, VMEM] + operator_specs + [VMEM, VMEM],
        [pltpu.VMEM((cases, rows), BF16)],
    )(correction, residual, *operator, *got)
    sums = lax.all_to_all(sums, AXES, 0, 0, tiled=True)
    iterate, residual = call(finish_kernel, [full, full], [VMEM] * 5)(iterate_in, direction, residual, image, sums)
    return iterate.T, residual.T


def solution(mesh):
    whole = P(AXES)

    def spec(rank):
        return P(AXES, *([None] * (rank - 1)))

    return jax.shard_map(
        shards,
        mesh=mesh,
        in_specs=tuple(spec(rank) for rank in (2, 2, 1, 5, 3, 2, 2, 3, 3, 3, 3, 3)),
        out_specs=(spec(2), spec(2)),
        check_vma=False,
    )
```

```python
import functools

import jax
import jax.numpy as jnp
from jax import lax
from jax.experimental import pallas as pl
from jax.experimental.pallas import tpu as pltpu
from jax.sharding import PartitionSpec as P

AXES = ("grp", "sub")
BF16 = jnp.bfloat16
F32 = jnp.float32
VMEM = pl.BlockSpec(memory_space=pltpu.VMEM)
HBM = pl.BlockSpec(memory_space=pltpu.HBM)


def mm(a, b):
    return jnp.dot(a, b, preferred_element_type=F32)


def mm_t(a, b, **kw):
    return lax.dot_general(a, b, (((0,), (0,)), ((), ())), preferred_element_type=F32, **kw)


def mm_nt(a, b, **kw):
    return lax.dot_general(a, b, (((1,), (1,)), ((), ())), preferred_element_type=F32, **kw)


def position():
    return lax.axis_index("grp") * lax.axis_size("sub") + lax.axis_index("sub")


def is_even():
    return position() % 2 == 0


def place_matrix(row, total):
    place = lax.broadcasted_iota(jnp.int32, (total, row.shape[1]), 0)
    return (place == row).astype(F32).astype(BF16)


def send_matrix(rows_ref, total):
    left, right = rows_ref[0, 0:1, :], rows_ref[0, 1:2, :]
    even = is_even()
    rows = jnp.concatenate([jnp.where(even, right, left), jnp.where(even, left, right)], axis=1)
    return place_matrix(rows, total)


def from_sides(pair_ref, other_ref):
    even = is_even()
    pair, other = pair_ref[...], other_ref[...]
    return jnp.where(even, other, pair), jnp.where(even, pair, other)


def copy_all(copies, sems):
    started = [pltpu.make_async_copy(source, target, sems.at[n]) for n, (source, target) in enumerate(copies)]
    for copy in started:
        copy.start()
    return started


def gather_kernel(x_hbm, rows_hbm, to_pair_ref, to_other_ref, x_ref, rows_ref, sems):
    for copy in copy_all([(rows_hbm, rows_ref), (x_hbm, x_ref)], sems):
        copy.wait()
    values = x_ref[...].astype(BF16)
    margin = rows_ref.shape[2]
    sent = mm(values, send_matrix(rows_ref, values.shape[1])).astype(BF16)
    to_pair_ref[...] = sent[:, :margin]
    to_other_ref[...] = sent[:, margin:]


def own_kernel(x_ref, b_hbm, diag_hbm, values_hbm, cols_hbm, cl_hbm, cr_hbm,
               partial_ref, operator_ref, diag_ref, cols_ref, b_ref, sems):
    blocks, nonzeros, size = values_hbm.shape[1], values_hbm.shape[2], values_hbm.shape[3]
    rows = x_ref.shape[1]
    margin = cl_hbm.shape[1]
    first = copy_all(
        [
            (cols_hbm, cols_ref),
            (diag_hbm, diag_ref),
            (b_hbm, b_ref),
            (cl_hbm, operator_ref.at[:, rows:rows + margin]),
            (cr_hbm, operator_ref.at[:, rows + margin:]),
        ],
        sems,
    )
    operator_ref[:, :rows] = jnp.zeros((rows, rows), BF16)
    first[0].wait()
    placed = []
    for i in range(blocks):
        for t in range(nonzeros):
            start = pl.multiple_of(cols_ref[t, 0, i] * size, size)
            target = operator_ref.at[i * size:(i + 1) * size, pl.ds(start, size)]
            copy = pltpu.make_async_copy(values_hbm.at[0, i, t], target, sems.at[len(first) + i * nonzeros + t])
            copy.start()
            placed.append(copy)
    for copy in first[1:] + placed:
        copy.wait()
    x = x_ref[...]
    diag = diag_ref[...].reshape(1, rows)
    partial_ref[...] = b_ref[...] - diag * x - mm_nt(x.astype(BF16), operator_ref[:, :rows])


def residual_kernel(partial_ref, operator_ref, rows_ref, pair_ref, other_ref, r_ref, rb_ref, to_pair_ref, to_other_ref):
    rows = partial_ref.shape[1]
    margin = rows_ref.shape[2]
    halo = jnp.concatenate(from_sides(pair_ref, other_ref), axis=1)
    r = partial_ref[...] - mm_nt(halo, operator_ref[:, rows:])
    r_ref[...] = r
    rounded = r.astype(BF16)
    rb_ref[...] = rounded
    sent = mm(rounded, send_matrix(rows_ref, rows)).astype(BF16)
    to_pair_ref[...] = sent[:, :margin]
    to_other_ref[...] = sent[:, margin:]


def inverse_kernel(rb_ref, inverse_hbm, basis_hbm, diag_hbm, up_hbm, local_ref, coarse_ref, ends_ref, basis_ref, blocks_ref,
                   own_ref, sems):
    rows = rb_ref.shape[1]
    total = inverse_hbm.shape[1]
    margin = (total - rows) // 2
    copies = copy_all(
        [
            (basis_hbm, basis_ref),
            (diag_hbm, blocks_ref.at[0:1]),
            (up_hbm, blocks_ref.at[1:2]),
            (inverse_hbm.at[0, margin:margin + rows], own_ref),
            (inverse_hbm.at[0, :margin], ends_ref.at[:margin]),
            (inverse_hbm.at[0, margin + rows:], ends_ref.at[margin:]),
        ],
        sems,
    )
    for copy in copies:
        copy.wait()
    rounded = rb_ref[...]
    local_ref[...] = mm(rounded, own_ref[...])
    coarse_ref[...] = mm_nt(basis_ref[0, :, margin:margin + rows], rounded)


def local_kernel(own_local_ref, own_coarse_ref, ends_ref, basis_ref, blocks_ref, pair_ref, other_ref,
                 local_ref, message_ref):
    margin = pair_ref.shape[1]
    halo = jnp.concatenate(from_sides(pair_ref, other_ref), axis=1)
    ends = jnp.concatenate([basis_ref[0, :, :margin], basis_ref[0, :, basis_ref.shape[2] - margin:]], axis=1)
    coarse_in = own_coarse_ref[...] + mm_nt(ends, halo)
    last = position() == lax.axis_size("grp") * lax.axis_size("sub") - 1
    up = jnp.where(last, 0.0, blocks_ref[1])
    message = jnp.concatenate([blocks_ref[0], jnp.transpose(up), up, coarse_in], axis=1)
    for slot in range(message_ref.shape[0]):
        message_ref[slot] = message
    local_ref[...] = own_local_ref[...] + mm(halo, ends_ref[...])


def reduce_rows(blocks):
    size, width = blocks[0].shape
    panel = 8 if len(blocks) <= 2 else 4
    lanes = 128
    here = lax.broadcasted_iota(jnp.int32, (size, 1), 0)

    def wide(value):
        return jnp.concatenate([value] * (width // lanes), axis=1)

    for first in range(0, size, panel):
        panels = [
            [jnp.broadcast_to(block[:, q:q + 1], (size, lanes)) for q in range(first, first + panel)] for block in blocks
        ]
        for a in range(panel):
            p = first + a
            done = []
            for block, columns in zip(blocks, panels):
                column = columns[a]
                inverse = 1.0 / column[p:p + 1, :]
                for b in range(a + 1, panel):
                    entry = columns[b][p:p + 1, :] * inverse
                    columns[b] = jnp.where(here == p, entry, columns[b] - column * entry)
                row = block[p:p + 1, :] * wide(inverse)
                done.append(jnp.where(here == p, row, block - wide(column) * row))
            blocks = done
    return blocks


def schur(block, solved, size):
    width = solved.shape[1]
    product = -mm_t(block[:, :4 * size], solved, precision=lax.Precision.HIGHEST)
    top, bottom = product[size:2 * size], product[2 * size:3 * size]
    zero = jnp.zeros((size, size), F32)
    to_left = jnp.concatenate([top[:, size:2 * size], zero, top[:, 2 * size:]], axis=1)
    to_right = jnp.concatenate([bottom[:, 2 * size:3 * size], bottom[:, size:2 * size], zero, bottom[:, 3 * size:]], axis=1)
    return to_left, to_right


def own_part(block, size):
    lane = lax.broadcasted_iota(jnp.int32, block.shape, 1)
    return jnp.where((lane >= size) & (lane < 3 * size), 0.0, block)


def eliminate(chain, size, keep):
    count = len(chain) - 1
    step = 1
    while step < count:
        inner = list(range(step, count, 2 * step))
        solved = dict(zip(inner, reduce_rows([chain[j] for j in inner])))
        parts = {j: schur(chain[j], solved[j], size) for j in inner}
        for j in inner:
            keep(j, solved[j])
        for i in range(0, count + 1, 2 * step):
            total = own_part(chain[i], size)
            if i + step in parts:
                total = total + parts[i + step][0]
            if i - step in parts:
                total = total + parts[i - step][1]
            chain[i] = total
        step = 2 * step
    return chain[0], chain[count]


def back(solved, left, right, size):
    zero = jnp.zeros_like(left)
    stacked = jnp.concatenate([zero, left, right, zero], axis=0)
    return solved[:, 3 * size:] - jnp.dot(
        solved[:, :4 * size], stacked, precision=lax.Precision.HIGHEST, preferred_element_type=F32)


def padded(count):
    total = 1
    while total < count:
        total = 2 * total
    return total


def chain_of(blocks, size):
    width = blocks[0].shape[1]
    lane = lax.broadcasted_iota(jnp.int32, (size, width), 1)
    row = lax.broadcasted_iota(jnp.int32, (size, width), 0)
    from_previous = (lane >= size) & (lane < 2 * size)
    own = [jnp.where(from_previous, 0.0, block) for block in blocks]
    chain = [own[0]]
    for j in range(1, len(blocks)):
        chain.append(jnp.where(from_previous, blocks[j - 1], blocks[j]))
    return chain, from_previous, (lane == row).astype(F32)


def group_kernel(gathered_ref, solved_ref, message_ref):
    members, size, width = gathered_ref.shape
    blocks = [gathered_ref[j] for j in range(members)]
    chain, from_previous, identity = chain_of(blocks, size)
    tail = jnp.where(from_previous, blocks[members - 1], 0.0)
    total = padded(members)
    if total > members:
        raise NotImplementedError("members")
    chain.append(tail)

    def keep(j, solved):
        solved_ref[j] = solved

    head, tail = eliminate(chain, size, keep)
    message_ref[:size, :] = head
    message_ref[size:, :] = tail


def solve_kernel(reduced_ref, solved_ref, local_ref, basis_ref, rows_ref,
                 corr_ref, to_pair_ref, to_other_ref, sep_ref, x_ref):
    groups, two_size, width = reduced_ref.shape
    size = two_size // 2
    members = solved_ref.shape[0]
    chain = []
    for g in range(groups):
        total = reduced_ref[g, :size, :]
        if g:
            total = total + reduced_ref[g - 1, size:, :]
        chain.append(total)
    count = padded(groups)
    row = lax.broadcasted_iota(jnp.int32, (size, width), 0)
    lane = lax.broadcasted_iota(jnp.int32, (size, width), 1)
    while len(chain) < count:
        chain.append((row == lane).astype(F32))
    chain.append(jnp.zeros((size, width), F32))
    factors = {}
    head, _ = eliminate(chain, size, factors.__setitem__)
    solution = {count: jnp.zeros((size, width - 3 * size), F32)}
    solution[0] = reduce_rows([head])[0][:, 3 * size:]
    step = count // 2
    while step >= 1:
        for j in range(step, count, 2 * step):
            solution[j] = back(factors[j], solution[j - step], solution[j + step], size)
        step = step // 2
    for g in range(groups):
        sep_ref[g] = solution[g]
    sep_ref[groups] = jnp.zeros((size, width - 3 * size), F32)
    group, member = lax.axis_index("grp"), lax.axis_index("sub")
    x_ref[0] = sep_ref[group]
    x_ref[members] = sep_ref[group + 1]
    step = members // 2
    while step >= 2:
        for j in range(step, members, 2 * step):
            x_ref[j] = back(solved_ref[j], x_ref[j - step], x_ref[j + step], size)
        step = step // 2
    odd = member // 2 * 2 + 1
    x_ref[odd] = back(solved_ref[odd], x_ref[odd - 1], x_ref[odd + 1], size)
    coarse = x_ref[member].astype(BF16)
    correction = local_ref[...] + mm_t(coarse, basis_ref[0])
    corr_ref[...] = correction
    margin = rows_ref.shape[2]
    owned = correction.shape[1] - 2 * margin
    rounded = correction.astype(BF16)
    even = is_even()
    head, tail = rounded[:, :margin], rounded[:, margin + owned:]
    sent = mm(rounded[:, margin:margin + owned], send_matrix(rows_ref, owned)).astype(BF16)
    to_pair_ref[:, :margin] = jnp.where(even, tail, head)
    to_other_ref[:, :margin] = jnp.where(even, head, tail)
    to_pair_ref[:, margin:] = sent[:, :margin]
    to_other_ref[:, margin:] = sent[:, margin:]


def image_kernel(corr_ref, r_ref, diag_ref, operator_ref, rows_ref, pair_ref, other_ref, p_ref, image_ref, sums_ref):
    margin = rows_ref.shape[2]
    owned = p_ref.shape[1]
    from_left, from_right = from_sides(pair_ref, other_ref)
    place = place_matrix(jnp.concatenate([rows_ref[0, 0:1, :], rows_ref[0, 1:2, :]], axis=1), owned)
    tails = jnp.concatenate([from_left[:, :margin], from_right[:, :margin]], axis=1)
    p = corr_ref[:, margin:margin + owned] + mm_nt(tails, place)
    p_ref[...] = p
    me = position()
    last = lax.axis_size("grp") * lax.axis_size("sub") - 1
    left = from_left[:, margin:].astype(F32) + corr_ref[:, :margin]
    right = from_right[:, margin:].astype(F32) + corr_ref[:, margin + owned:]
    left = jnp.where(me == 0, 0.0, left).astype(BF16)
    right = jnp.where(me == last, 0.0, right).astype(BF16)
    values = jnp.concatenate([p.astype(BF16), left, right], axis=1)
    image = diag_ref[...].reshape(1, owned) * p + mm_nt(values, operator_ref[...])
    image_ref[...] = image
    ones = jnp.ones((8, owned), F32)
    inner = mm_nt(ones, r_ref[...] * p, precision=lax.Precision.HIGHEST)
    curvature = mm_nt(ones, p * image, precision=lax.Precision.HIGHEST)
    sums = jnp.concatenate([inner[0:1], curvature[0:1]], axis=0)
    for slot in range(sums_ref.shape[0]):
        sums_ref[slot] = sums


def finish_kernel(x_ref, p_ref, r_ref, image_ref, sums_ref, out_x_ref, out_r_ref):
    sums = jnp.sum(sums_ref[...], axis=0)
    row = sums[0:1, :] / sums[1:2, :]
    lanes = 128
    step = jnp.transpose(jnp.broadcast_to(row, (lanes, row.shape[1])))
    for start in range(0, x_ref.shape[1], lanes):
        span = slice(start, start + lanes)
        out_x_ref[:, span] = x_ref[:, span] + step * p_ref[:, span]
        out_r_ref[:, span] = r_ref[:, span] - step * image_ref[:, span]


def call(kernel, out, in_specs, scratch=()):
    return pl.pallas_call(
        kernel,
        out_shape=out,
        in_specs=in_specs,
        out_specs=[VMEM] * len(out),
        scratch_shapes=list(scratch),
        name=kernel.__name__,
        compiler_params=pltpu.CompilerParams(vmem_limit_bytes=16 * 2**20),
    )


def far(*arrays):
    return [pltpu.with_memory_space_constraint(array, pltpu.HBM) for array in arrays]


def struct(shape, dtype):
    return jax.ShapeDtypeStruct(shape, dtype)


def shards(right_side, iterate_in, diagonal, block_values, block_cols, couple_left, couple_right, send_rows,
           local_inverse, coarse_basis, coarse_diag, coarse_up):
    groups, members = lax.axis_size("grp"), lax.axis_size("sub")
    total = groups * members
    rows, cases = right_side.shape
    margin = send_rows.shape[2]
    extended = local_inverse.shape[1]
    modes = coarse_basis.shape[2]
    width = 3 * modes + cases
    pairs = [(i, i ^ 1) for i in range(total)]
    others = [(i, i + 1 if i % 2 else i - 1) for i in range(1, total - 1)]
    right_side, iterate_in = right_side.T, iterate_in.T
    basis = jnp.swapaxes(coarse_basis, 1, 2)
    block_cols = jnp.transpose(block_cols, (2, 0, 1))

    def swap(to_pair, to_other):
        return lax.ppermute(to_pair, AXES, pairs), lax.ppermute(to_other, AXES, others)

    halo = struct((cases, margin), BF16)
    full = struct((cases, rows), F32)
    semaphores = pltpu.SemaphoreType.DMA
    to_pair, to_other, start, send_rows = call(
        gather_kernel, [halo, halo, full, struct(send_rows.shape, send_rows.dtype)], [HBM] * 2, [semaphores((2,))]
    )(*far(iterate_in, send_rows))
    got = swap(to_pair, to_other)
    nonzero_blocks = block_cols.size
    partial, operator, diag = call(
        own_kernel,
        [full, struct((rows, rows + 2 * margin), BF16), struct(diagonal.shape, F32)],
        [VMEM] + [HBM] * 6,
        [
            pltpu.SMEM(block_cols.shape, block_cols.dtype),
            pltpu.VMEM((cases, rows), F32),
            semaphores((5 + nonzero_blocks,)),
        ],
    )(start, *far(right_side, diagonal, block_values, block_cols, couple_left, couple_right))
    residual, rounded, *sent = call(
        residual_kernel, [full, struct((cases, rows), BF16), halo, halo], [VMEM] * 5
    )(partial, operator, send_rows, *got)
    got = swap(*sent)
    local, coarse, ends, basis, blocks = call(
        inverse_kernel,
        [
            struct((cases, extended), F32),
            struct((modes, cases), F32),
            struct((2 * margin, extended), BF16),
            struct(basis.shape, BF16),
            struct((2, modes, modes), F32),
        ],
        [VMEM] + [HBM] * 4,
        [pltpu.VMEM((rows, extended), BF16), semaphores((6,))],
    )(rounded, *far(local_inverse, basis, coarse_diag, coarse_up))
    local, message = call(
        local_kernel, [struct((cases, extended), F32), struct((members, modes, width), F32)], [VMEM] * 7
    )(local, coarse, ends, basis, blocks, *got)
    gathered = lax.all_to_all(message, "sub", 0, 0, tiled=True)
    solved, reduced = call(
        group_kernel, [struct((members, modes, width), F32), struct((2 * modes, width), F32)], [VMEM]
    )(gathered)
    reduced = lax.all_gather(reduced, "grp", axis=0)
    correction, *sent = call(
        solve_kernel,
        [struct((cases, extended), F32)] + [struct((cases, 2 * margin), BF16)] * 2,
        [VMEM] * 5,
        [pltpu.VMEM((groups + 1, modes, cases), F32), pltpu.VMEM((members + 1, modes, cases), F32)],
    )(reduced, solved, local, basis, send_rows)
    got = swap(*sent)
    direction, image, sums = call(image_kernel, [full, full, struct((total, 2, cases), F32)], [VMEM] * 7)(
        correction, residual, diag, operator, send_rows, *got
    )
    sums = lax.all_to_all(sums, AXES, 0, 0, tiled=True)
    iterate, residual = call(finish_kernel, [full, full], [VMEM] * 5)(start, direction, residual, image, sums)
    return iterate.T, residual.T


def solution(mesh):
    whole = P(AXES)

    def spec(rank):
        return P(AXES, *([None] * (rank - 1)))

    return jax.shard_map(
        shards,
        mesh=mesh,
        in_specs=tuple(spec(rank) for rank in (2, 2, 1, 5, 3, 2, 2, 3, 3, 3, 3, 3)),
        out_specs=(spec(2), spec(2)),
        check_vma=False,
    )
```

```python
import functools

import jax
import jax.numpy as jnp
from jax import lax
from jax.experimental import pallas as pl
from jax.experimental.pallas import tpu as pltpu
from jax.sharding import PartitionSpec as P

AXES = ("grp", "sub")
BF16 = jnp.bfloat16
F32 = jnp.float32
VMEM = pl.BlockSpec(memory_space=pltpu.VMEM)
HBM = pl.BlockSpec(memory_space=pltpu.HBM)


def mm(a, b):
    return jnp.dot(a, b, preferred_element_type=F32)


def mm_t(a, b, **kw):
    return lax.dot_general(a, b, (((0,), (0,)), ((), ())), preferred_element_type=F32, **kw)


def mm_nt(a, b, **kw):
    return lax.dot_general(a, b, (((1,), (1,)), ((), ())), preferred_element_type=F32, **kw)


def position():
    return lax.axis_index("grp") * lax.axis_size("sub") + lax.axis_index("sub")


def is_even():
    return position() % 2 == 0


def place_matrix(row, total):
    place = lax.broadcasted_iota(jnp.int32, (total, row.shape[1]), 0)
    return (place == row).astype(F32).astype(BF16)


def send_matrix(rows_ref, total):
    left, right = rows_ref[0, 0:1, :], rows_ref[0, 1:2, :]
    even = is_even()
    rows = jnp.concatenate([jnp.where(even, right, left), jnp.where(even, left, right)], axis=1)
    return place_matrix(rows, total)


def from_sides(pair_ref, other_ref):
    even = is_even()
    other = other_ref[...]
    pair = pair_ref[:other.shape[0], :]
    return jnp.where(even, other, pair), jnp.where(even, pair, other)


def copy_all(copies, sems):
    started = [pltpu.make_async_copy(source, target, sems.at[n]) for n, (source, target) in enumerate(copies)]
    for copy in started:
        copy.start()
    return started


def split_three(value):
    high = value.astype(BF16)
    rest = value - high.astype(F32)
    middle = rest.astype(BF16)
    return high, middle, (rest - middle.astype(F32)).astype(BF16)


def gather_kernel(x_hbm, rows_hbm, up_hbm, to_pair_ref, to_other_ref, x_ref, rows_ref, up_ref, sems):
    for copy in copy_all([(rows_hbm, rows_ref), (up_hbm, up_ref), (x_hbm, x_ref)], sems):
        copy.wait()
    values = x_ref[...].astype(BF16)
    cases = values.shape[0]
    margin = rows_ref.shape[2]
    sent = mm(values, send_matrix(rows_ref, values.shape[1])).astype(BF16)
    to_pair_ref[:cases, :] = sent[:, :margin]
    to_other_ref[...] = sent[:, margin:]
    parts = [part.astype(F32) for part in split_three(up_ref[0])]
    size = up_ref.shape[1]
    parts.append(jnp.zeros((size, margin - 3 * size), F32))
    to_pair_ref[cases:, :] = jnp.concatenate(parts, axis=1).astype(BF16)


def own_kernel(x_ref, b_hbm, diag_hbm, values_hbm, cols_hbm, cl_hbm, cr_hbm,
               partial_ref, operator_ref, diag_ref, cols_ref, b_ref, sems):
    blocks, nonzeros, size = values_hbm.shape[1], values_hbm.shape[2], values_hbm.shape[3]
    rows = x_ref.shape[1]
    margin = cl_hbm.shape[1]
    first = copy_all(
        [
            (cols_hbm, cols_ref),
            (diag_hbm, diag_ref),
            (b_hbm, b_ref),
            (cl_hbm, operator_ref.at[:, rows:rows + margin]),
            (cr_hbm, operator_ref.at[:, rows + margin:]),
        ],
        sems,
    )
    operator_ref[:, :rows] = jnp.zeros((rows, rows), BF16)
    first[0].wait()
    placed = []
    for i in range(blocks):
        for t in range(nonzeros):
            start = pl.multiple_of(cols_ref[t, 0, i] * size, size)
            target = operator_ref.at[i * size:(i + 1) * size, pl.ds(start, size)]
            copy = pltpu.make_async_copy(values_hbm.at[0, i, t], target, sems.at[len(first) + i * nonzeros + t])
            copy.start()
            placed.append(copy)
    for copy in first[1:] + placed:
        copy.wait()
    x = x_ref[...]
    diag = diag_ref[...].reshape(1, rows)
    partial_ref[...] = b_ref[...] - diag * x - mm_nt(x.astype(BF16), operator_ref[:, :rows])


def residual_kernel(partial_ref, operator_ref, rows_ref, pair_ref, other_ref, r_ref, rb_ref, to_pair_ref, to_other_ref):
    rows = partial_ref.shape[1]
    margin = rows_ref.shape[2]
    halo = jnp.concatenate(from_sides(pair_ref, other_ref), axis=1)
    r = partial_ref[...] - mm_nt(halo, operator_ref[:, rows:])
    r_ref[...] = r
    rounded = r.astype(BF16)
    rb_ref[...] = rounded
    sent = mm(rounded, send_matrix(rows_ref, rows)).astype(BF16)
    to_pair_ref[...] = sent[:, :margin]
    to_other_ref[...] = sent[:, margin:]


def inverse_kernel(rb_ref, first_pair_ref, inverse_hbm, basis_hbm, diag_hbm, up_hbm,
                   local_ref, coarse_ref, ends_ref, basis_ref, factor_ref, plain_ref, own_ref, blocks_ref, sems):
    cases, rows = rb_ref.shape
    total = inverse_hbm.shape[1]
    margin = (total - rows) // 2
    size = diag_hbm.shape[1]
    copies = copy_all(
        [
            (diag_hbm, blocks_ref.at[0:1]),
            (up_hbm, blocks_ref.at[1:2]),
            (basis_hbm, basis_ref),
            (inverse_hbm.at[0, margin:margin + rows], own_ref),
            (inverse_hbm.at[0, :margin], ends_ref.at[:margin]),
            (inverse_hbm.at[0, margin + rows:], ends_ref.at[margin:]),
        ],
        sems,
    )
    parts = first_pair_ref[cases:, :].astype(F32)
    up_left = parts[:, :size] + (parts[:, size:2 * size] + parts[:, 2 * size:3 * size])
    for copy in copies[:2]:
        copy.wait()
    last = position() == lax.axis_size("grp") * lax.axis_size("sub") - 1
    up = jnp.where(last, 0.0, blocks_ref[1])
    diag = blocks_ref[0]
    row = lax.broadcasted_iota(jnp.int32, (size, size), 0)
    lane = lax.broadcasted_iota(jnp.int32, (size, size), 1)
    identity = (row == lane).astype(F32)
    factor = reduce_rows([jnp.concatenate([diag, jnp.transpose(up_left), up, identity], axis=1)])[0]
    odd = jnp.concatenate([jnp.transpose(up), factor[:, size:3 * size], jnp.zeros((size, size), F32)], axis=1)
    even = jnp.concatenate([diag, up, jnp.zeros((size, 2 * size), F32)], axis=1)
    plain_ref[...] = jnp.where(is_even(), even, odd)
    place = jnp.concatenate([jnp.zeros((size, 3 * size), F32), identity], axis=1)
    lanes = lax.broadcasted_iota(jnp.int32, factor.shape, 1)
    factor_ref[...] = jnp.where(is_even(), place, jnp.where(lanes >= 3 * size, factor, 0.0))
    for copy in copies[2:]:
        copy.wait()
    rounded = rb_ref[...]
    local_ref[...] = mm(rounded, own_ref[...])
    coarse_ref[...] = mm_nt(basis_ref[0, :, margin:margin + rows], rounded)


def local_kernel(own_local_ref, own_coarse_ref, ends_ref, basis_ref, factor_ref, plain_ref, pair_ref, other_ref,
                 local_ref, message_ref):
    margin = pair_ref.shape[1]
    halo = jnp.concatenate(from_sides(pair_ref, other_ref), axis=1)
    ends = jnp.concatenate([basis_ref[0, :, :margin], basis_ref[0, :, basis_ref.shape[2] - margin:]], axis=1)
    coarse_in = own_coarse_ref[...] + mm_nt(ends, halo)
    size = coarse_in.shape[0]
    stacked = jnp.concatenate([jnp.zeros((3 * size, coarse_in.shape[1]), F32), coarse_in], axis=0)
    reduced = jnp.dot(factor_ref[...], stacked, precision=lax.Precision.HIGHEST, preferred_element_type=F32)
    right_side = jnp.where(is_even(), coarse_in, reduced)
    message = jnp.concatenate([plain_ref[:, :3 * size], right_side], axis=1)
    for slot in range(message_ref.shape[0]):
        message_ref[slot] = message
    local_ref[...] = own_local_ref[...] + mm(halo, ends_ref[...])


def reduce_rows(blocks):
    size, width = blocks[0].shape
    panel = 16 if len(blocks) == 1 else 8 if len(blocks) == 2 else 4
    lanes, tile = 128, 8
    here = lax.broadcasted_iota(jnp.int32, (tile, 1), 0)
    tiles = range(size // tile)
    blocks = [[block[t * tile:(t + 1) * tile, :] for t in tiles] for block in blocks]

    def wide(value):
        return jnp.concatenate([value] * (width // lanes), axis=1)

    for first in range(0, size, panel):
        panels = [
            [[jnp.broadcast_to(rows[:, q:q + 1], (tile, lanes)) for rows in block] for q in range(first, first + panel)]
            for block in blocks
        ]
        for a in range(panel):
            at, inside = divmod(first + a, tile)
            for block, columns in zip(blocks, panels):
                column = columns[a]
                inverse = 1.0 / column[at][inside:inside + 1, :]
                for b in range(a + 1, panel):
                    entry = columns[b][at][inside:inside + 1, :] * inverse
                    columns[b] = [
                        jnp.where(here == inside, entry, columns[b][t] - column[t] * entry)
                        if t == at else columns[b][t] - column[t] * entry
                        for t in tiles
                    ]
                row = block[at][inside:inside + 1, :] * wide(inverse)
                for t in tiles:
                    rest = block[t] - wide(column[t]) * row
                    block[t] = jnp.where(here == inside, row, rest) if t == at else rest
    return [jnp.concatenate(block, axis=0) for block in blocks]


def shares(top, bottom, size):
    zero = jnp.zeros((size, size), F32)
    to_left = jnp.concatenate([top[:, size:2 * size], zero, top[:, 2 * size:]], axis=1)
    to_right = jnp.concatenate([bottom[:, 2 * size:3 * size], bottom[:, size:2 * size], zero, bottom[:, 3 * size:]], axis=1)
    return to_left, to_right


def schur(block, solved, size):
    product = -mm_t(block[:, :4 * size], solved, precision=lax.Precision.HIGHEST)
    return shares(product[size:2 * size], product[2 * size:3 * size], size)


def first_schur(previous, block, size):
    highest = lax.Precision.HIGHEST
    zero = jnp.zeros_like(block)
    above = jnp.concatenate([zero, block, zero, zero], axis=0)
    below = jnp.concatenate([block, zero, zero, zero], axis=0)
    top = -jnp.dot(previous[:, :4 * size], above, precision=highest, preferred_element_type=F32)
    bottom = -jnp.dot(block[:, :4 * size], below, precision=highest, preferred_element_type=F32)
    return shares(top, bottom, size)


def own_part(block, size):
    lane = lax.broadcasted_iota(jnp.int32, block.shape, 1)
    return jnp.where((lane >= size) & (lane < 3 * size), 0.0, block)


def combine(chain, parts, step, size):
    for i in range(0, len(chain), 2 * step):
        total = own_part(chain[i], size)
        if i + step in parts:
            total = total + parts[i + step][0]
        if i - step in parts:
            total = total + parts[i - step][1]
        chain[i] = total


def eliminate(chain, size, keep, step=1):
    count = len(chain) - 1
    while step < count:
        inner = list(range(step, count, 2 * step))
        solved = dict(zip(inner, reduce_rows([chain[j] for j in inner])))
        parts = {j: schur(chain[j], solved[j], size) for j in inner}
        for j in inner:
            keep(j, solved[j])
        combine(chain, parts, step, size)
        step = 2 * step
    return chain[0], chain[count]


def back(solved, left, right, size):
    zero = jnp.zeros_like(left)
    stacked = jnp.concatenate([zero, left, right, zero], axis=0)
    return solved[:, 3 * size:] - jnp.dot(
        solved[:, :4 * size], stacked, precision=lax.Precision.HIGHEST, preferred_element_type=F32)


def padded(count):
    total = 1
    while total < count:
        total = 2 * total
    return total


def group_kernel(same_ref, opposite_ref, solved_ref, message_ref):
    half, size, width = same_ref.shape
    members = 2 * half
    even = is_even()
    chain = []
    for j in range(half):
        same, opposite = same_ref[j], opposite_ref[j]
        chain += [jnp.where(even, same, opposite), jnp.where(even, opposite, same)]
    chain.append(jnp.zeros((size, width), F32))

    def keep(j, solved):
        solved_ref[j] = solved

    parts = {}
    for j in range(1, members, 2):
        keep(j, chain[j])
        parts[j] = first_schur(chain[j - 1], chain[j], size)
    combine(chain, parts, 1, size)
    head, tail = eliminate(chain, size, keep, 2)
    message_ref[:size, :] = head
    message_ref[size:, :] = tail


def solve_kernel(reduced_ref, solved_ref, local_ref, basis_ref, rows_ref,
                 corr_ref, to_pair_ref, to_other_ref, sep_ref, x_ref):
    groups, two_size, width = reduced_ref.shape
    size = two_size // 2
    members = solved_ref.shape[0]
    chain = []
    for g in range(groups):
        total = reduced_ref[g, :size, :]
        if g:
            total = total + reduced_ref[g - 1, size:, :]
        chain.append(total)
    count = padded(groups)
    row = lax.broadcasted_iota(jnp.int32, (size, width), 0)
    lane = lax.broadcasted_iota(jnp.int32, (size, width), 1)
    while len(chain) < count:
        chain.append((row == lane).astype(F32))
    chain.append(jnp.zeros((size, width), F32))
    factors = {}
    head, _ = eliminate(chain, size, factors.__setitem__)
    solution = {count: jnp.zeros((size, width - 3 * size), F32)}
    solution[0] = reduce_rows([head])[0][:, 3 * size:]
    step = count // 2
    while step >= 1:
        for j in range(step, count, 2 * step):
            solution[j] = back(factors[j], solution[j - step], solution[j + step], size)
        step = step // 2
    for g in range(groups):
        sep_ref[g] = solution[g]
    sep_ref[groups] = jnp.zeros((size, width - 3 * size), F32)
    group, member = lax.axis_index("grp"), lax.axis_index("sub")
    x_ref[0] = sep_ref[group]
    x_ref[members] = sep_ref[group + 1]
    step = members // 2
    while step >= 2:
        for j in range(step, members, 2 * step):
            x_ref[j] = back(solved_ref[j], x_ref[j - step], x_ref[j + step], size)
        step = step // 2
    odd = member // 2 * 2 + 1
    x_ref[odd] = back(solved_ref[odd], x_ref[odd - 1], x_ref[odd + 1], size)
    coarse = x_ref[member].astype(BF16)
    correction = local_ref[...] + mm_t(coarse, basis_ref[0])
    corr_ref[...] = correction
    margin = rows_ref.shape[2]
    owned = correction.shape[1] - 2 * margin
    rounded = correction.astype(BF16)
    even = is_even()
    head, tail = rounded[:, :margin], rounded[:, margin + owned:]
    sent = mm(rounded[:, margin:margin + owned], send_matrix(rows_ref, owned)).astype(BF16)
    to_pair_ref[:, :margin] = jnp.where(even, tail, head)
    to_other_ref[:, :margin] = jnp.where(even, head, tail)
    to_pair_ref[:, margin:] = sent[:, :margin]
    to_other_ref[:, margin:] = sent[:, margin:]


def image_kernel(corr_ref, r_ref, diag_ref, operator_ref, rows_ref, pair_ref, other_ref, p_ref, image_ref, sums_ref):
    margin = rows_ref.shape[2]
    owned = p_ref.shape[1]
    from_left, from_right = from_sides(pair_ref, other_ref)
    place = place_matrix(jnp.concatenate([rows_ref[0, 0:1, :], rows_ref[0, 1:2, :]], axis=1), owned)
    tails = jnp.concatenate([from_left[:, :margin], from_right[:, :margin]], axis=1)
    p = corr_ref[:, margin:margin + owned] + mm_nt(tails, place)
    p_ref[...] = p
    me = position()
    last = lax.axis_size("grp") * lax.axis_size("sub") - 1
    left = from_left[:, margin:].astype(F32) + corr_ref[:, :margin]
    right = from_right[:, margin:].astype(F32) + corr_ref[:, margin + owned:]
    left = jnp.where(me == 0, 0.0, left).astype(BF16)
    right = jnp.where(me == last, 0.0, right).astype(BF16)
    values = jnp.concatenate([p.astype(BF16), left, right], axis=1)
    image = diag_ref[...].reshape(1, owned) * p + mm_nt(values, operator_ref[...])
    image_ref[...] = image
    ones = jnp.ones((8, owned), F32)
    inner = mm_nt(ones, r_ref[...] * p, precision=lax.Precision.HIGHEST)
    curvature = mm_nt(ones, p * image, precision=lax.Precision.HIGHEST)
    sums = jnp.concatenate([inner[0:1], curvature[0:1]], axis=0)
    for slot in range(sums_ref.shape[0]):
        sums_ref[slot] = sums


def finish_kernel(x_ref, p_ref, r_ref, image_ref, sums_ref, out_x_ref, out_r_ref):
    sums = jnp.sum(sums_ref[...], axis=0)
    row = sums[0:1, :] / sums[1:2, :]
    lanes = 128
    step = jnp.transpose(jnp.broadcast_to(row, (lanes, row.shape[1])))
    for start in range(0, x_ref.shape[1], lanes):
        span = slice(start, start + lanes)
        out_x_ref[:, span] = x_ref[:, span] + step * p_ref[:, span]
        out_r_ref[:, span] = r_ref[:, span] - step * image_ref[:, span]


def call(kernel, out, in_specs, scratch=()):
    return pl.pallas_call(
        kernel,
        out_shape=out,
        in_specs=in_specs,
        out_specs=[VMEM] * len(out),
        scratch_shapes=list(scratch),
        name=kernel.__name__,
        compiler_params=pltpu.CompilerParams(vmem_limit_bytes=16 * 2**20),
    )


def far(*arrays):
    return [pltpu.with_memory_space_constraint(array, pltpu.HBM) for array in arrays]


def struct(shape, dtype):
    return jax.ShapeDtypeStruct(shape, dtype)


def shards(right_side, iterate_in, diagonal, block_values, block_cols, couple_left, couple_right, send_rows,
           local_inverse, coarse_basis, coarse_diag, coarse_up):
    groups, members = lax.axis_size("grp"), lax.axis_size("sub")
    total = groups * members
    rows, cases = right_side.shape
    margin = send_rows.shape[2]
    extended = local_inverse.shape[1]
    modes = coarse_basis.shape[2]
    width = 3 * modes + cases
    pairs = [(i, i ^ 1) for i in range(total)]
    others = [(i, i + 1 if i % 2 else i - 1) for i in range(1, total - 1)]
    right_side, iterate_in = right_side.T, iterate_in.T
    basis = jnp.swapaxes(coarse_basis, 1, 2)
    block_cols = jnp.transpose(block_cols, (2, 0, 1))

    def swap(to_pair, to_other):
        return lax.ppermute(to_pair, AXES, pairs), lax.ppermute(to_other, AXES, others)

    halo = struct((cases, margin), BF16)
    full = struct((cases, rows), F32)
    semaphores = pltpu.SemaphoreType.DMA
    to_pair, to_other, start, send_rows = call(
        gather_kernel,
        [struct((cases + modes, margin), BF16), halo, full, struct(send_rows.shape, send_rows.dtype)],
        [HBM] * 3,
        [pltpu.VMEM(coarse_up.shape, F32), semaphores((3,))],
    )(*far(iterate_in, send_rows, coarse_up))
    got = swap(to_pair, to_other)
    first_pair = got[0]
    nonzero_blocks = block_cols.size
    partial, operator, diag = call(
        own_kernel,
        [full, struct((rows, rows + 2 * margin), BF16), struct(diagonal.shape, F32)],
        [VMEM] + [HBM] * 6,
        [
            pltpu.SMEM(block_cols.shape, block_cols.dtype),
            pltpu.VMEM((cases, rows), F32),
            semaphores((5 + nonzero_blocks,)),
        ],
    )(start, *far(right_side, diagonal, block_values, block_cols, couple_left, couple_right))
    residual, rounded, *sent = call(
        residual_kernel, [full, struct((cases, rows), BF16), halo, halo], [VMEM] * 5
    )(partial, operator, send_rows, *got)
    got = swap(*sent)
    local, coarse, ends, basis, factor, plain = call(
        inverse_kernel,
        [
            struct((cases, extended), F32),
            struct((modes, cases), F32),
            struct((2 * margin, extended), BF16),
            struct(basis.shape, BF16),
            struct((modes, 4 * modes), F32),
            struct((modes, 4 * modes), F32),
        ],
        [VMEM] * 2 + [HBM] * 4,
        [pltpu.VMEM((rows, extended), BF16), pltpu.VMEM((2, modes, modes), F32), semaphores((6,))],
    )(rounded, first_pair, *far(local_inverse, basis, coarse_diag, coarse_up))
    chips = members // 2
    local, message = call(
        local_kernel, [struct((cases, extended), F32), struct((chips, modes, width), F32)], [VMEM] * 8
    )(local, coarse, ends, basis, factor, plain, *got)
    cores = [[2 * chip + core for chip in range(chips)] for core in range(2)]
    same = lax.all_to_all(message, "sub", 0, 0, tiled=True, axis_index_groups=cores)
    opposite = lax.ppermute(same, AXES, pairs)
    solved, reduced = call(
        group_kernel, [struct((members, modes, width), F32), struct((2 * modes, width), F32)], [VMEM] * 2
    )(same, opposite)
    reduced = lax.all_gather(reduced, "grp", axis=0)
    correction, *sent = call(
        solve_kernel,
        [struct((cases, extended), F32)] + [struct((cases, 2 * margin), BF16)] * 2,
        [VMEM] * 5,
        [pltpu.VMEM((groups + 1, modes, cases), F32), pltpu.VMEM((members + 1, modes, cases), F32)],
    )(reduced, solved, local, basis, send_rows)
    got = swap(*sent)
    direction, image, sums = call(image_kernel, [full, full, struct((total, 2, cases), F32)], [VMEM] * 7)(
        correction, residual, diag, operator, send_rows, *got
    )
    sums = lax.all_to_all(sums, AXES, 0, 0, tiled=True)
    iterate, residual = call(finish_kernel, [full, full], [VMEM] * 5)(start, direction, residual, image, sums)
    return iterate.T, residual.T


def solution(mesh):
    whole = P(AXES)

    def spec(rank):
        return P(AXES, *([None] * (rank - 1)))

    return jax.shard_map(
        shards,
        mesh=mesh,
        in_specs=tuple(spec(rank) for rank in (2, 2, 1, 5, 3, 2, 2, 3, 3, 3, 3, 3)),
        out_specs=(spec(2), spec(2)),
        check_vma=False,
    )
```

```python
import functools

import jax
import jax.numpy as jnp
from jax import lax
from jax.experimental import pallas as pl
from jax.experimental.pallas import tpu as pltpu
from jax.sharding import PartitionSpec as P

AXES = ("grp", "sub")
BF16 = jnp.bfloat16
F32 = jnp.float32
VMEM = pl.BlockSpec(memory_space=pltpu.VMEM)
HBM = pl.BlockSpec(memory_space=pltpu.HBM)


def mm(a, b):
    return jnp.dot(a, b, preferred_element_type=F32)


def mm_t(a, b, **kw):
    return lax.dot_general(a, b, (((0,), (0,)), ((), ())), preferred_element_type=F32, **kw)


def mm_nt(a, b, **kw):
    return lax.dot_general(a, b, (((1,), (1,)), ((), ())), preferred_element_type=F32, **kw)


def position():
    return lax.axis_index("grp") * lax.axis_size("sub") + lax.axis_index("sub")


def is_even():
    return position() % 2 == 0


def place_matrix(row, total):
    place = lax.broadcasted_iota(jnp.int32, (total, row.shape[1]), 0)
    return (place == row).astype(F32).astype(BF16)


def send_matrix(rows_ref, total):
    left, right = rows_ref[0, 0:1, :], rows_ref[0, 1:2, :]
    even = is_even()
    rows = jnp.concatenate([jnp.where(even, right, left), jnp.where(even, left, right)], axis=1)
    return place_matrix(rows, total)


def from_sides(pair_ref, other_ref):
    even = is_even()
    other = other_ref[...]
    pair = pair_ref[:other.shape[0], :]
    return jnp.where(even, other, pair), jnp.where(even, pair, other)


def copy_all(copies, sems):
    started = [pltpu.make_async_copy(source, target, sems.at[n]) for n, (source, target) in enumerate(copies)]
    for copy in started:
        copy.start()
    return started


def split_three(value):
    high = value.astype(BF16)
    rest = value - high.astype(F32)
    middle = rest.astype(BF16)
    return high, middle, (rest - middle.astype(F32)).astype(BF16)


def gather_kernel(x_hbm, rows_hbm, up_hbm, to_pair_ref, to_other_ref, x_ref, rows_ref, up_ref, sems):
    for copy in copy_all([(rows_hbm, rows_ref), (up_hbm, up_ref), (x_hbm, x_ref)], sems):
        copy.wait()
    values = x_ref[...].astype(BF16)
    cases = values.shape[0]
    margin = rows_ref.shape[2]
    sent = mm(values, send_matrix(rows_ref, values.shape[1])).astype(BF16)
    to_pair_ref[:cases, :] = sent[:, :margin]
    to_other_ref[...] = sent[:, margin:]
    parts = [part.astype(F32) for part in split_three(up_ref[0])]
    size = up_ref.shape[1]
    parts.append(jnp.zeros((size, margin - 3 * size), F32))
    to_pair_ref[cases:, :] = jnp.concatenate(parts, axis=1).astype(BF16)


def own_kernel(x_ref, b_hbm, diag_hbm, values_hbm, cols_hbm, cl_hbm, cr_hbm,
               partial_ref, operator_ref, diag_ref, cols_ref, b_ref, values_ref, sems):
    blocks, nonzeros, size = values_hbm.shape[1], values_hbm.shape[2], values_hbm.shape[3]
    rows = x_ref.shape[1]
    margin = cl_hbm.shape[1]
    copies = copy_all(
        [
            (cols_hbm, cols_ref),
            (values_hbm, values_ref),
            (b_hbm, b_ref),
            (diag_hbm, diag_ref),
            (cl_hbm, operator_ref.at[:, rows:rows + margin]),
            (cr_hbm, operator_ref.at[:, rows + margin:]),
        ],
        sems,
    )
    operator_ref[:, :rows] = jnp.zeros((rows, rows), BF16)
    for copy in copies:
        copy.wait()
    for i in range(blocks):
        for t in range(nonzeros):
            start = pl.multiple_of(cols_ref[t, 0, i] * size, size)
            operator_ref[i * size:(i + 1) * size, pl.ds(start, size)] = values_ref[0, i, t]
    x = x_ref[...]
    diag = diag_ref[...].reshape(1, rows)
    partial_ref[...] = b_ref[...] - diag * x - mm_nt(x.astype(BF16), operator_ref[:, :rows])


def offer_kernel(partial_ref, operator_ref, rows_ref, pair_ref, to_other_ref, known_ref, message_ref):
    cases, rows = partial_ref.shape
    margin = rows_ref.shape[2]
    even = is_even()
    left, right = operator_ref[:, rows:rows + margin], operator_ref[:, rows + margin:]
    from_pair = jnp.where(even, right, left)
    from_other = jnp.where(even, left, right)
    known = partial_ref[...] - mm_nt(pair_ref[:cases, :], from_pair)
    known_ref[...] = known
    high = known.astype(BF16)
    low = (known - high.astype(F32)).astype(BF16)
    place = place_matrix(jnp.where(even, rows_ref[0, 0:1, :], rows_ref[0, 1:2, :]), rows)
    message_ref[:cases, :] = to_other_ref[...]
    message_ref[cases:2 * cases, :] = mm(high, place).astype(BF16)
    message_ref[2 * cases:3 * cases, :] = mm(low, place).astype(BF16)
    message_ref[3 * cases:, :] = mm_t(place, from_other).astype(BF16)


def inverse_kernel(first_pair_ref, inverse_hbm, basis_hbm, diag_hbm, up_hbm,
                   inverse_ref, basis_ref, factor_ref, plain_ref, blocks_ref, sems):
    size = diag_hbm.shape[1]
    cases = first_pair_ref.shape[0] - size
    copies = copy_all(
        [
            (diag_hbm, blocks_ref.at[0:1]),
            (up_hbm, blocks_ref.at[1:2]),
            (basis_hbm, basis_ref),
            (inverse_hbm, inverse_ref),
        ],
        sems,
    )
    parts = first_pair_ref[cases:, :].astype(F32)
    up_left = parts[:, :size] + (parts[:, size:2 * size] + parts[:, 2 * size:3 * size])
    for copy in copies[:2]:
        copy.wait()
    last = position() == lax.axis_size("grp") * lax.axis_size("sub") - 1
    up = jnp.where(last, 0.0, blocks_ref[1])
    diag = blocks_ref[0]
    row = lax.broadcasted_iota(jnp.int32, (size, size), 0)
    lane = lax.broadcasted_iota(jnp.int32, (size, size), 1)
    identity = (row == lane).astype(F32)
    factor = reduce_rows([jnp.concatenate([diag, jnp.transpose(up_left), up, identity], axis=1)])[0]
    odd = jnp.concatenate([jnp.transpose(up), factor[:, size:3 * size], jnp.zeros((size, size), F32)], axis=1)
    even = jnp.concatenate([diag, up, jnp.zeros((size, 2 * size), F32)], axis=1)
    plain_ref[...] = jnp.where(is_even(), even, odd)
    lanes = lax.broadcasted_iota(jnp.int32, factor.shape, 1)
    factor_ref[...] = jnp.where(lanes >= 3 * size, factor, 0.0)
    for copy in copies[2:]:
        copy.wait()


def residual_kernel(known_ref, operator_ref, rows_ref, sent_ref, other_ref, loaded_ref, r_ref, rb_ref, to_pair_ref, halo_ref):
    cases, rows = known_ref.shape
    margin = rows_ref.shape[2]
    even = is_even()
    from_other = jnp.where(even, operator_ref[:, rows:rows + margin], operator_ref[:, rows + margin:])
    r = known_ref[...] - mm_nt(other_ref[:cases, :], from_other)
    r_ref[...] = r
    rounded = r.astype(BF16)
    rb_ref[...] = rounded
    place = place_matrix(jnp.where(even, rows_ref[0, 1:2, :], rows_ref[0, 0:1, :]), rows)
    to_pair_ref[...] = mm(rounded, place).astype(BF16)
    offered = other_ref[cases:2 * cases, :].astype(F32) + other_ref[2 * cases:3 * cases, :].astype(F32)
    halo_ref[...] = (offered - mm_nt(sent_ref[...], other_ref[3 * cases:, :])).astype(BF16)


def own_local_kernel(rb_ref, inverse_ref, basis_ref, halo_ref, local_ref, coarse_ref):
    rows = rb_ref.shape[1]
    margin = (inverse_ref.shape[1] - rows) // 2
    even = is_even()
    me = position()
    exists = (me > 0) & (me < lax.axis_size("grp") * lax.axis_size("sub") - 1)
    halo = jnp.where(exists, halo_ref[...], jnp.zeros_like(halo_ref))
    zero = jnp.zeros_like(halo)
    extended = jnp.concatenate([jnp.where(even, halo, zero), rb_ref[...], jnp.where(even, zero, halo)], axis=1)
    local_ref[...] = mm(extended, inverse_ref[0])
    coarse_ref[...] = mm_nt(basis_ref[0], extended)


def local_kernel(own_local_ref, own_coarse_ref, inverse_ref, basis_ref, factor_ref, plain_ref, pair_ref,
                 local_ref, message_ref):
    margin = pair_ref.shape[1]
    even = is_even()
    pair = pair_ref[...]
    total = inverse_ref.shape[1]
    ends = jnp.where(even, basis_ref[0, :, total - margin:], basis_ref[0, :, :margin])
    coarse_in = own_coarse_ref[...] + mm_nt(ends, pair)
    size = coarse_in.shape[0]
    stacked = jnp.concatenate([jnp.zeros((3 * size, coarse_in.shape[1]), F32), coarse_in], axis=0)
    reduced = jnp.dot(factor_ref[...], stacked, precision=lax.Precision.HIGHEST, preferred_element_type=F32)
    right_side = jnp.where(even, coarse_in, reduced)
    message = jnp.concatenate([plain_ref[:, :3 * size], right_side], axis=1)
    for slot in range(message_ref.shape[0]):
        message_ref[slot] = message
    rows = jnp.where(even, inverse_ref[0, total - margin:, :], inverse_ref[0, :margin, :])
    local_ref[...] = own_local_ref[...] + mm(pair, rows)


def reduce_rows(blocks):
    size, width = blocks[0].shape
    panel = 16 if len(blocks) == 1 else 8 if len(blocks) == 2 else 4
    lanes, tile = 128, 8
    here = lax.broadcasted_iota(jnp.int32, (tile, 1), 0)
    tiles = range(size // tile)
    blocks = [[block[t * tile:(t + 1) * tile, :] for t in tiles] for block in blocks]

    def wide(value):
        return jnp.concatenate([value] * (width // lanes), axis=1)

    for first in range(0, size, panel):
        panels = [
            [[jnp.broadcast_to(rows[:, q:q + 1], (tile, lanes)) for rows in block] for q in range(first, first + panel)]
            for block in blocks
        ]
        for a in range(panel):
            at, inside = divmod(first + a, tile)
            for block, columns in zip(blocks, panels):
                column = columns[a]
                inverse = 1.0 / column[at][inside:inside + 1, :]
                for b in range(a + 1, panel):
                    entry = columns[b][at][inside:inside + 1, :] * inverse
                    columns[b] = [
                        jnp.where(here == inside, entry, columns[b][t] - column[t] * entry)
                        if t == at else columns[b][t] - column[t] * entry
                        for t in tiles
                    ]
                row = block[at][inside:inside + 1, :] * wide(inverse)
                for t in tiles:
                    rest = block[t] - wide(column[t]) * row
                    block[t] = jnp.where(here == inside, row, rest) if t == at else rest
    return [jnp.concatenate(block, axis=0) for block in blocks]


def shares(top, bottom, size):
    zero = jnp.zeros((size, size), F32)
    to_left = jnp.concatenate([top[:, size:2 * size], zero, top[:, 2 * size:]], axis=1)
    to_right = jnp.concatenate([bottom[:, 2 * size:3 * size], bottom[:, size:2 * size], zero, bottom[:, 3 * size:]], axis=1)
    return to_left, to_right


def schur(block, solved, size):
    product = -mm_t(block[:, :4 * size], solved, precision=lax.Precision.HIGHEST)
    return shares(product[size:2 * size], product[2 * size:3 * size], size)


def first_schur(previous, block, size):
    highest = lax.Precision.HIGHEST
    zero = jnp.zeros_like(block)
    above = jnp.concatenate([zero, block, zero, zero], axis=0)
    below = jnp.concatenate([block, zero, zero, zero], axis=0)
    top = -jnp.dot(previous[:, :4 * size], above, precision=highest, preferred_element_type=F32)
    bottom = -jnp.dot(block[:, :4 * size], below, precision=highest, preferred_element_type=F32)
    return shares(top, bottom, size)


def own_part(block, size):
    lane = lax.broadcasted_iota(jnp.int32, block.shape, 1)
    return jnp.where((lane >= size) & (lane < 3 * size), 0.0, block)


def combine(chain, parts, step, size):
    for i in range(0, len(chain), 2 * step):
        total = own_part(chain[i], size)
        if i + step in parts:
            total = total + parts[i + step][0]
        if i - step in parts:
            total = total + parts[i - step][1]
        chain[i] = total


def eliminate(chain, size, keep, step=1):
    count = len(chain) - 1
    while step < count:
        inner = list(range(step, count, 2 * step))
        solved = dict(zip(inner, reduce_rows([chain[j] for j in inner])))
        parts = {j: schur(chain[j], solved[j], size) for j in inner}
        for j in inner:
            keep(j, solved[j])
        combine(chain, parts, step, size)
        step = 2 * step
    return chain[0], chain[count]


def back(solved, left, right, size):
    zero = jnp.zeros_like(left)
    stacked = jnp.concatenate([zero, left, right, zero], axis=0)
    return solved[:, 3 * size:] - jnp.dot(
        solved[:, :4 * size], stacked, precision=lax.Precision.HIGHEST, preferred_element_type=F32)


def padded(count):
    total = 1
    while total < count:
        total = 2 * total
    return total


def group_kernel(same_ref, opposite_ref, solved_ref, message_ref):
    half, size, width = same_ref.shape
    members = 2 * half
    even = is_even()
    chain = []
    for j in range(half):
        same, opposite = same_ref[j], opposite_ref[j]
        chain += [jnp.where(even, same, opposite), jnp.where(even, opposite, same)]
    chain.append(jnp.zeros((size, width), F32))

    def keep(j, solved):
        solved_ref[j] = solved

    parts = {}
    for j in range(1, members, 2):
        keep(j, chain[j])
        parts[j] = first_schur(chain[j - 1], chain[j], size)
    combine(chain, parts, 1, size)
    head, tail = eliminate(chain, size, keep, 2)
    message_ref[:size, :] = head
    message_ref[size:, :] = tail


def solve_kernel(reduced_ref, solved_ref, local_ref, basis_ref, rows_ref,
                 corr_ref, to_pair_ref, to_other_ref, sep_ref, x_ref):
    groups, two_size, width = reduced_ref.shape
    size = two_size // 2
    members = solved_ref.shape[0]
    chain = []
    for g in range(groups):
        total = reduced_ref[g, :size, :]
        if g:
            total = total + reduced_ref[g - 1, size:, :]
        chain.append(total)
    count = padded(groups)
    row = lax.broadcasted_iota(jnp.int32, (size, width), 0)
    lane = lax.broadcasted_iota(jnp.int32, (size, width), 1)
    while len(chain) < count:
        chain.append((row == lane).astype(F32))
    chain.append(jnp.zeros((size, width), F32))
    factors = {}
    head, _ = eliminate(chain, size, factors.__setitem__)
    solution = {count: jnp.zeros((size, width - 3 * size), F32)}
    solution[0] = reduce_rows([head])[0][:, 3 * size:]
    step = count // 2
    while step >= 1:
        for j in range(step, count, 2 * step):
            solution[j] = back(factors[j], solution[j - step], solution[j + step], size)
        step = step // 2
    for g in range(groups):
        sep_ref[g] = solution[g]
    sep_ref[groups] = jnp.zeros((size, width - 3 * size), F32)
    group, member = lax.axis_index("grp"), lax.axis_index("sub")
    x_ref[0] = sep_ref[group]
    x_ref[members] = sep_ref[group + 1]
    step = members // 2
    while step >= 2:
        for j in range(step, members, 2 * step):
            x_ref[j] = back(solved_ref[j], x_ref[j - step], x_ref[j + step], size)
        step = step // 2
    odd = member // 2 * 2 + 1
    x_ref[odd] = back(solved_ref[odd], x_ref[odd - 1], x_ref[odd + 1], size)
    coarse = x_ref[member].astype(BF16)
    correction = local_ref[...] + mm_t(coarse, basis_ref[0])
    corr_ref[...] = correction
    margin = rows_ref.shape[2]
    owned = correction.shape[1] - 2 * margin
    rounded = correction.astype(BF16)
    even = is_even()
    head, tail = rounded[:, :margin], rounded[:, margin + owned:]
    sent = mm(rounded[:, margin:margin + owned], send_matrix(rows_ref, owned)).astype(BF16)
    to_pair_ref[:, :margin] = jnp.where(even, tail, head)
    to_other_ref[:, :margin] = jnp.where(even, head, tail)
    to_pair_ref[:, margin:] = sent[:, :margin]
    to_other_ref[:, margin:] = sent[:, margin:]


def image_kernel(corr_ref, r_ref, diag_ref, operator_ref, rows_ref, pair_ref, other_ref, p_ref, image_ref, sums_ref):
    margin = rows_ref.shape[2]
    owned = p_ref.shape[1]
    from_left, from_right = from_sides(pair_ref, other_ref)
    place = place_matrix(jnp.concatenate([rows_ref[0, 0:1, :], rows_ref[0, 1:2, :]], axis=1), owned)
    tails = jnp.concatenate([from_left[:, :margin], from_right[:, :margin]], axis=1)
    p = corr_ref[:, margin:margin + owned] + mm_nt(tails, place)
    p_ref[...] = p
    me = position()
    last = lax.axis_size("grp") * lax.axis_size("sub") - 1
    left = from_left[:, margin:].astype(F32) + corr_ref[:, :margin]
    right = from_right[:, margin:].astype(F32) + corr_ref[:, margin + owned:]
    left = jnp.where(me == 0, 0.0, left).astype(BF16)
    right = jnp.where(me == last, 0.0, right).astype(BF16)
    values = jnp.concatenate([p.astype(BF16), left, right], axis=1)
    image = diag_ref[...].reshape(1, owned) * p + mm_nt(values, operator_ref[...])
    image_ref[...] = image
    ones = jnp.ones((8, owned), F32)
    inner = mm_nt(ones, r_ref[...] * p, precision=lax.Precision.HIGHEST)
    curvature = mm_nt(ones, p * image, precision=lax.Precision.HIGHEST)
    sums = jnp.concatenate([inner[0:1], curvature[0:1]], axis=0)
    for slot in range(sums_ref.shape[0]):
        sums_ref[slot] = sums


def finish_kernel(x_ref, p_ref, r_ref, image_ref, sums_ref, out_x_ref, out_r_ref):
    sums = jnp.sum(sums_ref[...], axis=0)
    row = sums[0:1, :] / sums[1:2, :]
    lanes = 128
    step = jnp.transpose(jnp.broadcast_to(row, (lanes, row.shape[1])))
    for start in range(0, x_ref.shape[1], lanes):
        span = slice(start, start + lanes)
        out_x_ref[:, span] = x_ref[:, span] + step * p_ref[:, span]
        out_r_ref[:, span] = r_ref[:, span] - step * image_ref[:, span]


def call(kernel, out, in_specs, scratch=()):
    return pl.pallas_call(
        kernel,
        out_shape=out,
        in_specs=in_specs,
        out_specs=[VMEM] * len(out),
        scratch_shapes=list(scratch),
        name=kernel.__name__,
        compiler_params=pltpu.CompilerParams(vmem_limit_bytes=16 * 2**20),
    )


def far(*arrays):
    return [pltpu.with_memory_space_constraint(array, pltpu.HBM) for array in arrays]


def struct(shape, dtype):
    return jax.ShapeDtypeStruct(shape, dtype)


def shards(right_side, iterate_in, diagonal, block_values, block_cols, couple_left, couple_right, send_rows,
           local_inverse, coarse_basis, coarse_diag, coarse_up):
    groups, members = lax.axis_size("grp"), lax.axis_size("sub")
    total = groups * members
    rows, cases = right_side.shape
    margin = send_rows.shape[2]
    extended = local_inverse.shape[1]
    modes = coarse_basis.shape[2]
    width = 3 * modes + cases
    pairs = [(i, i ^ 1) for i in range(total)]
    others = [(i, i + 1 if i % 2 else i - 1) for i in range(1, total - 1)]
    right_side, iterate_in = right_side.T, iterate_in.T
    basis = jnp.swapaxes(coarse_basis, 1, 2)
    block_cols = jnp.transpose(block_cols, (2, 0, 1))

    halo = struct((cases, margin), BF16)
    full = struct((cases, rows), F32)
    semaphores = pltpu.SemaphoreType.DMA
    to_pair, to_other, start, send_rows = call(
        gather_kernel,
        [struct((cases + modes, margin), BF16), halo, full, struct(send_rows.shape, send_rows.dtype)],
        [HBM] * 3,
        [pltpu.VMEM(coarse_up.shape, F32), semaphores((3,))],
    )(*far(iterate_in, send_rows, coarse_up))
    first_pair = lax.ppermute(to_pair, AXES, pairs)
    partial, operator, diag = call(
        own_kernel,
        [full, struct((rows, rows + 2 * margin), BF16), struct(diagonal.shape, F32)],
        [VMEM] + [HBM] * 6,
        [
            pltpu.SMEM(block_cols.shape, block_cols.dtype),
            pltpu.VMEM((cases, rows), F32),
            pltpu.VMEM(block_values.shape, BF16),
            semaphores((6,)),
        ],
    )(start, *far(right_side, diagonal, block_values, block_cols, couple_left, couple_right))
    known, message = call(offer_kernel, [full, struct((3 * cases + margin, margin), BF16)], [VMEM] * 5)(
        partial, operator, send_rows, first_pair, to_other
    )
    first_other = lax.ppermute(message, AXES, others)
    inverse, basis, factor, plain = call(
        inverse_kernel,
        [
            struct(local_inverse.shape, BF16),
            struct(basis.shape, BF16),
            struct((modes, 4 * modes), F32),
            struct((modes, 4 * modes), F32),
        ],
        [VMEM] + [HBM] * 4,
        [pltpu.VMEM((2, modes, modes), F32), semaphores((4,))],
    )(first_pair, *far(local_inverse, basis, coarse_diag, coarse_up))
    residual, rounded, to_pair, other_halo = call(
        residual_kernel, [full, struct((cases, rows), BF16), halo, halo], [VMEM] * 6
    )(known, operator, send_rows, to_other, first_other, plain)
    pair_halo = lax.ppermute(to_pair, AXES, pairs)
    local, coarse = call(own_local_kernel, [struct((cases, extended), F32), struct((modes, cases), F32)], [VMEM] * 4)(
        rounded, inverse, basis, other_halo
    )
    chips = members // 2
    local, message = call(
        local_kernel, [struct((cases, extended), F32), struct((chips, modes, width), F32)], [VMEM] * 7
    )(local, coarse, inverse, basis, factor, plain, pair_halo)
    cores = [[2 * chip + core for chip in range(chips)] for core in range(2)]
    same = lax.all_to_all(message, "sub", 0, 0, tiled=True, axis_index_groups=cores)
    opposite = lax.ppermute(same, AXES, pairs)
    solved, reduced = call(
        group_kernel, [struct((members, modes, width), F32), struct((2 * modes, width), F32)], [VMEM] * 2
    )(same, opposite)
    reduced = lax.all_gather(reduced, "grp", axis=0)
    correction, *sent = call(
        solve_kernel,
        [struct((cases, extended), F32)] + [struct((cases, 2 * margin), BF16)] * 2,
        [VMEM] * 5,
        [pltpu.VMEM((groups + 1, modes, cases), F32), pltpu.VMEM((members + 1, modes, cases), F32)],
    )(reduced, solved, local, basis, send_rows)
    to_pair, to_other = sent
    from_other = lax.ppermute(to_other, AXES, others)
    from_pair = lax.ppermute(to_pair, AXES, pairs)
    direction, image, sums = call(image_kernel, [full, full, struct((total, 2, cases), F32)], [VMEM] * 7)(
        correction, residual, diag, operator, send_rows, from_pair, from_other
    )
    sums = lax.all_to_all(sums, AXES, 0, 0, tiled=True)
    iterate, residual = call(finish_kernel, [full, full], [VMEM] * 5)(start, direction, residual, image, sums)
    return iterate.T, residual.T


def solution(mesh):
    whole = P(AXES)

    def spec(rank):
        return P(AXES, *([None] * (rank - 1)))

    return jax.shard_map(
        shards,
        mesh=mesh,
        in_specs=tuple(spec(rank) for rank in (2, 2, 1, 5, 3, 2, 2, 3, 3, 3, 3, 3)),
        out_specs=(spec(2), spec(2)),
        check_vma=False,
    )
```

```python
import jax
import jax.numpy as jnp
from jax import lax
from jax.experimental import pallas as pl
from jax.experimental.pallas import tpu as pltpu
from jax.sharding import PartitionSpec as P


AXES = ("grp", "sub")
BF16 = jnp.bfloat16
F32 = jnp.float32
VMEM = pl.BlockSpec(memory_space=pltpu.VMEM)
HBM = pl.BlockSpec(memory_space=pltpu.HBM)


def mm(a, b):
    return jnp.dot(a, b, preferred_element_type=F32)


def mm_t(a, b, **kw):
    return lax.dot_general(a, b, (((0,), (0,)), ((), ())), preferred_element_type=F32, **kw)


def mm_nt(a, b, **kw):
    return lax.dot_general(a, b, (((1,), (1,)), ((), ())), preferred_element_type=F32, **kw)


def position():
    return lax.axis_index("grp") * lax.axis_size("sub") + lax.axis_index("sub")


def is_even():
    return position() % 2 == 0


def place_matrix(row, total):
    place = lax.broadcasted_iota(jnp.int32, (total, row.shape[1]), 0)
    return (place == row).astype(F32).astype(BF16)


def send_matrix(rows_ref, total):
    left, right = rows_ref[0, 0:1, :], rows_ref[0, 1:2, :]
    even = is_even()
    rows = jnp.concatenate([jnp.where(even, right, left), jnp.where(even, left, right)], axis=1)
    return place_matrix(rows, total)


def from_sides(pair_ref, other_ref):
    even = is_even()
    other = other_ref[...]
    pair = pair_ref[:other.shape[0], :]
    return jnp.where(even, other, pair), jnp.where(even, pair, other)


def copy_all(copies, sems):
    started = [pltpu.make_async_copy(source, target, sems.at[n]) for n, (source, target) in enumerate(copies)]
    for copy in started:
        copy.start()
    return started


def split_three(value):
    high = value.astype(BF16)
    rest = value - high.astype(F32)
    middle = rest.astype(BF16)
    return high, middle, (rest - middle.astype(F32)).astype(BF16)


def gather_kernel(x_hbm, rows_hbm, up_hbm, to_pair_ref, to_other_ref, x_ref, rows_ref, up_ref, sems):
    for copy in copy_all([(rows_hbm, rows_ref), (up_hbm, up_ref), (x_hbm, x_ref)], sems):
        copy.wait()
    values = x_ref[...].astype(BF16)
    cases = values.shape[0]
    margin = rows_ref.shape[2]
    sent = mm(values, send_matrix(rows_ref, values.shape[1])).astype(BF16)
    to_pair_ref[:cases, :] = sent[:, :margin]
    to_other_ref[...] = sent[:, margin:]
    parts = [part.astype(F32) for part in split_three(up_ref[0])]
    size = up_ref.shape[1]
    parts.append(jnp.zeros((size, margin - 3 * size), F32))
    to_pair_ref[cases:, :] = jnp.concatenate(parts, axis=1).astype(BF16)


def own_kernel(x_ref, b_hbm, diag_hbm, values_hbm, cols_hbm, cl_hbm, cr_hbm,
               partial_ref, operator_ref, diag_ref, cols_ref, b_ref, values_ref, sems):
    blocks, nonzeros, size = values_hbm.shape[1], values_hbm.shape[2], values_hbm.shape[3]
    rows = x_ref.shape[1]
    margin = cl_hbm.shape[1]
    copies = copy_all(
        [
            (cols_hbm, cols_ref),
            (values_hbm, values_ref),
            (b_hbm, b_ref),
            (diag_hbm, diag_ref),
            (cl_hbm, operator_ref.at[:, rows:rows + margin]),
            (cr_hbm, operator_ref.at[:, rows + margin:]),
        ],
        sems,
    )
    operator_ref[:, :rows] = jnp.zeros((rows, rows), BF16)
    for copy in copies:
        copy.wait()
    for i in range(blocks):
        for t in range(nonzeros):
            start = pl.multiple_of(cols_ref[t, 0, i] * size, size)
            operator_ref[i * size:(i + 1) * size, pl.ds(start, size)] = values_ref[0, i, t]
    x = x_ref[...]
    diag = diag_ref[...].reshape(1, rows)
    partial_ref[...] = b_ref[...] - diag * x - mm_nt(x.astype(BF16), operator_ref[:, :rows])


def offer_kernel(partial_ref, operator_ref, rows_ref, pair_ref, to_other_ref, known_ref, message_ref):
    cases, rows = partial_ref.shape
    margin = rows_ref.shape[2]
    even = is_even()
    left, right = operator_ref[:, rows:rows + margin], operator_ref[:, rows + margin:]
    from_pair = jnp.where(even, right, left)
    from_other = jnp.where(even, left, right)
    known = partial_ref[...] - mm_nt(pair_ref[:cases, :], from_pair)
    known_ref[...] = known
    high = known.astype(BF16)
    low = (known - high.astype(F32)).astype(BF16)
    place = place_matrix(jnp.where(even, rows_ref[0, 0:1, :], rows_ref[0, 1:2, :]), rows)
    message_ref[:cases, :] = to_other_ref[...]
    message_ref[cases:2 * cases, :] = mm(high, place).astype(BF16)
    message_ref[2 * cases:3 * cases, :] = mm(low, place).astype(BF16)
    message_ref[3 * cases:, :] = mm_t(place, from_other).astype(BF16)


def inverse_kernel(first_pair_ref, inverse_hbm, basis_hbm, diag_hbm, up_hbm,
                   inverse_ref, basis_ref, factor_ref, plain_ref, blocks_ref, sems):
    size = diag_hbm.shape[1]
    cases = first_pair_ref.shape[0] - size
    copies = copy_all(
        [
            (diag_hbm, blocks_ref.at[0:1]),
            (up_hbm, blocks_ref.at[1:2]),
            (basis_hbm, basis_ref),
            (inverse_hbm, inverse_ref),
        ],
        sems,
    )
    parts = first_pair_ref[cases:, :].astype(F32)
    up_left = parts[:, :size] + (parts[:, size:2 * size] + parts[:, 2 * size:3 * size])
    for copy in copies[:2]:
        copy.wait()
    last = position() == lax.axis_size("grp") * lax.axis_size("sub") - 1
    up = jnp.where(last, 0.0, blocks_ref[1])
    diag = blocks_ref[0]
    row = lax.broadcasted_iota(jnp.int32, (size, size), 0)
    lane = lax.broadcasted_iota(jnp.int32, (size, size), 1)
    identity = (row == lane).astype(F32)
    factor = reduce_rows([jnp.concatenate([diag, jnp.transpose(up_left), up, identity], axis=1)])[0]
    odd = jnp.concatenate([jnp.transpose(up), factor[:, size:3 * size], jnp.zeros((size, size), F32)], axis=1)
    even = jnp.concatenate([diag, up, jnp.zeros((size, 2 * size), F32)], axis=1)
    plain_ref[...] = jnp.where(is_even(), even, odd)
    lanes = lax.broadcasted_iota(jnp.int32, factor.shape, 1)
    factor_ref[...] = jnp.where(lanes >= 3 * size, factor, 0.0)
    for copy in copies[2:]:
        copy.wait()


def residual_kernel(known_ref, operator_ref, rows_ref, sent_ref, other_ref, loaded_ref, r_ref, rb_ref, to_pair_ref, halo_ref):
    cases, rows = known_ref.shape
    margin = rows_ref.shape[2]
    even = is_even()
    from_other = jnp.where(even, operator_ref[:, rows:rows + margin], operator_ref[:, rows + margin:])
    r = known_ref[...] - mm_nt(other_ref[:cases, :], from_other)
    r_ref[...] = r
    rounded = r.astype(BF16)
    rb_ref[...] = rounded
    place = place_matrix(jnp.where(even, rows_ref[0, 1:2, :], rows_ref[0, 0:1, :]), rows)
    to_pair_ref[...] = mm(rounded, place).astype(BF16)
    offered = other_ref[cases:2 * cases, :].astype(F32) + other_ref[2 * cases:3 * cases, :].astype(F32)
    halo_ref[...] = (offered - mm_nt(sent_ref[...], other_ref[3 * cases:, :])).astype(BF16)


def own_local_kernel(rb_ref, inverse_ref, basis_ref, halo_ref, local_ref, coarse_ref):
    even = is_even()
    me = position()
    exists = (me > 0) & (me < lax.axis_size("grp") * lax.axis_size("sub") - 1)
    halo = jnp.where(exists, halo_ref[...], jnp.zeros_like(halo_ref))
    zero = jnp.zeros_like(halo)
    extended = jnp.concatenate([jnp.where(even, halo, zero), rb_ref[...], jnp.where(even, zero, halo)], axis=1)
    local_ref[...] = mm(extended, inverse_ref[0])
    coarse_ref[...] = mm_nt(basis_ref[0], extended)


def local_kernel(own_local_ref, own_coarse_ref, inverse_ref, basis_ref, factor_ref, plain_ref, pair_ref,
                 local_ref, message_ref):
    margin = pair_ref.shape[1]
    even = is_even()
    pair = pair_ref[...]
    total = inverse_ref.shape[1]
    ends = jnp.where(even, basis_ref[0, :, total - margin:], basis_ref[0, :, :margin])
    coarse_in = own_coarse_ref[...] + mm_nt(ends, pair)
    size = coarse_in.shape[0]
    stacked = jnp.concatenate([jnp.zeros((3 * size, coarse_in.shape[1]), F32), coarse_in], axis=0)
    reduced = jnp.dot(factor_ref[...], stacked, precision=lax.Precision.HIGHEST, preferred_element_type=F32)
    right_side = jnp.where(even, coarse_in, reduced)
    message = jnp.concatenate([plain_ref[:, :3 * size], right_side], axis=1)
    for slot in range(message_ref.shape[0]):
        message_ref[slot] = message
    rows = jnp.where(even, inverse_ref[0, total - margin:, :], inverse_ref[0, :margin, :])
    local_ref[...] = own_local_ref[...] + mm(pair, rows)


def reduce_rows(blocks):
    size, width = blocks[0].shape
    panel = 16 if len(blocks) == 1 else 8 if len(blocks) == 2 else 4
    lanes, tile = 128, 8
    here = lax.broadcasted_iota(jnp.int32, (tile, 1), 0)
    tiles = range(size // tile)
    blocks = [[block[t * tile:(t + 1) * tile, :] for t in tiles] for block in blocks]

    def wide(value):
        return jnp.concatenate([value] * (width // lanes), axis=1)

    for first in range(0, size, panel):
        panels = [
            [[jnp.broadcast_to(rows[:, q:q + 1], (tile, lanes)) for rows in block] for q in range(first, first + panel)]
            for block in blocks
        ]
        for a in range(panel):
            at, inside = divmod(first + a, tile)
            for block, columns in zip(blocks, panels):
                column = columns[a]
                inverse = 1.0 / column[at][inside:inside + 1, :]
                for b in range(a + 1, panel):
                    entry = columns[b][at][inside:inside + 1, :] * inverse
                    columns[b] = [
                        jnp.where(here == inside, entry, columns[b][t] - column[t] * entry)
                        if t == at else columns[b][t] - column[t] * entry
                        for t in tiles
                    ]
                row = block[at][inside:inside + 1, :] * wide(inverse)
                for t in tiles:
                    rest = block[t] - wide(column[t]) * row
                    block[t] = jnp.where(here == inside, row, rest) if t == at else rest
    return [jnp.concatenate(block, axis=0) for block in blocks]


def shares(top, bottom, size):
    lanes = 4 * size
    lane = lax.broadcasted_iota(jnp.int32, (size, lanes), 1)

    def placed(product, slot, empty):
        first = product[:, :lanes]
        diag = pltpu.roll(first, lanes - slot * size, axis=1)
        first = jnp.where(lane < size, diag, jnp.where((lane >= empty * size) & (lane < (empty + 1) * size), 0.0, first))
        return jnp.concatenate([first, product[:, lanes:]], axis=1)

    return placed(top, 1, 1), placed(bottom, 2, 2)


def schur(block, solved, size):
    couplings = jnp.transpose(block[:, :4 * size])[size:3 * size]
    product = -jnp.dot(couplings, solved, precision=lax.Precision.HIGHEST, preferred_element_type=F32)
    return shares(product[:size], product[size:], size)


def first_schur(previous, block, size):
    highest = lax.Precision.HIGHEST
    zero = jnp.zeros_like(block)
    above = jnp.concatenate([zero, block, zero, zero], axis=0)
    below = jnp.concatenate([block, zero, zero, zero], axis=0)
    top = -jnp.dot(previous[:, :4 * size], above, precision=highest, preferred_element_type=F32)
    bottom = -jnp.dot(block[:, :4 * size], below, precision=highest, preferred_element_type=F32)
    return shares(top, bottom, size)


def own_part(block, size):
    lane = lax.broadcasted_iota(jnp.int32, block.shape, 1)
    return jnp.where((lane >= size) & (lane < 3 * size), 0.0, block)


def combine(chain, parts, step, size):
    for i in range(0, len(chain), 2 * step):
        total = own_part(chain[i], size)
        if i + step in parts:
            total = total + parts[i + step][0]
        if i - step in parts:
            total = total + parts[i - step][1]
        chain[i] = total


def eliminate(chain, size, keep, step=1):
    count = len(chain) - 1
    while step < count:
        inner = list(range(step, count, 2 * step))
        solved = dict(zip(inner, reduce_rows([chain[j] for j in inner])))
        parts = {j: schur(chain[j], solved[j], size) for j in inner}
        for j in inner:
            keep(j, solved[j])
        combine(chain, parts, step, size)
        step = 2 * step
    return chain[0], chain[count]


def back(solved, left, right, size):
    zero = jnp.zeros_like(left)
    stacked = jnp.concatenate([zero, left, right, zero], axis=0)
    return solved - jnp.dot(
        solved[:, :4 * size], stacked, precision=lax.Precision.HIGHEST, preferred_element_type=F32)


def padded(count):
    total = 1
    while total < count:
        total = 2 * total
    return total


def group_kernel(same_ref, opposite_ref, solved_ref, message_ref):
    half, size, width = same_ref.shape
    members = 2 * half
    even = is_even()
    chain = []
    for j in range(half):
        same, opposite = same_ref[j], opposite_ref[j]
        chain += [jnp.where(even, same, opposite), jnp.where(even, opposite, same)]
    chain.append(jnp.zeros((size, width), F32))

    def keep(j, solved):
        solved_ref[j] = solved

    parts = {}
    for j in range(1, members, 2):
        keep(j, chain[j])
        parts[j] = first_schur(chain[j - 1], chain[j], size)
    combine(chain, parts, 1, size)
    head, tail = eliminate(chain, size, keep, 2)
    message_ref[:size, :] = head
    message_ref[size:, :] = tail


def solve_kernel(reduced_ref, solved_ref, local_ref, basis_ref, rows_ref,
                 corr_ref, to_other_ref, sep_ref, x_ref):
    groups, two_size, width = reduced_ref.shape
    size = two_size // 2
    members = solved_ref.shape[0]
    chain = []
    for g in range(groups):
        total = reduced_ref[g, :size, :]
        if g:
            total = total + reduced_ref[g - 1, size:, :]
        chain.append(total)
    count = padded(groups)
    row = lax.broadcasted_iota(jnp.int32, (size, width), 0)
    lane = lax.broadcasted_iota(jnp.int32, (size, width), 1)
    while len(chain) < count:
        chain.append((row == lane).astype(F32))
    chain.append(jnp.zeros((size, width), F32))
    factors = {}
    head, _ = eliminate(chain, size, factors.__setitem__)
    solution = {count: jnp.zeros((size, width), F32)}
    solution[0] = reduce_rows([head])[0]
    step = count // 2
    while step >= 1:
        for j in range(step, count, 2 * step):
            solution[j] = back(factors[j], solution[j - step], solution[j + step], size)
        step = step // 2
    for g in range(groups):
        sep_ref[g] = solution[g]
    sep_ref[groups] = jnp.zeros((size, width), F32)
    group, member = lax.axis_index("grp"), lax.axis_index("sub")
    x_ref[0] = sep_ref[group]
    x_ref[members] = sep_ref[group + 1]
    step = members // 2
    while step >= 2:
        for j in range(step, members, 2 * step):
            x_ref[j] = back(solved_ref[j], x_ref[j - step], x_ref[j + step], size)
        step = step // 2
    odd = member // 2 * 2 + 1
    x_ref[odd] = back(solved_ref[odd], x_ref[odd - 1], x_ref[odd + 1], size)
    coarse = x_ref[member].astype(BF16)
    correction = local_ref[...] + mm_t(coarse, basis_ref[0])[3 * size:]
    corr_ref[...] = correction
    even = is_even()
    to_other_ref[...] = return_rows(
        correction, rows_ref.shape[2], jnp.where(even, rows_ref[0, 0:1, :], rows_ref[0, 1:2, :]), even)


def return_rows(correction, margin, rows, head):
    owned = correction.shape[1] - 2 * margin
    rounded = correction.astype(BF16)
    tail = jnp.where(head, rounded[:, :margin], rounded[:, margin + owned:])
    return jnp.concatenate([tail, mm(rounded[:, margin:margin + owned], place_matrix(rows, owned)).astype(BF16)], axis=1)


def pair_kernel(corr_ref, rows_ref, to_pair_ref):
    even = is_even()
    to_pair_ref[...] = return_rows(
        corr_ref[...], rows_ref.shape[2], jnp.where(even, rows_ref[0, 1:2, :], rows_ref[0, 0:1, :]), jnp.logical_not(even))


def row_sum(values):
    lanes = 128
    total = values[:, :lanes]
    for start in range(lanes, values.shape[1], lanes):
        total = total + values[:, start:start + lanes]
    return mm_nt(jnp.ones((8, lanes), F32), total, precision=lax.Precision.HIGHEST)


def image_kernel(corr_ref, r_ref, diag_ref, operator_ref, rows_ref, pair_ref, other_ref, p_ref, image_ref, sums_ref):
    margin = rows_ref.shape[2]
    owned = p_ref.shape[1]
    from_left, from_right = from_sides(pair_ref, other_ref)
    place = place_matrix(jnp.concatenate([rows_ref[0, 0:1, :], rows_ref[0, 1:2, :]], axis=1), owned)
    tails = jnp.concatenate([from_left[:, :margin], from_right[:, :margin]], axis=1)
    p = corr_ref[:, margin:margin + owned] + mm_nt(tails, place)
    p_ref[...] = p
    me = position()
    last = lax.axis_size("grp") * lax.axis_size("sub") - 1
    left = from_left[:, margin:].astype(F32) + corr_ref[:, :margin]
    right = from_right[:, margin:].astype(F32) + corr_ref[:, margin + owned:]
    left = jnp.where(me == 0, 0.0, left).astype(BF16)
    right = jnp.where(me == last, 0.0, right).astype(BF16)
    values = jnp.concatenate([p.astype(BF16), left, right], axis=1)
    image = diag_ref[...].reshape(1, owned) * p + mm_nt(values, operator_ref[...])
    image_ref[...] = image
    inner = row_sum(r_ref[...] * p)
    curvature = row_sum(p * image)
    sums = jnp.concatenate([inner[0:1], curvature[0:1]], axis=0)
    for slot in range(sums_ref.shape[0]):
        sums_ref[slot] = sums


def finish_kernel(x_ref, p_ref, r_ref, image_ref, sums_ref, out_x_ref, out_r_ref):
    sums = jnp.sum(sums_ref[...], axis=0)
    row = sums[0:1, :] / sums[1:2, :]
    lanes = 128
    step = jnp.transpose(jnp.broadcast_to(row, (lanes, row.shape[1])))
    for start in range(0, x_ref.shape[1], lanes):
        span = slice(start, start + lanes)
        out_x_ref[:, span] = x_ref[:, span] + step * p_ref[:, span]
        out_r_ref[:, span] = r_ref[:, span] - step * image_ref[:, span]


def call(kernel, out, in_specs, scratch=()):
    return pl.pallas_call(
        kernel,
        out_shape=out,
        in_specs=in_specs,
        out_specs=[VMEM] * len(out),
        scratch_shapes=list(scratch),
        compiler_params=pltpu.CompilerParams(vmem_limit_bytes=16 * 2**20),
    )


def far(*arrays):
    return [pltpu.with_memory_space_constraint(array, pltpu.HBM) for array in arrays]


def struct(shape, dtype):
    return jax.ShapeDtypeStruct(shape, dtype)


def shards(right_side, iterate_in, diagonal, block_values, block_cols, couple_left, couple_right, send_rows,
           local_inverse, coarse_basis, coarse_diag, coarse_up):
    groups, members = lax.axis_size("grp"), lax.axis_size("sub")
    total = groups * members
    rows, cases = right_side.shape
    margin = send_rows.shape[2]
    extended = local_inverse.shape[1]
    modes = coarse_basis.shape[2]
    width = 3 * modes + cases
    pairs = [(i, i ^ 1) for i in range(total)]
    others = [(i, i + 1 if i % 2 else i - 1) for i in range(1, total - 1)]
    right_side, iterate_in = right_side.T, iterate_in.T
    basis = jnp.swapaxes(coarse_basis, 1, 2)
    block_cols = jnp.transpose(block_cols, (2, 0, 1))

    halo = struct((cases, margin), BF16)
    full = struct((cases, rows), F32)
    semaphores = pltpu.SemaphoreType.DMA
    to_pair, to_other, start, send_rows = call(
        gather_kernel,
        [struct((cases + modes, margin), BF16), halo, full, struct(send_rows.shape, send_rows.dtype)],
        [HBM] * 3,
        [pltpu.VMEM(coarse_up.shape, F32), semaphores((3,))],
    )(*far(iterate_in, send_rows, coarse_up))
    first_pair = lax.ppermute(to_pair, AXES, pairs)
    partial, operator, diag = call(
        own_kernel,
        [full, struct((rows, rows + 2 * margin), BF16), struct(diagonal.shape, F32)],
        [VMEM] + [HBM] * 6,
        [
            pltpu.SMEM(block_cols.shape, block_cols.dtype),
            pltpu.VMEM((cases, rows), F32),
            pltpu.VMEM(block_values.shape, BF16),
            semaphores((6,)),
        ],
    )(start, *far(right_side, diagonal, block_values, block_cols, couple_left, couple_right))
    known, message = call(offer_kernel, [full, struct((3 * cases + margin, margin), BF16)], [VMEM] * 5)(
        partial, operator, send_rows, first_pair, to_other
    )
    first_other = lax.ppermute(message, AXES, others)
    inverse, basis, factor, plain = call(
        inverse_kernel,
        [
            struct(local_inverse.shape, BF16),
            struct(basis.shape, BF16),
            struct((modes, 4 * modes), F32),
            struct((modes, 4 * modes), F32),
        ],
        [VMEM] + [HBM] * 4,
        [pltpu.VMEM((2, modes, modes), F32), semaphores((4,))],
    )(first_pair, *far(local_inverse, basis, coarse_diag, coarse_up))
    residual, rounded, to_pair, other_halo = call(
        residual_kernel, [full, struct((cases, rows), BF16), halo, halo], [VMEM] * 6
    )(known, operator, send_rows, to_other, first_other, plain)
    pair_halo = lax.ppermute(to_pair, AXES, pairs)
    local, coarse = call(own_local_kernel, [struct((cases, extended), F32), struct((modes, cases), F32)], [VMEM] * 4)(
        rounded, inverse, basis, other_halo
    )
    chips = members // 2
    local, message = call(
        local_kernel, [struct((cases, extended), F32), struct((chips, modes, width), F32)], [VMEM] * 7
    )(local, coarse, inverse, basis, factor, plain, pair_halo)
    cores = [[2 * chip + core for chip in range(chips)] for core in range(2)]
    same = lax.all_to_all(message, "sub", 0, 0, tiled=True, axis_index_groups=cores)
    opposite = lax.ppermute(same, AXES, pairs)
    solved, reduced = call(
        group_kernel, [struct((members, modes, width), F32), struct((2 * modes, width), F32)], [VMEM] * 2
    )(same, opposite)
    reduced = lax.all_gather(reduced, "grp", axis=0)
    returned = struct((cases, 2 * margin), BF16)
    correction, to_other = call(
        solve_kernel,
        [struct((cases, extended), F32), returned],
        [VMEM] * 5,
        [pltpu.VMEM((groups + 1, modes, width), F32), pltpu.VMEM((members + 1, modes, width), F32)],
    )(reduced, solved, local, basis, send_rows)
    from_other = lax.ppermute(to_other, AXES, others)
    (to_pair,) = call(pair_kernel, [returned], [VMEM] * 2)(correction, send_rows)
    from_pair = lax.ppermute(to_pair, AXES, pairs)
    direction, image, sums = call(image_kernel, [full, full, struct((total, 2, cases), F32)], [VMEM] * 7)(
        correction, residual, diag, operator, send_rows, from_pair, from_other
    )
    sums = lax.all_to_all(sums, AXES, 0, 0, tiled=True)
    iterate, residual = call(finish_kernel, [full, full], [VMEM] * 5)(start, direction, residual, image, sums)
    return iterate.T, residual.T


def solution(mesh):
    def spec(rank):
        return P(AXES, *([None] * (rank - 1)))

    return jax.shard_map(
        shards,
        mesh=mesh,
        in_specs=tuple(spec(rank) for rank in (2, 2, 1, 5, 3, 2, 2, 3, 3, 3, 3, 3)),
        out_specs=(spec(2), spec(2)),
        check_vma=False,
    )
```

```python
import jax
import jax.numpy as jnp
from jax import lax
from jax.experimental import pallas as pl
from jax.experimental.pallas import tpu as pltpu
from jax.sharding import PartitionSpec as P


AXES = ("grp", "sub")
BF16 = jnp.bfloat16
F32 = jnp.float32
VMEM = pl.BlockSpec(memory_space=pltpu.VMEM)
HBM = pl.BlockSpec(memory_space=pltpu.HBM)


def mm(a, b):
    return jnp.dot(a, b, preferred_element_type=F32)


def mm_t(a, b, **kw):
    return lax.dot_general(a, b, (((0,), (0,)), ((), ())), preferred_element_type=F32, **kw)


def mm_nt(a, b, **kw):
    return lax.dot_general(a, b, (((1,), (1,)), ((), ())), preferred_element_type=F32, **kw)


def position():
    return lax.axis_index("grp") * lax.axis_size("sub") + lax.axis_index("sub")


def is_even():
    return position() % 2 == 0


def place_matrix(row, total):
    place = lax.broadcasted_iota(jnp.int32, (total, row.shape[1]), 0)
    return (place == row).astype(F32).astype(BF16)


def send_matrix(rows_ref, total):
    left, right = rows_ref[0, 0:1, :], rows_ref[0, 1:2, :]
    even = is_even()
    rows = jnp.concatenate([jnp.where(even, right, left), jnp.where(even, left, right)], axis=1)
    return place_matrix(rows, total)


def from_sides(pair_ref, other_ref):
    even = is_even()
    other = other_ref[...]
    pair = pair_ref[:other.shape[0], :]
    return jnp.where(even, other, pair), jnp.where(even, pair, other)


def copy_all(copies, sems):
    started = [pltpu.make_async_copy(source, target, sems.at[n]) for n, (source, target) in enumerate(copies)]
    for copy in started:
        copy.start()
    return started


def split_three(value):
    high = value.astype(BF16)
    rest = value - high.astype(F32)
    middle = rest.astype(BF16)
    return high, middle, (rest - middle.astype(F32)).astype(BF16)


def load_kernel(x_hbm, rows_hbm, up_hbm, b_hbm, diag_hbm, values_hbm, cols_hbm, cl_hbm, cr_hbm,
                to_pair_ref, to_other_ref, x_ref, rows_ref, b_ref, diag_ref, operator_ref,
                up_ref, cols_ref, values_ref, sems):
    blocks, nonzeros, size = values_hbm.shape[1], values_hbm.shape[2], values_hbm.shape[3]
    cases, rows = x_ref.shape
    margin = rows_ref.shape[2]
    copies = copy_all(
        [
            (rows_hbm, rows_ref),
            (x_hbm, x_ref),
            (up_hbm, up_ref),
            (cols_hbm, cols_ref),
            (values_hbm, values_ref),
            (cl_hbm, operator_ref.at[:, rows:rows + margin]),
            (cr_hbm, operator_ref.at[:, rows + margin:]),
            (diag_hbm, diag_ref),
            (b_hbm, b_ref),
        ],
        sems,
    )
    operator_ref[:, :rows] = jnp.zeros((rows, rows), BF16)
    for copy in copies[:3]:
        copy.wait()
    sent = mm(x_ref[...].astype(BF16), send_matrix(rows_ref, rows)).astype(BF16)
    to_pair_ref[:cases, :] = sent[:, :margin]
    to_other_ref[...] = sent[:, margin:]
    parts = [part.astype(F32) for part in split_three(up_ref[0])]
    modes = up_ref.shape[1]
    parts.append(jnp.zeros((modes, margin - 3 * modes), F32))
    to_pair_ref[cases:, :] = jnp.concatenate(parts, axis=1).astype(BF16)
    for copy in copies[3:]:
        copy.wait()
    for i in range(blocks):
        for t in range(nonzeros):
            start = pl.multiple_of(cols_ref[t, 0, i] * size, size)
            operator_ref[i * size:(i + 1) * size, pl.ds(start, size)] = values_ref[0, i, t]


def own_kernel(x_ref, b_ref, diag_ref, operator_ref, partial_ref):
    x = x_ref[...]
    rows = x.shape[1]
    diag = diag_ref[...].reshape(1, rows)
    partial_ref[...] = b_ref[...] - diag * x - mm_nt(x.astype(BF16), operator_ref[:, :rows])


def offer_kernel(partial_ref, operator_ref, rows_ref, pair_ref, to_other_ref, known_ref, message_ref):
    cases, rows = partial_ref.shape
    margin = rows_ref.shape[2]
    even = is_even()
    left, right = operator_ref[:, rows:rows + margin], operator_ref[:, rows + margin:]
    from_pair = jnp.where(even, right, left)
    from_other = jnp.where(even, left, right)
    known = partial_ref[...] - mm_nt(pair_ref[:cases, :], from_pair)
    known_ref[...] = known
    high = known.astype(BF16)
    low = (known - high.astype(F32)).astype(BF16)
    place = place_matrix(jnp.where(even, rows_ref[0, 0:1, :], rows_ref[0, 1:2, :]), rows)
    message_ref[:cases, :] = to_other_ref[...]
    message_ref[cases:2 * cases, :] = mm(high, place).astype(BF16)
    message_ref[2 * cases:3 * cases, :] = mm(low, place).astype(BF16)
    message_ref[3 * cases:, :] = mm_t(place, from_other).astype(BF16)


def inverse_kernel(first_pair_ref, inverse_hbm, basis_hbm, diag_hbm, up_hbm,
                   inverse_ref, basis_ref, factor_ref, plain_ref, blocks_ref, sems):
    size = diag_hbm.shape[1]
    cases = first_pair_ref.shape[0] - size
    copies = copy_all(
        [
            (diag_hbm, blocks_ref.at[0:1]),
            (up_hbm, blocks_ref.at[1:2]),
            (basis_hbm, basis_ref),
            (inverse_hbm, inverse_ref),
        ],
        sems,
    )
    parts = first_pair_ref[cases:, :].astype(F32)
    up_left = parts[:, :size] + (parts[:, size:2 * size] + parts[:, 2 * size:3 * size])
    for copy in copies[:2]:
        copy.wait()
    last = position() == lax.axis_size("grp") * lax.axis_size("sub") - 1
    up = jnp.where(last, 0.0, blocks_ref[1])
    diag = blocks_ref[0]
    row = lax.broadcasted_iota(jnp.int32, (size, size), 0)
    lane = lax.broadcasted_iota(jnp.int32, (size, size), 1)
    identity = (row == lane).astype(F32)
    factor = reduce_rows([jnp.concatenate([diag, jnp.transpose(up_left), up, identity], axis=1)])[0]
    odd = jnp.concatenate([jnp.transpose(up), factor[:, size:3 * size], jnp.zeros((size, size), F32)], axis=1)
    even = jnp.concatenate([diag, up, jnp.zeros((size, 2 * size), F32)], axis=1)
    plain_ref[...] = jnp.where(is_even(), even, odd)
    lanes = lax.broadcasted_iota(jnp.int32, factor.shape, 1)
    factor_ref[...] = jnp.where(lanes >= 3 * size, factor, 0.0)
    for copy in copies[2:]:
        copy.wait()


def residual_kernel(known_ref, operator_ref, rows_ref, sent_ref, other_ref, loaded_ref, r_ref, rb_ref, to_pair_ref, halo_ref):
    cases, rows = known_ref.shape
    margin = rows_ref.shape[2]
    even = is_even()
    from_other = jnp.where(even, operator_ref[:, rows:rows + margin], operator_ref[:, rows + margin:])
    r = known_ref[...] - mm_nt(other_ref[:cases, :], from_other)
    r_ref[...] = r
    rounded = r.astype(BF16)
    rb_ref[...] = rounded
    place = place_matrix(jnp.where(even, rows_ref[0, 1:2, :], rows_ref[0, 0:1, :]), rows)
    to_pair_ref[...] = mm(rounded, place).astype(BF16)
    offered = other_ref[cases:2 * cases, :].astype(F32) + other_ref[2 * cases:3 * cases, :].astype(F32)
    halo_ref[...] = (offered - mm_nt(sent_ref[...], other_ref[3 * cases:, :])).astype(BF16)


def own_local_kernel(rb_ref, inverse_ref, basis_ref, halo_ref, local_ref, coarse_ref):
    even = is_even()
    me = position()
    exists = (me > 0) & (me < lax.axis_size("grp") * lax.axis_size("sub") - 1)
    halo = jnp.where(exists, halo_ref[...], jnp.zeros_like(halo_ref))
    zero = jnp.zeros_like(halo)
    extended = jnp.concatenate([jnp.where(even, halo, zero), rb_ref[...], jnp.where(even, zero, halo)], axis=1)
    local_ref[...] = mm(extended, inverse_ref[0])
    coarse_ref[...] = mm_nt(basis_ref[0], extended)


def local_kernel(own_local_ref, own_coarse_ref, inverse_ref, basis_ref, factor_ref, plain_ref, pair_ref,
                 local_ref, message_ref):
    margin = pair_ref.shape[1]
    even = is_even()
    pair = pair_ref[...]
    total = inverse_ref.shape[1]
    ends = jnp.where(even, basis_ref[0, :, total - margin:], basis_ref[0, :, :margin])
    coarse_in = own_coarse_ref[...] + mm_nt(ends, pair)
    size = coarse_in.shape[0]
    stacked = jnp.concatenate([jnp.zeros((3 * size, coarse_in.shape[1]), F32), coarse_in], axis=0)
    reduced = jnp.dot(factor_ref[...], stacked, precision=lax.Precision.HIGHEST, preferred_element_type=F32)
    right_side = jnp.where(even, coarse_in, reduced)
    message = jnp.concatenate([plain_ref[:, :3 * size], right_side], axis=1)
    message_ref[...] = message
    rows = jnp.where(even, inverse_ref[0, total - margin:, :], inverse_ref[0, :margin, :])
    local_ref[...] = own_local_ref[...] + mm(pair, rows)


def reduce_rows(blocks):
    size, width = blocks[0].shape
    panel = 16 if len(blocks) == 1 else 8 if len(blocks) == 2 else 4
    lanes, tile = 128, 8
    here = lax.broadcasted_iota(jnp.int32, (tile, 1), 0)
    tiles = range(size // tile)
    blocks = [[block[t * tile:(t + 1) * tile, :] for t in tiles] for block in blocks]

    def wide(value):
        return jnp.concatenate([value] * (width // lanes), axis=1)

    for first in range(0, size, panel):
        panels = [
            [[jnp.broadcast_to(rows[:, q:q + 1], (tile, lanes)) for rows in block] for q in range(first, first + panel)]
            for block in blocks
        ]
        for a in range(panel):
            at, inside = divmod(first + a, tile)
            for block, columns in zip(blocks, panels):
                column = columns[a]
                inverse = 1.0 / column[at][inside:inside + 1, :]
                for b in range(a + 1, panel):
                    entry = columns[b][at][inside:inside + 1, :] * inverse
                    columns[b] = [
                        jnp.where(here == inside, entry, columns[b][t] - column[t] * entry)
                        if t == at else columns[b][t] - column[t] * entry
                        for t in tiles
                    ]
                row = block[at][inside:inside + 1, :] * wide(inverse)
                for t in tiles:
                    rest = block[t] - wide(column[t]) * row
                    block[t] = jnp.where(here == inside, row, rest) if t == at else rest
    return [jnp.concatenate(block, axis=0) for block in blocks]


def shares(top, bottom, size):
    lanes = 4 * size
    lane = lax.broadcasted_iota(jnp.int32, (size, lanes), 1)

    def placed(product, slot, empty):
        first = product[:, :lanes]
        diag = pltpu.roll(first, lanes - slot * size, axis=1)
        first = jnp.where(lane < size, diag, jnp.where((lane >= empty * size) & (lane < (empty + 1) * size), 0.0, first))
        return jnp.concatenate([first, product[:, lanes:]], axis=1)

    return placed(top, 1, 1), placed(bottom, 2, 2)


def schur(block, solved, size):
    couplings = jnp.transpose(block[:, :4 * size])[size:3 * size]
    product = -jnp.dot(couplings, solved, precision=lax.Precision.HIGHEST, preferred_element_type=F32)
    return shares(product[:size], product[size:], size)


def first_schur(previous, block, size):
    highest = lax.Precision.HIGHEST
    zero = jnp.zeros_like(block)
    above = jnp.concatenate([zero, block, zero, zero], axis=0)
    below = jnp.concatenate([block, zero, zero, zero], axis=0)
    top = -jnp.dot(previous[:, :4 * size], above, precision=highest, preferred_element_type=F32)
    bottom = -jnp.dot(block[:, :4 * size], below, precision=highest, preferred_element_type=F32)
    return shares(top, bottom, size)


def own_part(block, size):
    lane = lax.broadcasted_iota(jnp.int32, block.shape, 1)
    return jnp.where((lane >= size) & (lane < 3 * size), 0.0, block)


def combine(chain, parts, step, size):
    for i in range(0, len(chain), 2 * step):
        total = own_part(chain[i], size)
        if i + step in parts:
            total = total + parts[i + step][0]
        if i - step in parts:
            total = total + parts[i - step][1]
        chain[i] = total


def eliminate(chain, size, keep, step=1):
    count = len(chain) - 1
    while step < count:
        inner = list(range(step, count, 2 * step))
        solved = dict(zip(inner, reduce_rows([chain[j] for j in inner])))
        parts = {j: schur(chain[j], solved[j], size) for j in inner}
        for j in inner:
            keep(j, solved[j])
        combine(chain, parts, step, size)
        step = 2 * step
    return chain[0], chain[count]


def back(solved, left, right, size):
    zero = jnp.zeros_like(left)
    stacked = jnp.concatenate([zero, left, right, zero], axis=0)
    return solved - jnp.dot(
        solved[:, :4 * size], stacked, precision=lax.Precision.HIGHEST, preferred_element_type=F32)


def padded(count):
    total = 1
    while total < count:
        total = 2 * total
    return total


def group_kernel(*refs):
    *received, solved_ref, message_ref, blocks_ref = refs
    half = len(received) // 2
    size, width = received[0].shape
    members = 2 * half
    member = lax.axis_index("sub")
    for d in range(half):
        blocks_ref[member ^ (2 * d)] = received[d][...]
        blocks_ref[member ^ (2 * d + 1)] = received[half + d][...]
    chain = [blocks_ref[j] for j in range(members)]
    chain.append(jnp.zeros((size, width), F32))

    def keep(j, solved):
        solved_ref[j] = solved

    parts = {}
    for j in range(1, members, 2):
        keep(j, chain[j])
        parts[j] = first_schur(chain[j - 1], chain[j], size)
    combine(chain, parts, 1, size)
    head, tail = eliminate(chain, size, keep, 2)
    message_ref[:size, :] = head
    message_ref[size:, :] = tail


def solve_kernel(*refs):
    *received, solved_ref, local_ref, basis_ref, rows_ref, corr_ref, to_other_ref, messages_ref, sep_ref, x_ref = refs
    groups = len(received)
    two_size, width = received[0].shape
    size = two_size // 2
    members = solved_ref.shape[0]
    for d in range(groups):
        messages_ref[lax.axis_index("grp") ^ d] = received[d][...]
    chain = []
    for g in range(groups):
        total = messages_ref[g, :size, :]
        if g:
            total = total + messages_ref[g - 1, size:, :]
        chain.append(total)
    count = padded(groups)
    row = lax.broadcasted_iota(jnp.int32, (size, width), 0)
    lane = lax.broadcasted_iota(jnp.int32, (size, width), 1)
    while len(chain) < count:
        chain.append((row == lane).astype(F32))
    chain.append(jnp.zeros((size, width), F32))
    factors = {}
    head, _ = eliminate(chain, size, factors.__setitem__)
    solution = {count: jnp.zeros((size, width), F32)}
    solution[0] = reduce_rows([head])[0]
    step = count // 2
    while step >= 1:
        for j in range(step, count, 2 * step):
            solution[j] = back(factors[j], solution[j - step], solution[j + step], size)
        step = step // 2
    for g in range(groups):
        sep_ref[g] = solution[g]
    sep_ref[groups] = jnp.zeros((size, width), F32)
    group, member = lax.axis_index("grp"), lax.axis_index("sub")
    x_ref[0] = sep_ref[group]
    x_ref[members] = sep_ref[group + 1]
    step = members // 2
    while step >= 2:
        for j in range(step, members, 2 * step):
            x_ref[j] = back(solved_ref[j], x_ref[j - step], x_ref[j + step], size)
        step = step // 2
    odd = member // 2 * 2 + 1
    x_ref[odd] = back(solved_ref[odd], x_ref[odd - 1], x_ref[odd + 1], size)
    coarse = x_ref[member].astype(BF16)
    correction = local_ref[...] + mm_t(coarse, basis_ref[0])[3 * size:]
    corr_ref[...] = correction
    even = is_even()
    to_other_ref[...] = return_rows(
        correction, rows_ref.shape[2], jnp.where(even, rows_ref[0, 0:1, :], rows_ref[0, 1:2, :]), even)


def return_rows(correction, margin, rows, head):
    owned = correction.shape[1] - 2 * margin
    rounded = correction.astype(BF16)
    tail = jnp.where(head, rounded[:, :margin], rounded[:, margin + owned:])
    return jnp.concatenate([tail, mm(rounded[:, margin:margin + owned], place_matrix(rows, owned)).astype(BF16)], axis=1)


def pair_kernel(corr_ref, rows_ref, to_pair_ref):
    even = is_even()
    to_pair_ref[...] = return_rows(
        corr_ref[...], rows_ref.shape[2], jnp.where(even, rows_ref[0, 1:2, :], rows_ref[0, 0:1, :]), jnp.logical_not(even))


def row_sum(values):
    lanes = 128
    total = values[:, :lanes]
    for start in range(lanes, values.shape[1], lanes):
        total = total + values[:, start:start + lanes]
    return mm_nt(jnp.ones((8, lanes), F32), total, precision=lax.Precision.HIGHEST)


def image_kernel(corr_ref, r_ref, diag_ref, operator_ref, rows_ref, pair_ref, other_ref, p_ref, image_ref, sums_ref):
    margin = rows_ref.shape[2]
    owned = p_ref.shape[1]
    from_left, from_right = from_sides(pair_ref, other_ref)
    place = place_matrix(jnp.concatenate([rows_ref[0, 0:1, :], rows_ref[0, 1:2, :]], axis=1), owned)
    tails = jnp.concatenate([from_left[:, :margin], from_right[:, :margin]], axis=1)
    p = corr_ref[:, margin:margin + owned] + mm_nt(tails, place)
    p_ref[...] = p
    me = position()
    last = lax.axis_size("grp") * lax.axis_size("sub") - 1
    left = from_left[:, margin:].astype(F32) + corr_ref[:, :margin]
    right = from_right[:, margin:].astype(F32) + corr_ref[:, margin + owned:]
    left = jnp.where(me == 0, 0.0, left).astype(BF16)
    right = jnp.where(me == last, 0.0, right).astype(BF16)
    values = jnp.concatenate([p.astype(BF16), left, right], axis=1)
    image = diag_ref[...].reshape(1, owned) * p + mm_nt(values, operator_ref[...])
    image_ref[...] = image
    inner = row_sum(r_ref[...] * p)
    curvature = row_sum(p * image)
    sums = jnp.concatenate([inner[0:1], curvature[0:1]], axis=0)
    for slot in range(sums_ref.shape[0]):
        sums_ref[slot] = sums


def finish_kernel(x_ref, p_ref, r_ref, image_ref, sums_ref, out_x_ref, out_r_ref):
    sums = jnp.sum(sums_ref[...], axis=0)
    row = sums[0:1, :] / sums[1:2, :]
    lanes = 128
    step = jnp.transpose(jnp.broadcast_to(row, (lanes, row.shape[1])))
    for start in range(0, x_ref.shape[1], lanes):
        span = slice(start, start + lanes)
        out_x_ref[:, span] = x_ref[:, span] + step * p_ref[:, span]
        out_r_ref[:, span] = r_ref[:, span] - step * image_ref[:, span]


def call(kernel, out, in_specs, scratch=()):
    return pl.pallas_call(
        kernel,
        out_shape=out,
        in_specs=in_specs,
        out_specs=[VMEM] * len(out),
        scratch_shapes=list(scratch),
        compiler_params=pltpu.CompilerParams(vmem_limit_bytes=16 * 2**20),
    )


def far(*arrays):
    return [pltpu.with_memory_space_constraint(array, pltpu.HBM) for array in arrays]


def struct(shape, dtype):
    return jax.ShapeDtypeStruct(shape, dtype)


def shards(right_side, iterate_in, diagonal, block_values, block_cols, couple_left, couple_right, send_rows,
           local_inverse, coarse_basis, coarse_diag, coarse_up):
    groups, members = lax.axis_size("grp"), lax.axis_size("sub")
    total = groups * members
    rows, cases = right_side.shape
    margin = send_rows.shape[2]
    extended = local_inverse.shape[1]
    modes = coarse_basis.shape[2]
    width = 3 * modes + cases
    pairs = [(i, i ^ 1) for i in range(total)]
    others = [(i, i + 1 if i % 2 else i - 1) for i in range(1, total - 1)]
    right_side, iterate_in = right_side.T, iterate_in.T
    basis = jnp.swapaxes(coarse_basis, 1, 2)
    block_cols = jnp.transpose(block_cols, (2, 0, 1))

    halo = struct((cases, margin), BF16)
    full = struct((cases, rows), F32)
    semaphores = pltpu.SemaphoreType.DMA
    to_pair, to_other, start, send_rows, loads, diag, operator = call(
        load_kernel,
        [
            struct((cases + modes, margin), BF16),
            halo,
            full,
            struct(send_rows.shape, send_rows.dtype),
            full,
            struct(diagonal.shape, F32),
            struct((rows, rows + 2 * margin), BF16),
        ],
        [HBM] * 9,
        [
            pltpu.VMEM(coarse_up.shape, F32),
            pltpu.SMEM(block_cols.shape, block_cols.dtype),
            pltpu.VMEM(block_values.shape, BF16),
            semaphores((9,)),
        ],
    )(*far(
        iterate_in, send_rows, coarse_up, right_side, diagonal, block_values, block_cols, couple_left, couple_right
    ))
    first_pair = lax.ppermute(to_pair, AXES, pairs)
    (partial,) = call(own_kernel, [full], [VMEM] * 4)(start, loads, diag, operator)
    known, message = call(offer_kernel, [full, struct((3 * cases + margin, margin), BF16)], [VMEM] * 5)(
        partial, operator, send_rows, first_pair, to_other
    )
    first_other = lax.ppermute(message, AXES, others)
    inverse, basis, factor, plain = call(
        inverse_kernel,
        [
            struct(local_inverse.shape, BF16),
            struct(basis.shape, BF16),
            struct((modes, 4 * modes), F32),
            struct((modes, 4 * modes), F32),
        ],
        [VMEM] + [HBM] * 4,
        [pltpu.VMEM((2, modes, modes), F32), semaphores((4,))],
    )(first_pair, *far(local_inverse, basis, coarse_diag, coarse_up))
    residual, rounded, to_pair, other_halo = call(
        residual_kernel, [full, struct((cases, rows), BF16), halo, halo], [VMEM] * 6
    )(known, operator, send_rows, to_other, first_other, plain)
    pair_halo = lax.ppermute(to_pair, AXES, pairs)
    local, coarse = call(own_local_kernel, [struct((cases, extended), F32), struct((modes, cases), F32)], [VMEM] * 4)(
        rounded, inverse, basis, other_halo
    )
    chips = members // 2
    local, message = call(
        local_kernel, [struct((cases, extended), F32), struct((modes, width), F32)], [VMEM] * 7
    )(local, coarse, inverse, basis, factor, plain, pair_halo)

    def partners(value, stride, count):
        swaps = [[(i, i ^ (stride * d)) for i in range(total)] for d in range(1, count)]
        return [value] + [lax.ppermute(value, AXES, swap) for swap in swaps]

    same = partners(message, 2, chips)
    opposite = [lax.ppermute(value, AXES, pairs) for value in same]
    block = pltpu.VMEM((members, modes, width), F32)
    solved, reduced = call(
        group_kernel,
        [struct((members, modes, width), F32), struct((2 * modes, width), F32)],
        [VMEM] * members,
        [block],
    )(*same, *opposite)
    reduced = partners(reduced, members, groups)
    returned = struct((cases, 2 * margin), BF16)
    correction, to_other = call(
        solve_kernel,
        [struct((cases, extended), F32), returned],
        [VMEM] * (groups + 4),
        [
            pltpu.VMEM((groups, 2 * modes, width), F32),
            pltpu.VMEM((groups + 1, modes, width), F32),
            pltpu.VMEM((members + 1, modes, width), F32),
        ],
    )(*reduced, solved, local, basis, send_rows)
    from_other = lax.ppermute(to_other, AXES, others)
    (to_pair,) = call(pair_kernel, [returned], [VMEM] * 2)(correction, send_rows)
    from_pair = lax.ppermute(to_pair, AXES, pairs)
    direction, image, sums = call(image_kernel, [full, full, struct((total, 2, cases), F32)], [VMEM] * 7)(
        correction, residual, diag, operator, send_rows, from_pair, from_other
    )
    sums = lax.all_to_all(sums, AXES, 0, 0, tiled=True)
    iterate, residual = call(finish_kernel, [full, full], [VMEM] * 5)(start, direction, residual, image, sums)
    return iterate.T, residual.T


def solution(mesh):
    def spec(rank):
        return P(AXES, *([None] * (rank - 1)))

    return jax.shard_map(
        shards,
        mesh=mesh,
        in_specs=tuple(spec(rank) for rank in (2, 2, 1, 5, 3, 2, 2, 3, 3, 3, 3, 3)),
        out_specs=(spec(2), spec(2)),
        check_vma=False,
    )
```

```python
import jax
import jax.numpy as jnp
from jax import lax
from jax.experimental import pallas as pl
from jax.experimental.pallas import tpu as pltpu
from jax.sharding import PartitionSpec as P


AXES = ("grp", "sub")
BF16 = jnp.bfloat16
F32 = jnp.float32
VMEM = pl.BlockSpec(memory_space=pltpu.VMEM)
HBM = pl.BlockSpec(memory_space=pltpu.HBM)


def mm(a, b):
    return jnp.dot(a, b, preferred_element_type=F32)


def mm_t(a, b, **kw):
    return lax.dot_general(a, b, (((0,), (0,)), ((), ())), preferred_element_type=F32, **kw)


def mm_nt(a, b, **kw):
    return lax.dot_general(a, b, (((1,), (1,)), ((), ())), preferred_element_type=F32, **kw)


def position():
    return lax.axis_index("grp") * lax.axis_size("sub") + lax.axis_index("sub")


def is_even():
    return position() % 2 == 0


def place_matrix(row, total):
    place = lax.broadcasted_iota(jnp.int32, (total, row.shape[1]), 0)
    return (place == row).astype(F32).astype(BF16)


def send_matrix(rows_ref, total):
    left, right = rows_ref[0, 0:1, :], rows_ref[0, 1:2, :]
    even = is_even()
    rows = jnp.concatenate([jnp.where(even, right, left), jnp.where(even, left, right)], axis=1)
    return place_matrix(rows, total)


def copy_all(copies, sems):
    started = [pltpu.make_async_copy(source, target, sems.at[n]) for n, (source, target) in enumerate(copies)]
    for copy in started:
        copy.start()
    return started


def split_three(value):
    high = value.astype(BF16)
    rest = value - high.astype(F32)
    middle = rest.astype(BF16)
    return high, middle, (rest - middle.astype(F32)).astype(BF16)


def load_kernel(x_hbm, rows_hbm, up_hbm, basis_hbm, b_hbm, diag_hbm, values_hbm, cols_hbm, cl_hbm, cr_hbm,
                to_pair_ref, to_other_ref, basis_other_ref, x_ref, rows_ref, basis_ref, b_ref, diag_ref, operator_ref,
                up_ref, cols_ref, values_ref, sems):
    blocks, nonzeros, size = values_hbm.shape[1], values_hbm.shape[2], values_hbm.shape[3]
    cases, rows = x_ref.shape
    margin = rows_ref.shape[2]
    copies = copy_all(
        [
            (rows_hbm, rows_ref),
            (x_hbm, x_ref),
            (up_hbm, up_ref),
            (basis_hbm, basis_ref),
            (cols_hbm, cols_ref),
            (values_hbm, values_ref),
            (cl_hbm, operator_ref.at[:, rows:rows + margin]),
            (cr_hbm, operator_ref.at[:, rows + margin:]),
            (diag_hbm, diag_ref),
            (b_hbm, b_ref),
        ],
        sems,
    )
    operator_ref[:, :rows] = jnp.zeros((rows, rows), BF16)
    for copy in copies[:4]:
        copy.wait()
    place = send_matrix(rows_ref, rows)
    sent = mm(x_ref[...].astype(BF16), place).astype(BF16)
    to_pair_ref[:cases, :] = sent[:, :margin]
    to_other_ref[...] = sent[:, margin:]
    parts = [part.astype(F32) for part in split_three(up_ref[0])]
    modes = up_ref.shape[1]
    parts.append(jnp.zeros((modes, margin - 3 * modes), F32))
    to_pair_ref[cases:cases + modes, :] = jnp.concatenate(parts, axis=1).astype(BF16)
    basis = basis_ref[0]
    even = is_even()
    head, tail = basis[:, :margin], basis[:, margin + rows:]
    picked = mm(basis[:, margin:margin + rows], place).astype(BF16)
    to_pair_ref[cases + modes:cases + 2 * modes, :] = jnp.where(even, tail, head)
    to_pair_ref[cases + 2 * modes:, :] = picked[:, :margin]
    basis_other_ref[:modes, :] = jnp.where(even, head, tail)
    basis_other_ref[modes:, :] = picked[:, margin:]
    for copy in copies[4:]:
        copy.wait()
    for i in range(blocks):
        for t in range(nonzeros):
            start = pl.multiple_of(cols_ref[t, 0, i] * size, size)
            operator_ref[i * size:(i + 1) * size, pl.ds(start, size)] = values_ref[0, i, t]


def own_kernel(x_ref, b_ref, diag_ref, operator_ref, partial_ref):
    x = x_ref[...]
    rows = x.shape[1]
    diag = diag_ref[...].reshape(1, rows)
    partial_ref[...] = b_ref[...] - diag * x - mm_nt(x.astype(BF16), operator_ref[:, :rows])


def offer_kernel(partial_ref, operator_ref, rows_ref, pair_ref, to_other_ref, basis_other_ref, known_ref, message_ref):
    cases, rows = partial_ref.shape
    margin = rows_ref.shape[2]
    even = is_even()
    left, right = operator_ref[:, rows:rows + margin], operator_ref[:, rows + margin:]
    from_pair = jnp.where(even, right, left)
    from_other = jnp.where(even, left, right)
    known = partial_ref[...] - mm_nt(pair_ref[:cases, :], from_pair)
    known_ref[...] = known
    high = known.astype(BF16)
    low = (known - high.astype(F32)).astype(BF16)
    place = place_matrix(jnp.where(even, rows_ref[0, 0:1, :], rows_ref[0, 1:2, :]), rows)
    message_ref[:cases, :] = to_other_ref[...]
    message_ref[cases:2 * cases, :] = mm(high, place).astype(BF16)
    message_ref[2 * cases:3 * cases, :] = mm(low, place).astype(BF16)
    message_ref[3 * cases:3 * cases + margin, :] = mm_t(place, from_other).astype(BF16)
    message_ref[3 * cases + margin:, :] = basis_other_ref[...]


def inverse_kernel(first_pair_ref, inverse_hbm, diag_hbm, up_hbm,
                   inverse_ref, factor_ref, plain_ref, blocks_ref, sems):
    size = diag_hbm.shape[1]
    cases = first_pair_ref.shape[0] - 3 * size
    copies = copy_all(
        [
            (diag_hbm, blocks_ref.at[0:1]),
            (up_hbm, blocks_ref.at[1:2]),
            (inverse_hbm, inverse_ref),
        ],
        sems,
    )
    parts = first_pair_ref[cases:cases + size, :].astype(F32)
    up_left = parts[:, :size] + (parts[:, size:2 * size] + parts[:, 2 * size:3 * size])
    for copy in copies[:2]:
        copy.wait()
    last = position() == lax.axis_size("grp") * lax.axis_size("sub") - 1
    up = jnp.where(last, 0.0, blocks_ref[1])
    diag = blocks_ref[0]
    row = lax.broadcasted_iota(jnp.int32, (size, size), 0)
    lane = lax.broadcasted_iota(jnp.int32, (size, size), 1)
    identity = (row == lane).astype(F32)
    factor = reduce_rows([jnp.concatenate([diag, jnp.transpose(up_left), up, identity], axis=1)])[0]
    odd = jnp.concatenate([jnp.transpose(up), factor[:, size:3 * size], jnp.zeros((size, size), F32)], axis=1)
    even = jnp.concatenate([diag, up, jnp.zeros((size, 2 * size), F32)], axis=1)
    plain_ref[...] = jnp.where(is_even(), even, odd)
    lanes = lax.broadcasted_iota(jnp.int32, factor.shape, 1)
    factor_ref[...] = jnp.where(lanes >= 3 * size, factor, 0.0)
    for copy in copies[2:]:
        copy.wait()


def residual_kernel(known_ref, operator_ref, rows_ref, sent_ref, other_ref, loaded_ref, r_ref, rb_ref, to_pair_ref, halo_ref):
    cases, rows = known_ref.shape
    margin = rows_ref.shape[2]
    even = is_even()
    from_other = jnp.where(even, operator_ref[:, rows:rows + margin], operator_ref[:, rows + margin:])
    r = known_ref[...] - mm_nt(other_ref[:cases, :], from_other)
    r_ref[...] = r
    rounded = r.astype(BF16)
    rb_ref[...] = rounded
    place = place_matrix(jnp.where(even, rows_ref[0, 1:2, :], rows_ref[0, 0:1, :]), rows)
    to_pair_ref[...] = mm(rounded, place).astype(BF16)
    offered = other_ref[cases:2 * cases, :].astype(F32) + other_ref[2 * cases:3 * cases, :].astype(F32)
    halo_ref[...] = (offered - mm_nt(sent_ref[...], other_ref[3 * cases:3 * cases + margin, :])).astype(BF16)


def own_local_kernel(rb_ref, inverse_ref, basis_ref, halo_ref, local_ref, coarse_ref):
    even = is_even()
    me = position()
    exists = (me > 0) & (me < lax.axis_size("grp") * lax.axis_size("sub") - 1)
    halo = jnp.where(exists, halo_ref[...], jnp.zeros_like(halo_ref))
    zero = jnp.zeros_like(halo)
    extended = jnp.concatenate([jnp.where(even, halo, zero), rb_ref[...], jnp.where(even, zero, halo)], axis=1)
    local_ref[...] = mm(extended, inverse_ref[0])
    coarse_ref[...] = mm_nt(basis_ref[0], extended)


def local_kernel(own_local_ref, own_coarse_ref, inverse_ref, basis_ref, factor_ref, plain_ref, pair_ref, rows_ref,
                 local_ref, message_ref, to_pair_ref, to_other_ref):
    margin = pair_ref.shape[1]
    even = is_even()
    pair = pair_ref[...]
    total = inverse_ref.shape[1]
    ends = jnp.where(even, basis_ref[0, :, total - margin:], basis_ref[0, :, :margin])
    coarse_in = own_coarse_ref[...] + mm_nt(ends, pair)
    size = coarse_in.shape[0]
    stacked = jnp.concatenate([jnp.zeros((3 * size, coarse_in.shape[1]), F32), coarse_in], axis=0)
    reduced = jnp.dot(factor_ref[...], stacked, precision=lax.Precision.HIGHEST, preferred_element_type=F32)
    right_side = jnp.where(even, coarse_in, reduced)
    message = jnp.concatenate([plain_ref[:, :3 * size], right_side], axis=1)
    message_ref[...] = message
    rows = jnp.where(even, inverse_ref[0, total - margin:, :], inverse_ref[0, :margin, :])
    local = own_local_ref[...] + mm(pair, rows)
    local_ref[...] = local
    left, right = rows_ref[0, 0:1, :], rows_ref[0, 1:2, :]
    to_pair_ref[...] = return_rows(local, margin, jnp.where(even, right, left), jnp.logical_not(even))
    to_other_ref[...] = return_rows(local, margin, jnp.where(even, left, right), even)


def return_rows(local, margin, rows, head):
    owned = local.shape[1] - 2 * margin
    rounded = local.astype(BF16)
    tail = jnp.where(head, rounded[:, :margin], rounded[:, margin + owned:])
    return jnp.concatenate([tail, mm(rounded[:, margin:margin + owned], place_matrix(rows, owned)).astype(BF16)], axis=1)


def reduce_rows(blocks):
    size, width = blocks[0].shape
    panel = 16 if len(blocks) == 1 else 8 if len(blocks) == 2 else 4
    lanes, tile = 128, 8
    here = lax.broadcasted_iota(jnp.int32, (tile, 1), 0)
    tiles = range(size // tile)
    blocks = [[block[t * tile:(t + 1) * tile, :] for t in tiles] for block in blocks]

    def wide(value):
        return jnp.concatenate([value] * (width // lanes), axis=1)

    for first in range(0, size, panel):
        panels = [
            [[jnp.broadcast_to(rows[:, q:q + 1], (tile, lanes)) for rows in block] for q in range(first, first + panel)]
            for block in blocks
        ]
        for a in range(panel):
            at, inside = divmod(first + a, tile)
            for block, columns in zip(blocks, panels):
                column = columns[a]
                inverse = 1.0 / column[at][inside:inside + 1, :]
                for b in range(a + 1, panel):
                    entry = columns[b][at][inside:inside + 1, :] * inverse
                    columns[b] = [
                        jnp.where(here == inside, entry, columns[b][t] - column[t] * entry)
                        if t == at else columns[b][t] - column[t] * entry
                        for t in tiles
                    ]
                row = block[at][inside:inside + 1, :] * wide(inverse)
                for t in tiles:
                    rest = block[t] - wide(column[t]) * row
                    block[t] = jnp.where(here == inside, row, rest) if t == at else rest
    return [jnp.concatenate(block, axis=0) for block in blocks]


def shares(top, bottom, size):
    lanes = 4 * size
    lane = lax.broadcasted_iota(jnp.int32, (size, lanes), 1)

    def placed(product, slot, empty):
        first = product[:, :lanes]
        diag = pltpu.roll(first, lanes - slot * size, axis=1)
        first = jnp.where(lane < size, diag, jnp.where((lane >= empty * size) & (lane < (empty + 1) * size), 0.0, first))
        return jnp.concatenate([first, product[:, lanes:]], axis=1)

    return placed(top, 1, 1), placed(bottom, 2, 2)


def schur(block, solved, size):
    couplings = jnp.transpose(block[:, :4 * size])[size:3 * size]
    product = -jnp.dot(couplings, solved, precision=lax.Precision.HIGHEST, preferred_element_type=F32)
    return shares(product[:size], product[size:], size)


def first_schur(previous, block, size):
    highest = lax.Precision.HIGHEST
    zero = jnp.zeros_like(block)
    above = jnp.concatenate([zero, block, zero, zero], axis=0)
    below = jnp.concatenate([block, zero, zero, zero], axis=0)
    top = -jnp.dot(previous[:, :4 * size], above, precision=highest, preferred_element_type=F32)
    bottom = -jnp.dot(block[:, :4 * size], below, precision=highest, preferred_element_type=F32)
    return shares(top, bottom, size)


def own_part(block, size):
    lane = lax.broadcasted_iota(jnp.int32, block.shape, 1)
    return jnp.where((lane >= size) & (lane < 3 * size), 0.0, block)


def combine(chain, parts, step, size):
    for i in range(0, len(chain), 2 * step):
        total = own_part(chain[i], size)
        if i + step in parts:
            total = total + parts[i + step][0]
        if i - step in parts:
            total = total + parts[i - step][1]
        chain[i] = total


def eliminate(chain, size, keep, step=1):
    count = len(chain) - 1
    while step < count:
        inner = list(range(step, count, 2 * step))
        solved = dict(zip(inner, reduce_rows([chain[j] for j in inner])))
        parts = {j: schur(chain[j], solved[j], size) for j in inner}
        for j in inner:
            keep(j, solved[j])
        combine(chain, parts, step, size)
        step = 2 * step
    return chain[0], chain[count]


def back(solved, left, right, size):
    zero = jnp.zeros_like(left)
    stacked = jnp.concatenate([zero, left, right, zero], axis=0)
    return solved - jnp.dot(
        solved[:, :4 * size], stacked, precision=lax.Precision.HIGHEST, preferred_element_type=F32)


def padded(count):
    total = 1
    while total < count:
        total = 2 * total
    return total


def group_kernel(*refs):
    *received, solved_ref, message_ref, blocks_ref = refs
    half = len(received) // 2
    size, width = received[0].shape
    members = 2 * half
    member = lax.axis_index("sub")
    for d in range(half):
        blocks_ref[member ^ (2 * d)] = received[d][...]
        blocks_ref[member ^ (2 * d + 1)] = received[half + d][...]
    chain = [blocks_ref[j] for j in range(members)]
    chain.append(jnp.zeros((size, width), F32))

    def keep(j, solved):
        solved_ref[j] = solved

    parts = {}
    for j in range(1, members, 2):
        keep(j, chain[j])
        parts[j] = first_schur(chain[j - 1], chain[j], size)
    combine(chain, parts, 1, size)
    head, tail = eliminate(chain, size, keep, 2)
    message_ref[:size, :] = head
    message_ref[size:2 * size, :] = tail
    lane = lax.broadcasted_iota(jnp.int32, (size, width), 1)
    step = members // 2
    at = step
    whole = solved_ref[at]
    zero = jnp.zeros((size, width), F32)
    while at < members - 1:
        step = step // 2
        at = at + step
        block = solved_ref[at]
        stacked = jnp.concatenate([zero, whole, zero, zero], axis=0)
        through = jnp.dot(
            block[:, :4 * size], stacked, precision=lax.Precision.HIGHEST, preferred_element_type=F32)
        whole = jnp.where((lane >= size) & (lane < 2 * size), 0.0, block) - through
    message_ref[2 * size:, :] = whole


def solve_kernel(*refs):
    (*received, solved_ref, local_ref, basis_ref, rows_ref, first_pair_ref, first_other_ref, pair_ref, other_ref,
     r_ref, diag_ref, operator_ref, p_ref, image_ref, sums_ref, messages_ref, sep_ref, x_ref) = refs
    groups = len(received)
    size, width = received[0].shape
    size = size // 3
    members = solved_ref.shape[0]
    for d in range(groups):
        messages_ref[lax.axis_index("grp") ^ d] = received[d][...]
    chain = []
    for g in range(groups):
        total = messages_ref[g, :size, :]
        if g:
            total = total + messages_ref[g - 1, size:2 * size, :]
        chain.append(total)
    count = padded(groups)
    row = lax.broadcasted_iota(jnp.int32, (size, width), 0)
    lane = lax.broadcasted_iota(jnp.int32, (size, width), 1)
    while len(chain) < count:
        chain.append((row == lane).astype(F32))
    chain.append(jnp.zeros((size, width), F32))
    factors = {}
    head, _ = eliminate(chain, size, factors.__setitem__)
    solution = {count: jnp.zeros((size, width), F32)}
    solution[0] = reduce_rows([head])[0]
    step = count // 2
    while step >= 1:
        for j in range(step, count, 2 * step):
            solution[j] = back(factors[j], solution[j - step], solution[j + step], size)
        step = step // 2
    for g in range(groups):
        sep_ref[g] = solution[g]
    sep_ref[groups] = jnp.zeros((size, width), F32)
    group, member = lax.axis_index("grp"), lax.axis_index("sub")
    x_ref[0] = sep_ref[group]
    x_ref[members] = sep_ref[group + 1]
    step = members // 2
    while step >= 2:
        for j in range(step, members, 2 * step):
            x_ref[j] = back(solved_ref[j], x_ref[j - step], x_ref[j + step], size)
        step = step // 2
    before = jnp.maximum(group - 1, 0)
    earlier = back(messages_ref[before, 2 * size:, :], sep_ref[before], sep_ref[group], size)
    lower = jnp.maximum(member - 1, 0)
    for odd in (member // 2 * 2 + 1, lower // 2 * 2 + 1):
        x_ref[odd] = back(solved_ref[odd], x_ref[odd - 1], x_ref[odd + 1], size)
    left_solution = jnp.where(member == 0, earlier, x_ref[lower])
    right_solution = x_ref[member + 1]

    def lifted(solution, basis):
        return mm_t(solution.astype(BF16), basis)[3 * size:]

    cases = pair_ref.shape[0]
    margin = rows_ref.shape[2]
    owned = p_ref.shape[1]
    even = is_even()

    def columns(ref, start):
        return jnp.concatenate([ref[start:start + size, :], ref[start + size:start + 2 * size, :]], axis=1)

    pair_basis = columns(first_pair_ref, cases + size)
    other_basis = columns(first_other_ref, 3 * cases + margin)
    pair, other = pair_ref[...].astype(F32), other_ref[...].astype(F32)
    left = jnp.where(even, other, pair) + lifted(left_solution, jnp.where(even, other_basis, pair_basis))
    right = jnp.where(even, pair, other) + lifted(right_solution, jnp.where(even, pair_basis, other_basis))
    correction = local_ref[...] + lifted(x_ref[member], basis_ref[0])
    place = place_matrix(jnp.concatenate([rows_ref[0, 0:1, :], rows_ref[0, 1:2, :]], axis=1), owned)
    tails = jnp.concatenate([left[:, :margin], right[:, :margin]], axis=1).astype(BF16)
    p = correction[:, margin:margin + owned] + mm_nt(tails, place)
    p_ref[...] = p
    me = position()
    last = lax.axis_size("grp") * lax.axis_size("sub") - 1
    left = jnp.where(me == 0, 0.0, left[:, margin:] + correction[:, :margin]).astype(BF16)
    right = jnp.where(me == last, 0.0, right[:, margin:] + correction[:, margin + owned:]).astype(BF16)
    values = jnp.concatenate([p.astype(BF16), left, right], axis=1)
    image = diag_ref[...].reshape(1, owned) * p + mm_nt(values, operator_ref[...])
    image_ref[...] = image
    inner = row_sum(r_ref[...] * p)
    curvature = row_sum(p * image)
    sums = jnp.concatenate([inner[0:1], curvature[0:1]], axis=0)
    for slot in range(sums_ref.shape[0]):
        sums_ref[slot] = sums


def row_sum(values):
    lanes = 128
    total = values[:, :lanes]
    for start in range(lanes, values.shape[1], lanes):
        total = total + values[:, start:start + lanes]
    return mm_nt(jnp.ones((8, lanes), F32), total, precision=lax.Precision.HIGHEST)


def finish_kernel(x_ref, p_ref, r_ref, image_ref, sums_ref, out_x_ref, out_r_ref):
    sums = jnp.sum(sums_ref[...], axis=0)
    row = sums[0:1, :] / sums[1:2, :]
    lanes = 128
    step = jnp.transpose(jnp.broadcast_to(row, (lanes, row.shape[1])))
    for start in range(0, x_ref.shape[1], lanes):
        span = slice(start, start + lanes)
        out_x_ref[:, span] = x_ref[:, span] + step * p_ref[:, span]
        out_r_ref[:, span] = r_ref[:, span] - step * image_ref[:, span]


def call(kernel, out, in_specs, scratch=()):
    return pl.pallas_call(
        kernel,
        out_shape=out,
        in_specs=in_specs,
        out_specs=[VMEM] * len(out),
        scratch_shapes=list(scratch),
        compiler_params=pltpu.CompilerParams(vmem_limit_bytes=16 * 2**20),
    )


def far(*arrays):
    return [pltpu.with_memory_space_constraint(array, pltpu.HBM) for array in arrays]


def struct(shape, dtype):
    return jax.ShapeDtypeStruct(shape, dtype)


def shards(right_side, iterate_in, diagonal, block_values, block_cols, couple_left, couple_right, send_rows,
           local_inverse, coarse_basis, coarse_diag, coarse_up):
    groups, members = lax.axis_size("grp"), lax.axis_size("sub")
    total = groups * members
    rows, cases = right_side.shape
    margin = send_rows.shape[2]
    extended = local_inverse.shape[1]
    modes = coarse_basis.shape[2]
    width = 3 * modes + cases
    pairs = [(i, i ^ 1) for i in range(total)]
    others = [(i, i + 1 if i % 2 else i - 1) for i in range(1, total - 1)]
    right_side, iterate_in = right_side.T, iterate_in.T
    basis = jnp.swapaxes(coarse_basis, 1, 2)
    block_cols = jnp.transpose(block_cols, (2, 0, 1))

    halo = struct((cases, margin), BF16)
    full = struct((cases, rows), F32)
    semaphores = pltpu.SemaphoreType.DMA
    to_pair, to_other, basis_other, start, send_rows, basis, loads, diag, operator = call(
        load_kernel,
        [
            struct((cases + 3 * modes, margin), BF16),
            halo,
            struct((2 * modes, margin), BF16),
            full,
            struct(send_rows.shape, send_rows.dtype),
            struct(basis.shape, BF16),
            full,
            struct(diagonal.shape, F32),
            struct((rows, rows + 2 * margin), BF16),
        ],
        [HBM] * 10,
        [
            pltpu.VMEM(coarse_up.shape, F32),
            pltpu.SMEM(block_cols.shape, block_cols.dtype),
            pltpu.VMEM(block_values.shape, BF16),
            semaphores((10,)),
        ],
    )(*far(
        iterate_in, send_rows, coarse_up, basis, right_side, diagonal, block_values, block_cols, couple_left, couple_right
    ))
    first_pair = lax.ppermute(to_pair, AXES, pairs)
    (partial,) = call(own_kernel, [full], [VMEM] * 4)(start, loads, diag, operator)
    known, message = call(
        offer_kernel, [full, struct((3 * cases + margin + 2 * modes, margin), BF16)], [VMEM] * 6
    )(partial, operator, send_rows, first_pair, to_other, basis_other)
    first_other = lax.ppermute(message, AXES, others)
    inverse, factor, plain = call(
        inverse_kernel,
        [struct(local_inverse.shape, BF16), struct((modes, 4 * modes), F32), struct((modes, 4 * modes), F32)],
        [VMEM] + [HBM] * 3,
        [pltpu.VMEM((2, modes, modes), F32), semaphores((3,))],
    )(first_pair, *far(local_inverse, coarse_diag, coarse_up))
    residual, rounded, to_pair, other_halo = call(
        residual_kernel, [full, struct((cases, rows), BF16), halo, halo], [VMEM] * 6
    )(known, operator, send_rows, to_other, first_other, plain)
    pair_halo = lax.ppermute(to_pair, AXES, pairs)
    local, coarse = call(own_local_kernel, [struct((cases, extended), F32), struct((modes, cases), F32)], [VMEM] * 4)(
        rounded, inverse, basis, other_halo
    )
    chips = members // 2
    returned = struct((cases, 2 * margin), BF16)
    local, message, to_pair, to_other = call(
        local_kernel, [struct((cases, extended), F32), struct((modes, width), F32), returned, returned], [VMEM] * 8
    )(local, coarse, inverse, basis, factor, plain, pair_halo, send_rows)
    from_other = lax.ppermute(to_other, AXES, others)
    from_pair = lax.ppermute(to_pair, AXES, pairs)

    def partners(value, stride, count):
        swaps = [[(i, i ^ (stride * d)) for i in range(total)] for d in range(1, count)]
        return [value] + [lax.ppermute(value, AXES, swap) for swap in swaps]

    same = partners(message, 2, chips)
    opposite = [lax.ppermute(value, AXES, pairs) for value in same]
    block = pltpu.VMEM((members, modes, width), F32)
    solved, reduced = call(
        group_kernel,
        [struct((members, modes, width), F32), struct((3 * modes, width), F32)],
        [VMEM] * members,
        [block],
    )(*same, *opposite)
    reduced = partners(reduced, members, groups)
    direction, image, sums = call(
        solve_kernel,
        [full, full, struct((total, 2, cases), F32)],
        [VMEM] * (groups + 11),
        [
            pltpu.VMEM((groups, 3 * modes, width), F32),
            pltpu.VMEM((groups + 1, modes, width), F32),
            pltpu.VMEM((members + 1, modes, width), F32),
        ],
    )(
        *reduced, solved, local, basis, send_rows, first_pair, first_other, from_pair, from_other,
        residual, diag, operator
    )
    sums = lax.all_to_all(sums, AXES, 0, 0, tiled=True)
    iterate, residual = call(finish_kernel, [full, full], [VMEM] * 5)(start, direction, residual, image, sums)
    return iterate.T, residual.T


def solution(mesh):
    def spec(rank):
        return P(AXES, *([None] * (rank - 1)))

    return jax.shard_map(
        shards,
        mesh=mesh,
        in_specs=tuple(spec(rank) for rank in (2, 2, 1, 5, 3, 2, 2, 3, 3, 3, 3, 3)),
        out_specs=(spec(2), spec(2)),
        check_vma=False,
    )
```

```python
import jax
import jax.numpy as jnp
from jax import lax
from jax.experimental import pallas as pl
from jax.experimental.pallas import tpu as pltpu
from jax.sharding import PartitionSpec as P


AXES = ("grp", "sub")
BF16 = jnp.bfloat16
F32 = jnp.float32
VMEM = pl.BlockSpec(memory_space=pltpu.VMEM)
HBM = pl.BlockSpec(memory_space=pltpu.HBM)


def mm(a, b):
    return jnp.dot(a, b, preferred_element_type=F32)


def mm_t(a, b, **kw):
    return lax.dot_general(a, b, (((0,), (0,)), ((), ())), preferred_element_type=F32, **kw)


def mm_nt(a, b, **kw):
    return lax.dot_general(a, b, (((1,), (1,)), ((), ())), preferred_element_type=F32, **kw)


def position():
    return lax.axis_index("grp") * lax.axis_size("sub") + lax.axis_index("sub")


def is_even():
    return position() % 2 == 0


def place_matrix(row, total):
    place = lax.broadcasted_iota(jnp.int32, (total, row.shape[1]), 0)
    return (place == row).astype(F32).astype(BF16)


def send_matrix(rows_ref, total):
    left, right = rows_ref[0, 0:1, :], rows_ref[0, 1:2, :]
    even = is_even()
    rows = jnp.concatenate([jnp.where(even, right, left), jnp.where(even, left, right)], axis=1)
    return place_matrix(rows, total)


def copy_all(copies, sems):
    started = [pltpu.make_async_copy(source, target, sems.at[n]) for n, (source, target) in enumerate(copies)]
    for copy in started:
        copy.start()
    return started


def split_three(value):
    high = value.astype(BF16)
    rest = value - high.astype(F32)
    middle = rest.astype(BF16)
    return high, middle, (rest - middle.astype(F32)).astype(BF16)


def load_kernel(x_hbm, rows_hbm, up_hbm, basis_hbm, b_hbm, diag_hbm, values_hbm, cols_hbm, cl_hbm, cr_hbm,
                to_pair_ref, to_other_ref, basis_pair_ref, basis_other_ref, x_ref, rows_ref, basis_ref, b_ref, diag_ref, operator_ref,
                up_ref, cols_ref, values_ref, sems):
    blocks, nonzeros, size = values_hbm.shape[1], values_hbm.shape[2], values_hbm.shape[3]
    cases, rows = x_ref.shape
    margin = rows_ref.shape[2]
    copies = copy_all(
        [
            (rows_hbm, rows_ref),
            (x_hbm, x_ref),
            (up_hbm, up_ref),
            (basis_hbm, basis_ref),
            (cols_hbm, cols_ref),
            (values_hbm, values_ref),
            (cl_hbm, operator_ref.at[:, rows:rows + margin]),
            (cr_hbm, operator_ref.at[:, rows + margin:]),
            (diag_hbm, diag_ref),
            (b_hbm, b_ref),
        ],
        sems,
    )
    operator_ref[:, :rows] = jnp.zeros((rows, rows), BF16)
    for copy in copies[:4]:
        copy.wait()
    place = send_matrix(rows_ref, rows)
    sent = mm(x_ref[...].astype(BF16), place).astype(BF16)
    to_pair_ref[:cases, :] = sent[:, :margin]
    to_other_ref[...] = sent[:, margin:]
    parts = [part.astype(F32) for part in split_three(up_ref[0])]
    modes = up_ref.shape[1]
    parts.append(jnp.zeros((modes, margin - 3 * modes), F32))
    to_pair_ref[cases:, :] = jnp.concatenate(parts, axis=1).astype(BF16)
    basis = basis_ref[0]
    even = is_even()
    head, tail = basis[:, :margin], basis[:, margin + rows:]
    picked = mm(basis[:, margin:margin + rows], place).astype(BF16)
    basis_pair_ref[:, :margin] = jnp.where(even, tail, head)
    basis_pair_ref[:, margin:] = picked[:, :margin]
    basis_other_ref[:, :margin] = jnp.where(even, head, tail)
    basis_other_ref[:, margin:] = picked[:, margin:]
    for copy in copies[4:6]:
        copy.wait()
    for i in range(blocks):
        for t in range(nonzeros):
            start = pl.multiple_of(cols_ref[t, 0, i] * size, size)
            operator_ref[i * size:(i + 1) * size, pl.ds(start, size)] = values_ref[0, i, t]
    for copy in copies[6:]:
        copy.wait()


def own_kernel(x_ref, b_ref, diag_ref, operator_ref, partial_ref):
    x = x_ref[...]
    rows = x.shape[1]
    diag = diag_ref[...].reshape(1, rows)
    partial_ref[...] = b_ref[...] - diag * x - mm_nt(x.astype(BF16), operator_ref[:, :rows])


def offer_kernel(partial_ref, operator_ref, rows_ref, pair_ref, to_other_ref, known_ref, message_ref):
    cases, rows = partial_ref.shape
    margin = rows_ref.shape[2]
    even = is_even()
    left, right = operator_ref[:, rows:rows + margin], operator_ref[:, rows + margin:]
    from_pair = jnp.where(even, right, left)
    from_other = jnp.where(even, left, right)
    known = partial_ref[...] - mm_nt(pair_ref[:cases, :], from_pair)
    known_ref[...] = known
    high = known.astype(BF16)
    low = (known - high.astype(F32)).astype(BF16)
    place = place_matrix(jnp.where(even, rows_ref[0, 0:1, :], rows_ref[0, 1:2, :]), rows)
    message_ref[:cases, :] = to_other_ref[...]
    message_ref[cases:2 * cases, :] = mm(high, place).astype(BF16)
    message_ref[2 * cases:3 * cases, :] = mm(low, place).astype(BF16)
    message_ref[3 * cases:, :] = mm_t(place, from_other).astype(BF16)


def inverse_kernel(first_pair_ref, inverse_hbm, diag_hbm, up_hbm,
                   inverse_ref, factor_ref, plain_ref, blocks_ref, sems):
    size = diag_hbm.shape[1]
    cases = first_pair_ref.shape[0] - size
    copies = copy_all(
        [
            (diag_hbm, blocks_ref.at[0:1]),
            (up_hbm, blocks_ref.at[1:2]),
            (inverse_hbm, inverse_ref),
        ],
        sems,
    )
    parts = first_pair_ref[cases:, :].astype(F32)
    up_left = parts[:, :size] + (parts[:, size:2 * size] + parts[:, 2 * size:3 * size])
    for copy in copies[:2]:
        copy.wait()
    last = position() == lax.axis_size("grp") * lax.axis_size("sub") - 1
    up = jnp.where(last, 0.0, blocks_ref[1])
    diag = blocks_ref[0]
    row = lax.broadcasted_iota(jnp.int32, (size, size), 0)
    lane = lax.broadcasted_iota(jnp.int32, (size, size), 1)
    identity = (row == lane).astype(F32)
    factor = reduce_rows([jnp.concatenate([diag, jnp.transpose(up_left), up, identity], axis=1)])[0]
    odd = jnp.concatenate([jnp.transpose(up), factor[:, size:3 * size], jnp.zeros((size, size), F32)], axis=1)
    even = jnp.concatenate([diag, up, jnp.zeros((size, 2 * size), F32)], axis=1)
    plain_ref[...] = jnp.where(is_even(), even, odd)
    lanes = lax.broadcasted_iota(jnp.int32, factor.shape, 1)
    factor_ref[...] = jnp.where(lanes >= 3 * size, factor, 0.0)
    for copy in copies[2:]:
        copy.wait()


def residual_kernel(known_ref, operator_ref, rows_ref, sent_ref, other_ref, loaded_ref, r_ref, rb_ref, to_pair_ref, halo_ref):
    cases, rows = known_ref.shape
    margin = rows_ref.shape[2]
    even = is_even()
    from_other = jnp.where(even, operator_ref[:, rows:rows + margin], operator_ref[:, rows + margin:])
    r = known_ref[...] - mm_nt(other_ref[:cases, :], from_other)
    r_ref[...] = r
    rounded = r.astype(BF16)
    rb_ref[...] = rounded
    place = place_matrix(jnp.where(even, rows_ref[0, 1:2, :], rows_ref[0, 0:1, :]), rows)
    to_pair_ref[...] = mm(rounded, place).astype(BF16)
    offered = other_ref[cases:2 * cases, :].astype(F32) + other_ref[2 * cases:3 * cases, :].astype(F32)
    halo_ref[...] = (offered - mm_nt(sent_ref[...], other_ref[3 * cases:, :])).astype(BF16)


def own_local_kernel(rb_ref, inverse_ref, basis_ref, halo_ref, local_ref, coarse_ref):
    even = is_even()
    me = position()
    exists = (me > 0) & (me < lax.axis_size("grp") * lax.axis_size("sub") - 1)
    halo = jnp.where(exists, halo_ref[...], jnp.zeros_like(halo_ref))
    zero = jnp.zeros_like(halo)
    extended = jnp.concatenate([jnp.where(even, halo, zero), rb_ref[...], jnp.where(even, zero, halo)], axis=1)
    local_ref[...] = mm(extended, inverse_ref[0])
    coarse_ref[...] = mm_nt(basis_ref[0], extended)


def local_kernel(own_local_ref, own_coarse_ref, inverse_ref, basis_ref, factor_ref, plain_ref, pair_ref,
                 local_ref, message_ref):
    margin = pair_ref.shape[1]
    even = is_even()
    pair = pair_ref[...]
    total = inverse_ref.shape[1]
    ends = jnp.where(even, basis_ref[0, :, total - margin:], basis_ref[0, :, :margin])
    coarse_in = own_coarse_ref[...] + mm_nt(ends, pair)
    size = coarse_in.shape[0]
    stacked = jnp.concatenate([jnp.zeros((3 * size, coarse_in.shape[1]), F32), coarse_in], axis=0)
    reduced = jnp.dot(factor_ref[...], stacked, precision=lax.Precision.HIGHEST, preferred_element_type=F32)
    right_side = jnp.where(even, coarse_in, reduced)
    message = jnp.concatenate([plain_ref[:, :3 * size], right_side], axis=1)
    message_ref[...] = message
    rows = jnp.where(even, inverse_ref[0, total - margin:, :], inverse_ref[0, :margin, :])
    local_ref[...] = own_local_ref[...] + mm(pair, rows)


def return_kernel(local_ref, basis_pair_ref, basis_other_ref, rows_ref, to_pair_ref, to_other_ref):
    cases = local_ref.shape[0]
    margin = rows_ref.shape[2]
    even = is_even()
    local = local_ref[...]
    left, right = rows_ref[0, 0:1, :], rows_ref[0, 1:2, :]
    to_pair_ref[:cases, :] = return_rows(local, margin, jnp.where(even, right, left), jnp.logical_not(even))
    to_pair_ref[cases:, :] = basis_pair_ref[...]
    to_other_ref[:cases, :] = return_rows(local, margin, jnp.where(even, left, right), even)
    to_other_ref[cases:, :] = basis_other_ref[...]


def return_rows(local, margin, rows, head):
    owned = local.shape[1] - 2 * margin
    rounded = local.astype(BF16)
    tail = jnp.where(head, rounded[:, :margin], rounded[:, margin + owned:])
    return jnp.concatenate([tail, mm(rounded[:, margin:margin + owned], place_matrix(rows, owned)).astype(BF16)], axis=1)


def reduce_rows(blocks):
    size, width = blocks[0].shape
    panel = 16 if len(blocks) == 1 else 8 if len(blocks) == 2 else 4
    lanes, tile = 128, 8
    here = lax.broadcasted_iota(jnp.int32, (tile, 1), 0)
    tiles = range(size // tile)
    blocks = [[block[t * tile:(t + 1) * tile, :] for t in tiles] for block in blocks]

    def wide(value):
        return jnp.concatenate([value] * (width // lanes), axis=1)

    for first in range(0, size, panel):
        panels = [
            [[jnp.broadcast_to(rows[:, q:q + 1], (tile, lanes)) for rows in block] for q in range(first, first + panel)]
            for block in blocks
        ]
        for a in range(panel):
            at, inside = divmod(first + a, tile)
            for block, columns in zip(blocks, panels):
                column = columns[a]
                inverse = 1.0 / column[at][inside:inside + 1, :]
                for b in range(a + 1, panel):
                    entry = columns[b][at][inside:inside + 1, :] * inverse
                    columns[b] = [
                        jnp.where(here == inside, entry, columns[b][t] - column[t] * entry)
                        if t == at else columns[b][t] - column[t] * entry
                        for t in tiles
                    ]
                row = block[at][inside:inside + 1, :] * wide(inverse)
                for t in tiles:
                    rest = block[t] - wide(column[t]) * row
                    block[t] = jnp.where(here == inside, row, rest) if t == at else rest
    return [jnp.concatenate(block, axis=0) for block in blocks]


def shares(top, bottom, size):
    lanes = 4 * size
    lane = lax.broadcasted_iota(jnp.int32, (size, lanes), 1)

    def placed(product, slot, empty):
        first = product[:, :lanes]
        diag = pltpu.roll(first, lanes - slot * size, axis=1)
        first = jnp.where(lane < size, diag, jnp.where((lane >= empty * size) & (lane < (empty + 1) * size), 0.0, first))
        return jnp.concatenate([first, product[:, lanes:]], axis=1)

    return placed(top, 1, 1), placed(bottom, 2, 2)


def exact_product(left, right):
    a, b, c = split_three(left)
    x, y, z = split_three(right)
    return mm(jnp.concatenate([a, a, b, a, b, c], axis=1), jnp.concatenate([x, y, x, z, y, x], axis=0))


def schur(block, solved, size):
    couplings = jnp.transpose(block[:, :4 * size])[size:3 * size]
    product = -exact_product(couplings, solved)
    return shares(product[:size], product[size:], size)


def first_schur(previous, block, size):
    couplings = jnp.concatenate([previous[:, size:2 * size], block[:, :size]], axis=0)
    product = -exact_product(couplings, block)
    return shares(product[:size], product[size:], size)


def own_part(block, size):
    lane = lax.broadcasted_iota(jnp.int32, block.shape, 1)
    return jnp.where((lane >= size) & (lane < 3 * size), 0.0, block)


def combine(chain, parts, step, size):
    for i in range(0, len(chain), 2 * step):
        total = own_part(chain[i], size)
        if i + step in parts:
            total = total + parts[i + step][0]
        if i - step in parts:
            total = total + parts[i - step][1]
        chain[i] = total


def eliminate(chain, size, keep, step=1):
    count = len(chain) - 1
    while step < count:
        inner = list(range(step, count, 2 * step))
        solved = dict(zip(inner, reduce_rows([chain[j] for j in inner])))
        parts = {j: schur(chain[j], solved[j], size) for j in inner}
        for j in inner:
            keep(j, solved[j])
        combine(chain, parts, step, size)
        step = 2 * step
    return chain[0], chain[count]


def back(solved, left, right, size, alone=None):
    zero = jnp.zeros_like(left)
    stacked = jnp.concatenate([zero, left, right, zero], axis=0)
    alone = solved if alone is None else alone
    return alone - jnp.dot(
        solved[:, :4 * size], stacked, precision=lax.Precision.HIGHEST, preferred_element_type=F32)


def padded(count):
    total = 1
    while total < count:
        total = 2 * total
    return total


def group_kernel(*refs):
    *received, solved_ref, message_ref, blocks_ref = refs
    half = len(received) // 2
    size, width = received[0].shape
    members = 2 * half
    member = lax.axis_index("sub")
    for d in range(half):
        blocks_ref[member ^ (2 * d)] = received[d][...]
        blocks_ref[member ^ (2 * d + 1)] = received[half + d][...]
    chain = [blocks_ref[j] for j in range(members)]
    chain.append(jnp.zeros((size, width), F32))

    def keep(j, solved):
        solved_ref[j] = solved

    parts = {}
    for j in range(1, members, 2):
        keep(j, chain[j])
        parts[j] = first_schur(chain[j - 1], chain[j], size)
    combine(chain, parts, 1, size)
    head, tail = eliminate(chain, size, keep, 2)
    message_ref[:size, :] = head
    message_ref[size:2 * size, :] = tail
    lane = lax.broadcasted_iota(jnp.int32, (size, width), 1)
    step = members // 2
    at = step
    whole = solved_ref[at]
    zero = jnp.zeros((size, width), F32)
    while at < members - 1:
        step = step // 2
        at = at + step
        block = solved_ref[at]
        stacked = jnp.concatenate([zero, whole, zero, zero], axis=0)
        through = jnp.dot(
            block[:, :4 * size], stacked, precision=lax.Precision.HIGHEST, preferred_element_type=F32)
        whole = jnp.where((lane >= size) & (lane < 2 * size), 0.0, block) - through
    message_ref[2 * size:, :] = whole


def compose_kernel(solved_ref, maps_ref, all_ref):
    members, size, width = solved_ref.shape
    lane = lax.broadcasted_iota(jnp.int32, (size, width), 1)
    row = lax.broadcasted_iota(jnp.int32, (size, width), 0)
    maps = {0: -(lane == row + size).astype(F32), members: -(lane == row + 2 * size).astype(F32)}
    step = members // 2
    while step >= 1:
        for j in range(step, members, 2 * step):
            block = solved_ref[j]
            maps[j] = back(block, maps[j - step], maps[j + step], size, own_part(block, size))
        step = step // 2
    for j in range(members + 1):
        all_ref[j] = maps[j]
    member = lax.axis_index("sub")
    maps_ref[0] = all_ref[jnp.maximum(member - 1, 0)]
    maps_ref[1] = all_ref[member]
    maps_ref[2] = all_ref[member + 1]


def solve_kernel(*refs):
    (*received, maps_ref, local_ref, basis_ref, rows_ref, pair_ref, other_ref, r_ref, diag_ref, operator_ref,
     p_ref, image_ref, sums_ref, messages_ref, sep_ref) = refs
    groups = len(received)
    size, width = received[0].shape
    size = size // 3
    for d in range(groups):
        messages_ref[lax.axis_index("grp") ^ d] = received[d][...]
    chain = []
    for g in range(groups):
        total = messages_ref[g, :size, :]
        if g:
            total = total + messages_ref[g - 1, size:2 * size, :]
        chain.append(total)
    count = padded(groups)
    row = lax.broadcasted_iota(jnp.int32, (size, width), 0)
    lane = lax.broadcasted_iota(jnp.int32, (size, width), 1)
    while len(chain) < count:
        chain.append((row == lane).astype(F32))
    chain.append(jnp.zeros((size, width), F32))
    factors = {}
    head, _ = eliminate(chain, size, factors.__setitem__)
    solution = {count: jnp.zeros((size, width), F32)}
    solution[0] = reduce_rows([head])[0]
    step = count // 2
    while step >= 1:
        for j in range(step, count, 2 * step):
            solution[j] = back(factors[j], solution[j - step], solution[j + step], size)
        step = step // 2
    for g in range(groups):
        sep_ref[g] = solution[g]
    sep_ref[groups] = jnp.zeros((size, width), F32)
    group, member = lax.axis_index("grp"), lax.axis_index("sub")
    first, after = sep_ref[group], sep_ref[group + 1]
    before = jnp.maximum(group - 1, 0)
    is_first = member == 0
    left_map = jnp.where(is_first, messages_ref[before, 2 * size:, :], maps_ref[0])
    left_solution = back(
        left_map, jnp.where(is_first, sep_ref[before], first), jnp.where(is_first, first, after), size)
    own_solution = back(maps_ref[1], first, after, size)
    right_solution = back(maps_ref[2], first, after, size)

    def lifted(solution, basis):
        return mm_t(solution.astype(BF16), basis)[3 * size:]

    cases = local_ref.shape[0]
    margin = rows_ref.shape[2]
    owned = p_ref.shape[1]
    even = is_even()
    pair, other = pair_ref[...], other_ref[...]
    left, right = jnp.where(even, other, pair), jnp.where(even, pair, other)
    left = left[:cases].astype(F32) + lifted(left_solution, left[cases:])
    right = right[:cases].astype(F32) + lifted(right_solution, right[cases:])
    correction = local_ref[...] + lifted(own_solution, basis_ref[0])
    place = place_matrix(jnp.concatenate([rows_ref[0, 0:1, :], rows_ref[0, 1:2, :]], axis=1), owned)
    tails = jnp.concatenate([left[:, :margin], right[:, :margin]], axis=1).astype(BF16)
    p = correction[:, margin:margin + owned] + mm_nt(tails, place)
    p_ref[...] = p
    me = position()
    last = lax.axis_size("grp") * lax.axis_size("sub") - 1
    left = jnp.where(me == 0, 0.0, left[:, margin:] + correction[:, :margin]).astype(BF16)
    right = jnp.where(me == last, 0.0, right[:, margin:] + correction[:, margin + owned:]).astype(BF16)
    values = jnp.concatenate([p.astype(BF16), left, right], axis=1)
    image = diag_ref[...].reshape(1, owned) * p + mm_nt(values, operator_ref[...])
    image_ref[...] = image
    inner = row_sum(r_ref[...] * p)
    curvature = row_sum(p * image)
    sums = jnp.concatenate([inner[0:1], curvature[0:1]], axis=0)
    for slot in range(sums_ref.shape[0]):
        sums_ref[slot] = sums


def row_sum(values):
    lanes = 128
    total = values[:, :lanes]
    for start in range(lanes, values.shape[1], lanes):
        total = total + values[:, start:start + lanes]
    return mm_nt(jnp.ones((8, lanes), F32), total, precision=lax.Precision.HIGHEST)


def finish_kernel(x_ref, p_ref, r_ref, image_ref, sums_ref, out_x_hbm, out_r_hbm, new_x_ref, new_r_ref, sems):
    sums = jnp.sum(sums_ref[...], axis=0)
    row = sums[0:1, :] / sums[1:2, :]
    lanes = 128
    step = jnp.transpose(jnp.broadcast_to(row, (lanes, row.shape[1])))
    copies = []
    for chunk in range(x_ref.shape[1] // lanes):
        span = slice(chunk * lanes, (chunk + 1) * lanes)
        new_x_ref[:, span] = x_ref[:, span] + step * p_ref[:, span]
        new_r_ref[:, span] = r_ref[:, span] - step * image_ref[:, span]
        for n, (source, target) in enumerate(((new_x_ref, out_x_hbm), (new_r_ref, out_r_hbm))):
            copy = pltpu.make_async_copy(source.at[:, span], target.at[:, span], sems.at[n, chunk])
            copy.start()
            copies.append(copy)
    for copy in copies:
        copy.wait()


def call(kernel, out, in_specs, scratch=(), out_spec=VMEM):
    return pl.pallas_call(
        kernel,
        out_shape=out,
        in_specs=in_specs,
        out_specs=[out_spec] * len(out),
        scratch_shapes=list(scratch),
        compiler_params=pltpu.CompilerParams(vmem_limit_bytes=16 * 2**20),
    )


def far(*arrays):
    return [pltpu.with_memory_space_constraint(array, pltpu.HBM) for array in arrays]


def struct(shape, dtype):
    return jax.ShapeDtypeStruct(shape, dtype)


def shards(right_side, iterate_in, diagonal, block_values, block_cols, couple_left, couple_right, send_rows,
           local_inverse, coarse_basis, coarse_diag, coarse_up):
    groups, members = lax.axis_size("grp"), lax.axis_size("sub")
    total = groups * members
    rows, cases = right_side.shape
    margin = send_rows.shape[2]
    extended = local_inverse.shape[1]
    modes = coarse_basis.shape[2]
    width = 3 * modes + cases
    pairs = [(i, i ^ 1) for i in range(total)]
    others = [(i, i + 1 if i % 2 else i - 1) for i in range(1, total - 1)]
    right_side, iterate_in = right_side.T, iterate_in.T
    basis = jnp.swapaxes(coarse_basis, 1, 2)
    block_cols = jnp.transpose(block_cols, (2, 0, 1))

    halo = struct((cases, margin), BF16)
    full = struct((cases, rows), F32)
    semaphores = pltpu.SemaphoreType.DMA
    to_pair, to_other, basis_pair, basis_other, start, send_rows, basis, loads, diag, operator = call(
        load_kernel,
        [
            struct((cases + modes, margin), BF16),
            halo,
            struct((modes, 2 * margin), BF16),
            struct((modes, 2 * margin), BF16),
            full,
            struct(send_rows.shape, send_rows.dtype),
            struct(basis.shape, BF16),
            full,
            struct(diagonal.shape, F32),
            struct((rows, rows + 2 * margin), BF16),
        ],
        [HBM] * 10,
        [
            pltpu.VMEM(coarse_up.shape, F32),
            pltpu.SMEM(block_cols.shape, block_cols.dtype),
            pltpu.VMEM(block_values.shape, BF16),
            semaphores((10,)),
        ],
    )(*far(
        iterate_in, send_rows, coarse_up, basis, right_side, diagonal, block_values, block_cols, couple_left, couple_right
    ))
    first_pair = lax.ppermute(to_pair, AXES, pairs)
    (partial,) = call(own_kernel, [full], [VMEM] * 4)(start, loads, diag, operator)
    known, message = call(offer_kernel, [full, struct((3 * cases + margin, margin), BF16)], [VMEM] * 5)(
        partial, operator, send_rows, first_pair, to_other
    )
    first_other = lax.ppermute(message, AXES, others)
    inverse, factor, plain = call(
        inverse_kernel,
        [struct(local_inverse.shape, BF16), struct((modes, 4 * modes), F32), struct((modes, 4 * modes), F32)],
        [VMEM] + [HBM] * 3,
        [pltpu.VMEM((2, modes, modes), F32), semaphores((3,))],
    )(first_pair, *far(local_inverse, coarse_diag, coarse_up))
    residual, rounded, to_pair, other_halo = call(
        residual_kernel, [full, struct((cases, rows), BF16), halo, halo], [VMEM] * 6
    )(known, operator, send_rows, to_other, first_other, plain)
    pair_halo = lax.ppermute(to_pair, AXES, pairs)
    local, coarse = call(own_local_kernel, [struct((cases, extended), F32), struct((modes, cases), F32)], [VMEM] * 4)(
        rounded, inverse, basis, other_halo
    )
    chips = members // 2
    local, message = call(
        local_kernel, [struct((cases, extended), F32), struct((modes, width), F32)], [VMEM] * 7
    )(local, coarse, inverse, basis, factor, plain, pair_halo)
    returned = struct((cases + modes, 2 * margin), BF16)
    to_pair, to_other = call(return_kernel, [returned, returned], [VMEM] * 4)(local, basis_pair, basis_other, send_rows)
    from_other = lax.ppermute(to_other, AXES, others)
    from_pair = lax.ppermute(to_pair, AXES, pairs)

    def partners(value, stride, count):
        swaps = [[(i, i ^ (stride * d)) for i in range(total)] for d in range(1, count)]
        return [value] + [lax.ppermute(value, AXES, swap) for swap in swaps]

    same = partners(message, 2, chips)
    opposite = [lax.ppermute(value, AXES, pairs) for value in same]
    block = pltpu.VMEM((members, modes, width), F32)
    solved, reduced = call(
        group_kernel,
        [struct((members, modes, width), F32), struct((3 * modes, width), F32)],
        [VMEM] * members,
        [block],
    )(*same, *opposite)
    reduced = partners(reduced, members, groups)
    (maps,) = call(
        compose_kernel,
        [struct((3, modes, width), F32)],
        [VMEM],
        [pltpu.VMEM((members + 1, modes, width), F32)],
    )(solved)
    direction, image, sums = call(
        solve_kernel,
        [full, full, struct((total, 2, cases), F32)],
        [VMEM] * (groups + 9),
        [pltpu.VMEM((groups, 3 * modes, width), F32), pltpu.VMEM((groups + 1, modes, width), F32)],
    )(*reduced, maps, local, basis, send_rows, from_pair, from_other, residual, diag, operator)
    sums = lax.all_to_all(sums, AXES, 0, 0, tiled=True)
    iterate, residual = call(
        finish_kernel,
        [full, full],
        [VMEM] * 5,
        [pltpu.VMEM((cases, rows), F32), pltpu.VMEM((cases, rows), F32), semaphores((2, rows // margin))],
        HBM,
    )(start, direction, residual, image, sums)
    return iterate.T, residual.T


def solution(mesh):
    def spec(rank):
        return P(AXES, *([None] * (rank - 1)))

    return jax.shard_map(
        shards,
        mesh=mesh,
        in_specs=tuple(spec(rank) for rank in (2, 2, 1, 5, 3, 2, 2, 3, 3, 3, 3, 3)),
        out_specs=(spec(2), spec(2)),
        check_vma=False,
    )
```

```python
import jax
import jax.numpy as jnp
from jax import lax
from jax.experimental import pallas as pl
from jax.experimental.pallas import tpu as pltpu
from jax.sharding import PartitionSpec as P


AXES = ("grp", "sub")
BF16 = jnp.bfloat16
F32 = jnp.float32
VMEM = pl.BlockSpec(memory_space=pltpu.VMEM)
HBM = pl.BlockSpec(memory_space=pltpu.HBM)


def mm(a, b):
    return jnp.dot(a, b, preferred_element_type=F32)


def mm_t(a, b, **kw):
    return lax.dot_general(a, b, (((0,), (0,)), ((), ())), preferred_element_type=F32, **kw)


def mm_nt(a, b, **kw):
    return lax.dot_general(a, b, (((1,), (1,)), ((), ())), preferred_element_type=F32, **kw)


def position():
    return lax.axis_index("grp") * lax.axis_size("sub") + lax.axis_index("sub")


def is_even():
    return position() % 2 == 0


def place_matrix(row, total):
    place = lax.broadcasted_iota(jnp.int32, (total, row.shape[1]), 0)
    return (place == row).astype(F32).astype(BF16)


def send_matrix(rows_ref, total):
    left, right = rows_ref[0, 0:1, :], rows_ref[0, 1:2, :]
    even = is_even()
    rows = jnp.concatenate([jnp.where(even, right, left), jnp.where(even, left, right)], axis=1)
    return place_matrix(rows, total)


def copy_all(copies, sems):
    started = [pltpu.make_async_copy(source, target, sems.at[n]) for n, (source, target) in enumerate(copies)]
    for copy in started:
        copy.start()
    return started


def split_three(value):
    high = value.astype(BF16)
    rest = value - high.astype(F32)
    middle = rest.astype(BF16)
    return high, middle, (rest - middle.astype(F32)).astype(BF16)


def load_kernel(x_hbm, rows_hbm, up_hbm, basis_hbm, b_hbm, diag_hbm, values_hbm, cols_hbm, cl_hbm, cr_hbm,
                to_pair_ref, to_other_ref, basis_pair_ref, basis_other_ref, x_ref, rows_ref, basis_ref, b_ref, diag_ref, operator_ref,
                up_ref, cols_ref, values_ref, sems):
    blocks, nonzeros, size = values_hbm.shape[1], values_hbm.shape[2], values_hbm.shape[3]
    cases, rows = x_ref.shape
    margin = rows_ref.shape[2]
    copies = copy_all(
        [
            (rows_hbm, rows_ref),
            (x_hbm, x_ref),
            (up_hbm, up_ref),
            (basis_hbm, basis_ref),
            (cols_hbm, cols_ref),
            (values_hbm, values_ref),
            (cl_hbm, operator_ref.at[:, rows:rows + margin]),
            (cr_hbm, operator_ref.at[:, rows + margin:]),
            (diag_hbm, diag_ref),
            (b_hbm, b_ref),
        ],
        sems,
    )
    operator_ref[:, :rows] = jnp.zeros((rows, rows), BF16)
    for copy in copies[:4]:
        copy.wait()
    place = send_matrix(rows_ref, rows)
    sent = mm(x_ref[...].astype(BF16), place).astype(BF16)
    to_pair_ref[:cases, :] = sent[:, :margin]
    to_other_ref[...] = sent[:, margin:]
    parts = [part.astype(F32) for part in split_three(up_ref[0])]
    modes = up_ref.shape[1]
    parts.append(jnp.zeros((modes, margin - 3 * modes), F32))
    to_pair_ref[cases:, :] = jnp.concatenate(parts, axis=1).astype(BF16)
    basis = basis_ref[0]
    even = is_even()
    head, tail = basis[:, :margin], basis[:, margin + rows:]
    picked = mm(basis[:, margin:margin + rows], place).astype(BF16)
    basis_pair_ref[:, :margin] = jnp.where(even, tail, head)
    basis_pair_ref[:, margin:] = picked[:, :margin]
    basis_other_ref[:, :margin] = jnp.where(even, head, tail)
    basis_other_ref[:, margin:] = picked[:, margin:]
    for copy in copies[4:6]:
        copy.wait()
    for i in range(blocks):
        for t in range(nonzeros):
            start = pl.multiple_of(cols_ref[t, 0, i] * size, size)
            operator_ref[i * size:(i + 1) * size, pl.ds(start, size)] = values_ref[0, i, t]
    for copy in copies[6:]:
        copy.wait()


def own_kernel(x_ref, b_ref, diag_ref, operator_ref, partial_ref):
    x = x_ref[...]
    rows = x.shape[1]
    diag = diag_ref[...].reshape(1, rows)
    partial_ref[...] = b_ref[...] - diag * x - mm_nt(x.astype(BF16), operator_ref[:, :rows])


def offer_kernel(partial_ref, operator_ref, rows_ref, pair_ref, to_other_ref, known_ref, message_ref):
    cases, rows = partial_ref.shape
    margin = rows_ref.shape[2]
    even = is_even()
    left, right = operator_ref[:, rows:rows + margin], operator_ref[:, rows + margin:]
    from_pair = jnp.where(even, right, left)
    from_other = jnp.where(even, left, right)
    known = partial_ref[...] - mm_nt(pair_ref[:cases, :], from_pair)
    known_ref[...] = known
    high = known.astype(BF16)
    low = (known - high.astype(F32)).astype(BF16)
    place = place_matrix(jnp.where(even, rows_ref[0, 0:1, :], rows_ref[0, 1:2, :]), rows)
    message_ref[:cases, :] = to_other_ref[...]
    message_ref[cases:2 * cases, :] = mm(high, place).astype(BF16)
    message_ref[2 * cases:3 * cases, :] = mm(low, place).astype(BF16)
    message_ref[3 * cases:, :] = mm_t(place, from_other).astype(BF16)


def inverse_kernel(first_pair_ref, inverse_hbm, diag_hbm, up_hbm,
                   inverse_ref, factor_ref, plain_ref, blocks_ref, sems):
    size = diag_hbm.shape[1]
    cases = first_pair_ref.shape[0] - size
    copies = copy_all(
        [
            (diag_hbm, blocks_ref.at[0:1]),
            (up_hbm, blocks_ref.at[1:2]),
            (inverse_hbm, inverse_ref),
        ],
        sems,
    )
    parts = first_pair_ref[cases:, :].astype(F32)
    up_left = parts[:, :size] + (parts[:, size:2 * size] + parts[:, 2 * size:3 * size])
    for copy in copies[:2]:
        copy.wait()
    last = position() == lax.axis_size("grp") * lax.axis_size("sub") - 1
    up = jnp.where(last, 0.0, blocks_ref[1])
    diag = blocks_ref[0]
    row = lax.broadcasted_iota(jnp.int32, (size, size), 0)
    lane = lax.broadcasted_iota(jnp.int32, (size, size), 1)
    identity = (row == lane).astype(F32)
    factor = reduce_rows([jnp.concatenate([diag, jnp.transpose(up_left), up, identity], axis=1)])[0]
    odd = jnp.concatenate([jnp.transpose(up), factor[:, size:3 * size], jnp.zeros((size, size), F32)], axis=1)
    even = jnp.concatenate([diag, up, jnp.zeros((size, 2 * size), F32)], axis=1)
    plain_ref[...] = jnp.where(is_even(), even, odd)
    lanes = lax.broadcasted_iota(jnp.int32, factor.shape, 1)
    factor_ref[...] = jnp.where(lanes >= 3 * size, factor, 0.0)
    for copy in copies[2:]:
        copy.wait()


def residual_kernel(known_ref, operator_ref, rows_ref, sent_ref, other_ref, loaded_ref, r_ref, rb_ref, to_pair_ref, halo_ref):
    cases, rows = known_ref.shape
    margin = rows_ref.shape[2]
    even = is_even()
    from_other = jnp.where(even, operator_ref[:, rows:rows + margin], operator_ref[:, rows + margin:])
    r = known_ref[...] - mm_nt(other_ref[:cases, :], from_other)
    r_ref[...] = r
    rounded = r.astype(BF16)
    rb_ref[...] = rounded
    place = place_matrix(jnp.where(even, rows_ref[0, 1:2, :], rows_ref[0, 0:1, :]), rows)
    to_pair_ref[...] = mm(rounded, place).astype(BF16)
    offered = other_ref[cases:2 * cases, :].astype(F32) + other_ref[2 * cases:3 * cases, :].astype(F32)
    halo_ref[...] = (offered - mm_nt(sent_ref[...], other_ref[3 * cases:, :])).astype(BF16)


def own_local_kernel(rb_ref, inverse_ref, basis_ref, halo_ref, local_ref, coarse_ref):
    even = is_even()
    me = position()
    exists = (me > 0) & (me < lax.axis_size("grp") * lax.axis_size("sub") - 1)
    halo = jnp.where(exists, halo_ref[...], jnp.zeros_like(halo_ref))
    zero = jnp.zeros_like(halo)
    extended = jnp.concatenate([jnp.where(even, halo, zero), rb_ref[...], jnp.where(even, zero, halo)], axis=1)
    local_ref[...] = mm(extended, inverse_ref[0])
    coarse_ref[...] = mm_nt(basis_ref[0], extended)


def local_kernel(own_local_ref, own_coarse_ref, inverse_ref, basis_ref, factor_ref, plain_ref, pair_ref,
                 local_ref, message_ref):
    margin = pair_ref.shape[1]
    even = is_even()
    pair = pair_ref[...]
    total = inverse_ref.shape[1]
    ends = jnp.where(even, basis_ref[0, :, total - margin:], basis_ref[0, :, :margin])
    coarse_in = own_coarse_ref[...] + mm_nt(ends, pair)
    size = coarse_in.shape[0]
    stacked = jnp.concatenate([jnp.zeros((3 * size, coarse_in.shape[1]), F32), coarse_in], axis=0)
    reduced = jnp.dot(factor_ref[...], stacked, precision=lax.Precision.HIGHEST, preferred_element_type=F32)
    right_side = jnp.where(even, coarse_in, reduced)
    message = jnp.concatenate([plain_ref[:, :3 * size], right_side], axis=1)
    message_ref[...] = message
    rows = jnp.where(even, inverse_ref[0, total - margin:, :], inverse_ref[0, :margin, :])
    local_ref[...] = own_local_ref[...] + mm(pair, rows)


def return_kernel(local_ref, basis_pair_ref, basis_other_ref, rows_ref, to_pair_ref, to_other_ref):
    cases = local_ref.shape[0]
    margin = rows_ref.shape[2]
    even = is_even()
    local = local_ref[...]
    left, right = rows_ref[0, 0:1, :], rows_ref[0, 1:2, :]
    to_pair_ref[:cases, :] = return_rows(local, margin, jnp.where(even, right, left), jnp.logical_not(even))
    to_pair_ref[cases:, :] = basis_pair_ref[...]
    to_other_ref[:cases, :] = return_rows(local, margin, jnp.where(even, left, right), even)
    to_other_ref[cases:, :] = basis_other_ref[...]


def return_rows(local, margin, rows, head):
    owned = local.shape[1] - 2 * margin
    rounded = local.astype(BF16)
    tail = jnp.where(head, rounded[:, :margin], rounded[:, margin + owned:])
    return jnp.concatenate([tail, mm(rounded[:, margin:margin + owned], place_matrix(rows, owned)).astype(BF16)], axis=1)


def reduce_rows(blocks):
    size, width = blocks[0].shape
    panel = 16 if len(blocks) == 1 else 8 if len(blocks) == 2 else 4
    lanes, tile = 128, 8
    here = lax.broadcasted_iota(jnp.int32, (tile, 1), 0)
    tiles = range(size // tile)
    blocks = [[block[t * tile:(t + 1) * tile, :] for t in tiles] for block in blocks]

    def wide(value):
        return jnp.concatenate([value] * (width // lanes), axis=1)

    for first in range(0, size, panel):
        panels = [
            [[jnp.broadcast_to(rows[:, q:q + 1], (tile, lanes)) for rows in block] for q in range(first, first + panel)]
            for block in blocks
        ]
        for a in range(panel):
            at, inside = divmod(first + a, tile)
            for block, columns in zip(blocks, panels):
                column = columns[a]
                inverse = 1.0 / column[at][inside:inside + 1, :]
                for b in range(a + 1, panel):
                    entry = columns[b][at][inside:inside + 1, :] * inverse
                    columns[b] = [
                        jnp.where(here == inside, entry, columns[b][t] - column[t] * entry)
                        if t == at else columns[b][t] - column[t] * entry
                        for t in tiles
                    ]
                row = block[at][inside:inside + 1, :] * wide(inverse)
                for t in tiles:
                    rest = block[t] - wide(column[t]) * row
                    block[t] = jnp.where(here == inside, row, rest) if t == at else rest
    return [jnp.concatenate(block, axis=0) for block in blocks]


def shares(top, bottom, size):
    lanes = 4 * size
    lane = lax.broadcasted_iota(jnp.int32, (size, lanes), 1)

    def placed(product, slot, empty):
        first = product[:, :lanes]
        diag = pltpu.roll(first, lanes - slot * size, axis=1)
        first = jnp.where(lane < size, diag, jnp.where((lane >= empty * size) & (lane < (empty + 1) * size), 0.0, first))
        return jnp.concatenate([first, product[:, lanes:]], axis=1)

    return placed(top, 1, 1), placed(bottom, 2, 2)


def exact_product(left, right):
    a, b, c = split_three(left)
    x, y, z = split_three(right)
    return mm(jnp.concatenate([a, a, b, a, b, c], axis=1), jnp.concatenate([x, y, x, z, y, x], axis=0))


def schur(block, solved, size):
    couplings = jnp.transpose(block[:, :4 * size])[size:3 * size]
    product = -exact_product(couplings, solved)
    return shares(product[:size], product[size:], size)


def first_schur(previous, block, size):
    couplings = jnp.concatenate([previous[:, size:2 * size], block[:, :size]], axis=0)
    product = -exact_product(couplings, block)
    return shares(product[:size], product[size:], size)


def own_part(block, size):
    lane = lax.broadcasted_iota(jnp.int32, block.shape, 1)
    return jnp.where((lane >= size) & (lane < 3 * size), 0.0, block)


def combine(chain, parts, step, size):
    for i in range(0, len(chain), 2 * step):
        total = own_part(chain[i], size)
        if i + step in parts:
            total = total + parts[i + step][0]
        if i - step in parts:
            total = total + parts[i - step][1]
        chain[i] = total


def eliminate(chain, size, keep, step=1):
    count = len(chain) - 1
    while step < count:
        inner = list(range(step, count, 2 * step))
        solved = dict(zip(inner, reduce_rows([chain[j] for j in inner])))
        parts = {j: schur(chain[j], solved[j], size) for j in inner}
        for j in inner:
            keep(j, solved[j])
        combine(chain, parts, step, size)
        step = 2 * step
    return chain[0], chain[count]


def back(solved, left, right, size, alone=None):
    zero = jnp.zeros_like(left)
    stacked = jnp.concatenate([zero, left, right, zero], axis=0)
    alone = solved if alone is None else alone
    return alone - jnp.dot(
        solved[:, :4 * size], stacked, precision=lax.Precision.HIGHEST, preferred_element_type=F32)


def padded(count):
    total = 1
    while total < count:
        total = 2 * total
    return total


def group_kernel(*refs):
    *received, solved_ref, message_ref, blocks_ref = refs
    half = len(received) // 2
    size, width = received[0].shape
    members = 2 * half
    member = lax.axis_index("sub")
    for d in range(half):
        blocks_ref[member ^ (2 * d)] = received[d][...]
        blocks_ref[member ^ (2 * d + 1)] = received[half + d][...]
    chain = [blocks_ref[j] for j in range(members)]
    chain.append(jnp.zeros((size, width), F32))

    def keep(j, solved):
        solved_ref[j] = solved

    parts = {}
    for j in range(1, members, 2):
        keep(j, chain[j])
        parts[j] = first_schur(chain[j - 1], chain[j], size)
    combine(chain, parts, 1, size)
    head, tail = eliminate(chain, size, keep, 2)
    message_ref[:size, :] = head
    message_ref[size:2 * size, :] = tail
    lane = lax.broadcasted_iota(jnp.int32, (size, width), 1)
    step = members // 2
    at = step
    whole = solved_ref[at]
    zero = jnp.zeros((size, width), F32)
    while at < members - 1:
        step = step // 2
        at = at + step
        block = solved_ref[at]
        stacked = jnp.concatenate([zero, whole, zero, zero], axis=0)
        through = jnp.dot(
            block[:, :4 * size], stacked, precision=lax.Precision.HIGHEST, preferred_element_type=F32)
        whole = jnp.where((lane >= size) & (lane < 2 * size), 0.0, block) - through
    message_ref[2 * size:, :] = whole


def compose_kernel(solved_ref, maps_ref, all_ref):
    members, size, width = solved_ref.shape
    lane = lax.broadcasted_iota(jnp.int32, (size, width), 1)
    row = lax.broadcasted_iota(jnp.int32, (size, width), 0)
    maps = {0: -(lane == row + size).astype(F32), members: -(lane == row + 2 * size).astype(F32)}
    step = members // 2
    while step >= 1:
        for j in range(step, members, 2 * step):
            block = solved_ref[j]
            maps[j] = back(block, maps[j - step], maps[j + step], size, own_part(block, size))
        step = step // 2
    for j in range(members + 1):
        all_ref[j] = maps[j]
    member = lax.axis_index("sub")
    maps_ref[0] = all_ref[jnp.maximum(member - 1, 0)]
    maps_ref[1] = all_ref[member]
    maps_ref[2] = all_ref[member + 1]


def solve_kernel(*refs):
    (*received, maps_ref, local_ref, basis_ref, rows_ref, pair_ref, other_ref, r_ref, diag_ref, operator_ref,
     p_ref, image_ref, sums_ref, messages_ref, sep_ref) = refs
    groups = len(received)
    size, width = received[0].shape
    size = size // 3
    for d in range(groups):
        messages_ref[lax.axis_index("grp") ^ d] = received[d][...]
    chain = []
    for g in range(groups):
        total = messages_ref[g, :size, :]
        if g:
            total = total + messages_ref[g - 1, size:2 * size, :]
        chain.append(total)
    count = padded(groups)
    row = lax.broadcasted_iota(jnp.int32, (size, width), 0)
    lane = lax.broadcasted_iota(jnp.int32, (size, width), 1)
    while len(chain) < count:
        chain.append((row == lane).astype(F32))
    chain.append(jnp.zeros((size, width), F32))
    factors = {}
    head, _ = eliminate(chain, size, factors.__setitem__)
    solution = {count: jnp.zeros((size, width), F32)}
    solution[0] = reduce_rows([head])[0]
    step = count // 2
    while step >= 1:
        for j in range(step, count, 2 * step):
            solution[j] = back(factors[j], solution[j - step], solution[j + step], size)
        step = step // 2
    for g in range(groups):
        sep_ref[g] = solution[g]
    sep_ref[groups] = jnp.zeros((size, width), F32)
    group, member = lax.axis_index("grp"), lax.axis_index("sub")
    first, after = sep_ref[group], sep_ref[group + 1]
    before = jnp.maximum(group - 1, 0)
    is_first = member == 0
    left_map = jnp.where(is_first, messages_ref[before, 2 * size:, :], maps_ref[0])
    left_solution = back(
        left_map, jnp.where(is_first, sep_ref[before], first), jnp.where(is_first, first, after), size)
    own_solution = back(maps_ref[1], first, after, size)
    right_solution = back(maps_ref[2], first, after, size)

    def lifted(solution, basis):
        return mm_t(solution.astype(BF16), basis)[3 * size:]

    cases = local_ref.shape[0]
    margin = rows_ref.shape[2]
    owned = p_ref.shape[1]
    even = is_even()
    pair, other = pair_ref[...], other_ref[...]
    left, right = jnp.where(even, other, pair), jnp.where(even, pair, other)
    left = left[:cases].astype(F32) + lifted(left_solution, left[cases:])
    right = right[:cases].astype(F32) + lifted(right_solution, right[cases:])
    correction = local_ref[...] + lifted(own_solution, basis_ref[0])
    place = place_matrix(jnp.concatenate([rows_ref[0, 0:1, :], rows_ref[0, 1:2, :]], axis=1), owned)
    tails = jnp.concatenate([left[:, :margin], right[:, :margin]], axis=1).astype(BF16)
    p = correction[:, margin:margin + owned] + mm_nt(tails, place)
    p_ref[...] = p
    me = position()
    last = lax.axis_size("grp") * lax.axis_size("sub") - 1
    left = jnp.where(me == 0, 0.0, left[:, margin:] + correction[:, :margin]).astype(BF16)
    right = jnp.where(me == last, 0.0, right[:, margin:] + correction[:, margin + owned:]).astype(BF16)
    values = jnp.concatenate([p.astype(BF16), left, right], axis=1)
    image = diag_ref[...].reshape(1, owned) * p + mm_nt(values, operator_ref[...])
    image_ref[...] = image
    inner = row_sum(r_ref[...] * p)
    curvature = row_sum(p * image)
    sums = jnp.concatenate([inner[0:1], curvature[0:1]], axis=0)
    for slot in range(sums_ref.shape[0]):
        sums_ref[slot] = sums


def row_sum(values):
    lanes = 128
    total = values[:, :lanes]
    for start in range(lanes, values.shape[1], lanes):
        total = total + values[:, start:start + lanes]
    return mm_nt(jnp.ones((8, lanes), F32), total, precision=lax.Precision.HIGHEST)


def finish_kernel(x_ref, p_ref, r_ref, image_ref, sums_ref, out_x_ref, out_r_ref):
    sums = jnp.sum(sums_ref[...], axis=0)
    row = sums[0:1, :] / sums[1:2, :]
    lanes = 128
    step = jnp.transpose(jnp.broadcast_to(row, (lanes, row.shape[1])))
    for start in range(0, x_ref.shape[1], lanes):
        span = slice(start, start + lanes)
        out_x_ref[:, span] = x_ref[:, span] + step * p_ref[:, span]
        out_r_ref[:, span] = r_ref[:, span] - step * image_ref[:, span]


def call(kernel, out, in_specs, scratch=()):
    return pl.pallas_call(
        kernel,
        out_shape=out,
        in_specs=in_specs,
        out_specs=[VMEM] * len(out),
        scratch_shapes=list(scratch),
        compiler_params=pltpu.CompilerParams(vmem_limit_bytes=16 * 2**20),
    )


def far(*arrays):
    return [pltpu.with_memory_space_constraint(array, pltpu.HBM) for array in arrays]


def struct(shape, dtype):
    return jax.ShapeDtypeStruct(shape, dtype)


def shards(right_side, iterate_in, diagonal, block_values, block_cols, couple_left, couple_right, send_rows,
           local_inverse, coarse_basis, coarse_diag, coarse_up):
    groups, members = lax.axis_size("grp"), lax.axis_size("sub")
    total = groups * members
    rows, cases = right_side.shape
    margin = send_rows.shape[2]
    extended = local_inverse.shape[1]
    modes = coarse_basis.shape[2]
    width = 3 * modes + cases
    pairs = [(i, i ^ 1) for i in range(total)]
    others = [(i, i + 1 if i % 2 else i - 1) for i in range(1, total - 1)]
    right_side, iterate_in = right_side.T, iterate_in.T
    basis = jnp.swapaxes(coarse_basis, 1, 2)
    block_cols = jnp.transpose(block_cols, (2, 0, 1))

    halo = struct((cases, margin), BF16)
    full = struct((cases, rows), F32)
    semaphores = pltpu.SemaphoreType.DMA
    to_pair, to_other, basis_pair, basis_other, start, send_rows, basis, loads, diag, operator = call(
        load_kernel,
        [
            struct((cases + modes, margin), BF16),
            halo,
            struct((modes, 2 * margin), BF16),
            struct((modes, 2 * margin), BF16),
            full,
            struct(send_rows.shape, send_rows.dtype),
            struct(basis.shape, BF16),
            full,
            struct(diagonal.shape, F32),
            struct((rows, rows + 2 * margin), BF16),
        ],
        [HBM] * 10,
        [
            pltpu.VMEM(coarse_up.shape, F32),
            pltpu.SMEM(block_cols.shape, block_cols.dtype),
            pltpu.VMEM(block_values.shape, BF16),
            semaphores((10,)),
        ],
    )(*far(
        iterate_in, send_rows, coarse_up, basis, right_side, diagonal, block_values, block_cols, couple_left, couple_right
    ))
    first_pair = lax.ppermute(to_pair, AXES, pairs)
    (partial,) = call(own_kernel, [full], [VMEM] * 4)(start, loads, diag, operator)
    known, message = call(offer_kernel, [full, struct((3 * cases + margin, margin), BF16)], [VMEM] * 5)(
        partial, operator, send_rows, first_pair, to_other
    )
    first_other = lax.ppermute(message, AXES, others)
    inverse, factor, plain = call(
        inverse_kernel,
        [struct(local_inverse.shape, BF16), struct((modes, 4 * modes), F32), struct((modes, 4 * modes), F32)],
        [VMEM] + [HBM] * 3,
        [pltpu.VMEM((2, modes, modes), F32), semaphores((3,))],
    )(first_pair, *far(local_inverse, coarse_diag, coarse_up))
    residual, rounded, to_pair, other_halo = call(
        residual_kernel, [full, struct((cases, rows), BF16), halo, halo], [VMEM] * 6
    )(known, operator, send_rows, to_other, first_other, plain)
    pair_halo = lax.ppermute(to_pair, AXES, pairs)
    local, coarse = call(own_local_kernel, [struct((cases, extended), F32), struct((modes, cases), F32)], [VMEM] * 4)(
        rounded, inverse, basis, other_halo
    )
    chips = members // 2
    local, message = call(
        local_kernel, [struct((cases, extended), F32), struct((modes, width), F32)], [VMEM] * 7
    )(local, coarse, inverse, basis, factor, plain, pair_halo)
    returned = struct((cases + modes, 2 * margin), BF16)
    to_pair, to_other = call(return_kernel, [returned, returned], [VMEM] * 4)(local, basis_pair, basis_other, send_rows)
    from_other = lax.ppermute(to_other, AXES, others)
    from_pair = lax.ppermute(to_pair, AXES, pairs)

    def partners(value, stride, count):
        swaps = [[(i, i ^ (stride * d)) for i in range(total)] for d in range(1, count)]
        return [value] + [lax.ppermute(value, AXES, swap) for swap in swaps]

    same = partners(message, 2, chips)
    opposite = [lax.ppermute(same[0], AXES, pairs)]
    opposite += [lax.ppermute(value, AXES, pairs) for value in same[1:]]
    block = pltpu.VMEM((members, modes, width), F32)
    solved, reduced = call(
        group_kernel,
        [struct((members, modes, width), F32), struct((3 * modes, width), F32)],
        [VMEM] * members,
        [block],
    )(*same, *opposite)
    reduced = partners(reduced, members, groups)
    (maps,) = call(
        compose_kernel,
        [struct((3, modes, width), F32)],
        [VMEM],
        [pltpu.VMEM((members + 1, modes, width), F32)],
    )(solved)
    direction, image, sums = call(
        solve_kernel,
        [full, full, struct((total, 2, cases), F32)],
        [VMEM] * (groups + 9),
        [pltpu.VMEM((groups, 3 * modes, width), F32), pltpu.VMEM((groups + 1, modes, width), F32)],
    )(*reduced, maps, local, basis, send_rows, from_pair, from_other, residual, diag, operator)
    sums = lax.all_to_all(sums, AXES, 0, 0, tiled=True)
    iterate, residual = call(finish_kernel, [full, full], [VMEM] * 5)(start, direction, residual, image, sums)
    return iterate.T, residual.T


def solution(mesh):
    def spec(rank):
        return P(AXES, *([None] * (rank - 1)))

    return jax.shard_map(
        shards,
        mesh=mesh,
        in_specs=tuple(spec(rank) for rank in (2, 2, 1, 5, 3, 2, 2, 3, 3, 3, 3, 3)),
        out_specs=(spec(2), spec(2)),
        check_vma=False,
    )
```

```python
import jax
import jax.numpy as jnp
from jax import lax
from jax.experimental import pallas as pl
from jax.experimental.pallas import tpu as pltpu
from jax.sharding import PartitionSpec as P


AXES = ("grp", "sub")
BF16 = jnp.bfloat16
F32 = jnp.float32
VMEM = pl.BlockSpec(memory_space=pltpu.VMEM)
HBM = pl.BlockSpec(memory_space=pltpu.HBM)


def mm(a, b):
    return jnp.dot(a, b, preferred_element_type=F32)


def mm_t(a, b, **kw):
    return lax.dot_general(a, b, (((0,), (0,)), ((), ())), preferred_element_type=F32, **kw)


def mm_nt(a, b, **kw):
    return lax.dot_general(a, b, (((1,), (1,)), ((), ())), preferred_element_type=F32, **kw)


def position():
    return lax.axis_index("grp") * lax.axis_size("sub") + lax.axis_index("sub")


def is_even():
    return position() % 2 == 0


def place_matrix(row, total):
    place = lax.broadcasted_iota(jnp.int32, (total, row.shape[1]), 0)
    return (place == row).astype(F32).astype(BF16)


def send_matrix(rows_ref, total):
    left, right = rows_ref[0, 0:1, :], rows_ref[0, 1:2, :]
    even = is_even()
    rows = jnp.concatenate([jnp.where(even, right, left), jnp.where(even, left, right)], axis=1)
    return place_matrix(rows, total)


def copy_all(copies, sems):
    started = [pltpu.make_async_copy(source, target, sems.at[n]) for n, (source, target) in enumerate(copies)]
    for copy in started:
        copy.start()
    return started


def split_three(value):
    high = value.astype(BF16)
    rest = value - high.astype(F32)
    middle = rest.astype(BF16)
    return high, middle, (rest - middle.astype(F32)).astype(BF16)


def load_kernel(x_hbm, rows_hbm, up_hbm, basis_hbm, b_hbm, diag_hbm, values_hbm, cols_hbm, cl_hbm, cr_hbm,
                to_pair_ref, to_other_ref, basis_pair_ref, basis_other_ref, x_ref, rows_ref, basis_ref, b_ref, diag_ref, operator_ref,
                up_ref, cols_ref, values_ref, sems):
    blocks, nonzeros, size = values_hbm.shape[1], values_hbm.shape[2], values_hbm.shape[3]
    cases, rows = x_ref.shape
    margin = rows_ref.shape[2]
    copies = copy_all(
        [
            (rows_hbm, rows_ref),
            (x_hbm, x_ref),
            (up_hbm, up_ref),
            (basis_hbm, basis_ref),
            (cols_hbm, cols_ref),
            (values_hbm, values_ref),
            (cl_hbm, operator_ref.at[:, rows:rows + margin]),
            (cr_hbm, operator_ref.at[:, rows + margin:]),
            (diag_hbm, diag_ref),
            (b_hbm, b_ref),
        ],
        sems,
    )
    operator_ref[:, :rows] = jnp.zeros((rows, rows), BF16)
    for copy in copies[:4]:
        copy.wait()
    place = send_matrix(rows_ref, rows)
    sent = mm(x_ref[...].astype(BF16), place).astype(BF16)
    to_pair_ref[:cases, :] = sent[:, :margin]
    to_other_ref[...] = sent[:, margin:]
    parts = [part.astype(F32) for part in split_three(up_ref[0])]
    modes = up_ref.shape[1]
    parts.append(jnp.zeros((modes, margin - 3 * modes), F32))
    to_pair_ref[cases:, :] = jnp.concatenate(parts, axis=1).astype(BF16)
    basis = basis_ref[0]
    even = is_even()
    head, tail = basis[:, :margin], basis[:, margin + rows:]
    picked = mm(basis[:, margin:margin + rows], place).astype(BF16)
    basis_pair_ref[:, :margin] = jnp.where(even, tail, head)
    basis_pair_ref[:, margin:] = picked[:, :margin]
    basis_other_ref[:, :margin] = jnp.where(even, head, tail)
    basis_other_ref[:, margin:] = picked[:, margin:]
    for copy in copies[4:6]:
        copy.wait()
    for i in range(blocks):
        for t in range(nonzeros):
            start = pl.multiple_of(cols_ref[t, 0, i] * size, size)
            operator_ref[i * size:(i + 1) * size, pl.ds(start, size)] = values_ref[0, i, t]
    for copy in copies[6:]:
        copy.wait()


def own_kernel(x_ref, b_ref, diag_ref, operator_ref, partial_ref):
    x = x_ref[...]
    rows = x.shape[1]
    diag = diag_ref[...].reshape(1, rows)
    partial_ref[...] = b_ref[...] - diag * x - mm_nt(x.astype(BF16), operator_ref[:, :rows])


def offer_kernel(partial_ref, operator_ref, rows_ref, pair_ref, to_other_ref, known_ref, message_ref):
    cases, rows = partial_ref.shape
    margin = rows_ref.shape[2]
    even = is_even()
    left, right = operator_ref[:, rows:rows + margin], operator_ref[:, rows + margin:]
    from_pair = jnp.where(even, right, left)
    from_other = jnp.where(even, left, right)
    known = partial_ref[...] - mm_nt(pair_ref[:cases, :], from_pair)
    known_ref[...] = known
    high = known.astype(BF16)
    low = (known - high.astype(F32)).astype(BF16)
    place = place_matrix(jnp.where(even, rows_ref[0, 0:1, :], rows_ref[0, 1:2, :]), rows)
    message_ref[:cases, :] = to_other_ref[...]
    message_ref[cases:2 * cases, :] = mm(high, place).astype(BF16)
    message_ref[2 * cases:3 * cases, :] = mm(low, place).astype(BF16)
    message_ref[3 * cases:, :] = mm_t(place, from_other).astype(BF16)


def inverse_kernel(first_pair_ref, inverse_hbm, diag_hbm, up_hbm,
                   inverse_ref, factor_ref, plain_ref, blocks_ref, sems):
    size = diag_hbm.shape[1]
    cases = first_pair_ref.shape[0] - size
    copies = copy_all(
        [
            (diag_hbm, blocks_ref.at[0:1]),
            (up_hbm, blocks_ref.at[1:2]),
            (inverse_hbm, inverse_ref),
        ],
        sems,
    )
    parts = first_pair_ref[cases:, :].astype(F32)
    up_left = parts[:, :size] + (parts[:, size:2 * size] + parts[:, 2 * size:3 * size])
    for copy in copies[:2]:
        copy.wait()
    last = position() == lax.axis_size("grp") * lax.axis_size("sub") - 1
    up = jnp.where(last, 0.0, blocks_ref[1])
    diag = blocks_ref[0]
    row = lax.broadcasted_iota(jnp.int32, (size, size), 0)
    lane = lax.broadcasted_iota(jnp.int32, (size, size), 1)
    identity = (row == lane).astype(F32)
    factor = reduce_rows([jnp.concatenate([diag, jnp.transpose(up_left), up, identity], axis=1)])[0]
    odd = jnp.concatenate([jnp.transpose(up), factor[:, size:3 * size], jnp.zeros((size, size), F32)], axis=1)
    even = jnp.concatenate([diag, up, jnp.zeros((size, 2 * size), F32)], axis=1)
    plain_ref[...] = jnp.where(is_even(), even, odd)
    lanes = lax.broadcasted_iota(jnp.int32, factor.shape, 1)
    factor_ref[...] = jnp.where(lanes >= 3 * size, factor, 0.0)
    for copy in copies[2:]:
        copy.wait()


def residual_kernel(known_ref, operator_ref, rows_ref, sent_ref, other_ref, loaded_ref, r_ref, rb_ref, to_pair_ref, halo_ref):
    cases, rows = known_ref.shape
    margin = rows_ref.shape[2]
    even = is_even()
    from_other = jnp.where(even, operator_ref[:, rows:rows + margin], operator_ref[:, rows + margin:])
    r = known_ref[...] - mm_nt(other_ref[:cases, :], from_other)
    r_ref[...] = r
    rounded = r.astype(BF16)
    rb_ref[...] = rounded
    place = place_matrix(jnp.where(even, rows_ref[0, 1:2, :], rows_ref[0, 0:1, :]), rows)
    to_pair_ref[...] = mm(rounded, place).astype(BF16)
    offered = other_ref[cases:2 * cases, :].astype(F32) + other_ref[2 * cases:3 * cases, :].astype(F32)
    halo_ref[...] = (offered - mm_nt(sent_ref[...], other_ref[3 * cases:, :])).astype(BF16)


def own_local_kernel(rb_ref, inverse_ref, basis_ref, halo_ref, local_ref, coarse_ref):
    even = is_even()
    me = position()
    exists = (me > 0) & (me < lax.axis_size("grp") * lax.axis_size("sub") - 1)
    halo = jnp.where(exists, halo_ref[...], jnp.zeros_like(halo_ref))
    zero = jnp.zeros_like(halo)
    extended = jnp.concatenate([jnp.where(even, halo, zero), rb_ref[...], jnp.where(even, zero, halo)], axis=1)
    local_ref[...] = mm(extended, inverse_ref[0])
    coarse_ref[...] = mm_nt(basis_ref[0], extended)


def local_kernel(own_local_ref, own_coarse_ref, inverse_ref, basis_ref, factor_ref, plain_ref, pair_ref,
                 local_ref, message_ref):
    margin = pair_ref.shape[1]
    even = is_even()
    pair = pair_ref[...]
    total = inverse_ref.shape[1]
    ends = jnp.where(even, basis_ref[0, :, total - margin:], basis_ref[0, :, :margin])
    coarse_in = own_coarse_ref[...] + mm_nt(ends, pair)
    size = coarse_in.shape[0]
    stacked = jnp.concatenate([jnp.zeros((3 * size, coarse_in.shape[1]), F32), coarse_in], axis=0)
    reduced = jnp.dot(factor_ref[...], stacked, precision=lax.Precision.HIGHEST, preferred_element_type=F32)
    right_side = jnp.where(even, coarse_in, reduced)
    message = jnp.concatenate([plain_ref[:, :3 * size], right_side], axis=1)
    message_ref[...] = message
    rows = jnp.where(even, inverse_ref[0, total - margin:, :], inverse_ref[0, :margin, :])
    local_ref[...] = own_local_ref[...] + mm(pair, rows)


def return_kernel(local_ref, basis_pair_ref, basis_other_ref, rows_ref, to_pair_ref, to_other_ref):
    cases = local_ref.shape[0]
    margin = rows_ref.shape[2]
    even = is_even()
    local = local_ref[...]
    left, right = rows_ref[0, 0:1, :], rows_ref[0, 1:2, :]
    to_pair_ref[:cases, :] = return_rows(local, margin, jnp.where(even, right, left), jnp.logical_not(even))
    to_pair_ref[cases:, :] = basis_pair_ref[...]
    to_other_ref[:cases, :] = return_rows(local, margin, jnp.where(even, left, right), even)
    to_other_ref[cases:, :] = basis_other_ref[...]


def return_rows(local, margin, rows, head):
    owned = local.shape[1] - 2 * margin
    rounded = local.astype(BF16)
    tail = jnp.where(head, rounded[:, :margin], rounded[:, margin + owned:])
    return jnp.concatenate([tail, mm(rounded[:, margin:margin + owned], place_matrix(rows, owned)).astype(BF16)], axis=1)


def reduce_rows(blocks):
    size, width = blocks[0].shape
    panel = 16 if len(blocks) == 1 else 8 if len(blocks) == 2 else 4
    lanes, tile = 128, 8
    here = lax.broadcasted_iota(jnp.int32, (tile, 1), 0)
    tiles = range(size // tile)
    blocks = [[block[t * tile:(t + 1) * tile, :] for t in tiles] for block in blocks]

    def wide(value):
        return jnp.concatenate([value] * (width // lanes), axis=1)

    for first in range(0, size, panel):
        panels = [
            [[jnp.broadcast_to(rows[:, q:q + 1], (tile, lanes)) for rows in block] for q in range(first, first + panel)]
            for block in blocks
        ]
        for a in range(panel):
            at, inside = divmod(first + a, tile)
            for block, columns in zip(blocks, panels):
                column = columns[a]
                inverse = 1.0 / column[at][inside:inside + 1, :]
                for b in range(a + 1, panel):
                    entry = columns[b][at][inside:inside + 1, :] * inverse
                    columns[b] = [
                        jnp.where(here == inside, entry, columns[b][t] - column[t] * entry)
                        if t == at else columns[b][t] - column[t] * entry
                        for t in tiles
                    ]
                row = block[at][inside:inside + 1, :] * wide(inverse)
                for t in tiles:
                    rest = block[t] - wide(column[t]) * row
                    block[t] = jnp.where(here == inside, row, rest) if t == at else rest
    return [jnp.concatenate(block, axis=0) for block in blocks]


def shares(top, bottom, size):
    lanes = 4 * size
    lane = lax.broadcasted_iota(jnp.int32, (size, lanes), 1)

    def placed(product, slot, empty):
        first = product[:, :lanes]
        diag = pltpu.roll(first, lanes - slot * size, axis=1)
        first = jnp.where(lane < size, diag, jnp.where((lane >= empty * size) & (lane < (empty + 1) * size), 0.0, first))
        return jnp.concatenate([first, product[:, lanes:]], axis=1)

    return placed(top, 1, 1), placed(bottom, 2, 2)


def exact_product(left, right):
    a, b, c = split_three(left)
    x, y, z = split_three(right)
    return mm(jnp.concatenate([a, a, b, a, b, c], axis=1), jnp.concatenate([x, y, x, z, y, x], axis=0))


def schur(block, solved, size):
    couplings = jnp.transpose(block[:, :4 * size])[size:3 * size]
    product = -exact_product(couplings, solved)
    return shares(product[:size], product[size:], size)


def first_schur(previous, block, size):
    couplings = jnp.concatenate([previous[:, size:2 * size], block[:, :size]], axis=0)
    product = -exact_product(couplings, block)
    return shares(product[:size], product[size:], size)


def own_part(block, size):
    lane = lax.broadcasted_iota(jnp.int32, block.shape, 1)
    return jnp.where((lane >= size) & (lane < 3 * size), 0.0, block)


def combine(chain, parts, step, size):
    for i in range(0, len(chain), 2 * step):
        total = own_part(chain[i], size)
        if i + step in parts:
            total = total + parts[i + step][0]
        if i - step in parts:
            total = total + parts[i - step][1]
        chain[i] = total


def eliminate(chain, size, keep, step=1):
    count = len(chain) - 1
    while step < count:
        inner = list(range(step, count, 2 * step))
        solved = dict(zip(inner, reduce_rows([chain[j] for j in inner])))
        parts = {j: schur(chain[j], solved[j], size) for j in inner}
        for j in inner:
            keep(j, solved[j])
        combine(chain, parts, step, size)
        step = 2 * step
    return chain[0], chain[count]


def back(solved, left, right, size, alone=None):
    zero = jnp.zeros_like(left)
    stacked = jnp.concatenate([zero, left, right, zero], axis=0)
    alone = solved if alone is None else alone
    return alone - jnp.dot(
        solved[:, :4 * size], stacked, precision=lax.Precision.HIGHEST, preferred_element_type=F32)


def padded(count):
    total = 1
    while total < count:
        total = 2 * total
    return total


def group_kernel(*refs):
    *received, solved_ref, message_ref, blocks_ref = refs
    half = len(received) // 2
    size, width = received[0].shape
    members = 2 * half
    member = lax.axis_index("sub")
    for d in range(half):
        blocks_ref[member ^ (2 * d)] = received[d][...]
        blocks_ref[member ^ (2 * d + 1)] = received[half + d][...]
    chain = [blocks_ref[j] for j in range(members)]
    chain.append(jnp.zeros((size, width), F32))

    def keep(j, solved):
        solved_ref[j] = solved

    parts = {}
    for j in range(1, members, 2):
        keep(j, chain[j])
        parts[j] = first_schur(chain[j - 1], chain[j], size)
    combine(chain, parts, 1, size)
    head, tail = eliminate(chain, size, keep, 2)
    message_ref[:size, :] = head
    message_ref[size:2 * size, :] = tail
    lane = lax.broadcasted_iota(jnp.int32, (size, width), 1)
    step = members // 2
    at = step
    whole = solved_ref[at]
    zero = jnp.zeros((size, width), F32)
    while at < members - 1:
        step = step // 2
        at = at + step
        block = solved_ref[at]
        stacked = jnp.concatenate([zero, whole, zero, zero], axis=0)
        through = jnp.dot(
            block[:, :4 * size], stacked, precision=lax.Precision.HIGHEST, preferred_element_type=F32)
        whole = jnp.where((lane >= size) & (lane < 2 * size), 0.0, block) - through
    message_ref[2 * size:, :] = whole


def compose_kernel(solved_ref, rows_ref, maps_ref, place_ref, all_ref):
    rows = jnp.concatenate([rows_ref[0, 0:1, :], rows_ref[0, 1:2, :]], axis=1)
    place_ref[...] = place_matrix(rows, place_ref.shape[0])
    members, size, width = solved_ref.shape
    lane = lax.broadcasted_iota(jnp.int32, (size, width), 1)
    row = lax.broadcasted_iota(jnp.int32, (size, width), 0)
    maps = {0: -(lane == row + size).astype(F32), members: -(lane == row + 2 * size).astype(F32)}
    step = members // 2
    while step >= 1:
        for j in range(step, members, 2 * step):
            block = solved_ref[j]
            maps[j] = back(block, maps[j - step], maps[j + step], size, own_part(block, size))
        step = step // 2
    for j in range(members + 1):
        all_ref[j] = maps[j]
    member = lax.axis_index("sub")
    maps_ref[0] = all_ref[jnp.maximum(member - 1, 0)]
    maps_ref[1] = all_ref[member]
    maps_ref[2] = all_ref[member + 1]


def solve_kernel(*refs):
    (*received, maps_ref, local_ref, basis_ref, place_ref, pair_ref, other_ref, r_ref, diag_ref, operator_ref,
     p_ref, image_ref, sums_ref, messages_ref, sep_ref) = refs
    groups = len(received)
    size, width = received[0].shape
    size = size // 3
    for d in range(groups):
        messages_ref[lax.axis_index("grp") ^ d] = received[d][...]
    chain = []
    for g in range(groups):
        total = messages_ref[g, :size, :]
        if g:
            total = total + messages_ref[g - 1, size:2 * size, :]
        chain.append(total)
    count = padded(groups)
    row = lax.broadcasted_iota(jnp.int32, (size, width), 0)
    lane = lax.broadcasted_iota(jnp.int32, (size, width), 1)
    while len(chain) < count:
        chain.append((row == lane).astype(F32))
    chain.append(jnp.zeros((size, width), F32))
    factors = {}
    head, _ = eliminate(chain, size, factors.__setitem__)
    solution = {count: jnp.zeros((size, width), F32)}
    solution[0] = reduce_rows([head])[0]
    step = count // 2
    while step >= 1:
        for j in range(step, count, 2 * step):
            solution[j] = back(factors[j], solution[j - step], solution[j + step], size)
        step = step // 2
    for g in range(groups):
        sep_ref[g] = solution[g]
    sep_ref[groups] = jnp.zeros((size, width), F32)
    group, member = lax.axis_index("grp"), lax.axis_index("sub")
    first, after = sep_ref[group], sep_ref[group + 1]
    before = jnp.maximum(group - 1, 0)
    is_first = member == 0
    left_map = jnp.where(is_first, messages_ref[before, 2 * size:, :], maps_ref[0])
    left_solution = back(
        left_map, jnp.where(is_first, sep_ref[before], first), jnp.where(is_first, first, after), size)
    own_solution = back(maps_ref[1], first, after, size)
    right_solution = back(maps_ref[2], first, after, size)

    def lifted(solution, basis):
        return mm_t(solution.astype(BF16), basis)[3 * size:]

    cases = local_ref.shape[0]
    margin = place_ref.shape[1] // 2
    owned = p_ref.shape[1]
    even = is_even()
    pair, other = pair_ref[...], other_ref[...]
    left, right = jnp.where(even, other, pair), jnp.where(even, pair, other)
    left = left[:cases].astype(F32) + lifted(left_solution, left[cases:])
    right = right[:cases].astype(F32) + lifted(right_solution, right[cases:])
    correction = local_ref[...] + lifted(own_solution, basis_ref[0])
    tails = jnp.concatenate([left[:, :margin], right[:, :margin]], axis=1).astype(BF16)
    p = correction[:, margin:margin + owned] + mm_nt(tails, place_ref[...])
    p_ref[...] = p
    me = position()
    last = lax.axis_size("grp") * lax.axis_size("sub") - 1
    left = jnp.where(me == 0, 0.0, left[:, margin:] + correction[:, :margin]).astype(BF16)
    right = jnp.where(me == last, 0.0, right[:, margin:] + correction[:, margin + owned:]).astype(BF16)
    values = jnp.concatenate([p.astype(BF16), left, right], axis=1)
    image = diag_ref[...].reshape(1, owned) * p + mm_nt(values, operator_ref[...])
    image_ref[...] = image
    inner = row_sum(r_ref[...] * p)
    curvature = row_sum(p * image)
    sums = jnp.concatenate([inner[0:1], curvature[0:1]], axis=0)
    for slot in range(sums_ref.shape[0]):
        sums_ref[slot] = sums


def row_sum(values):
    lanes = 128
    total = values[:, :lanes]
    for start in range(lanes, values.shape[1], lanes):
        total = total + values[:, start:start + lanes]
    return mm_nt(jnp.ones((8, lanes), F32), total, precision=lax.Precision.HIGHEST)


def finish_kernel(x_ref, p_ref, r_ref, image_ref, sums_ref, out_x_ref, out_r_ref):
    sums = jnp.sum(sums_ref[...], axis=0)
    row = sums[0:1, :] / sums[1:2, :]
    lanes = 128
    step = jnp.transpose(jnp.broadcast_to(row, (lanes, row.shape[1])))
    for start in range(0, x_ref.shape[1], lanes):
        span = slice(start, start + lanes)
        out_x_ref[:, span] = x_ref[:, span] + step * p_ref[:, span]
        out_r_ref[:, span] = r_ref[:, span] - step * image_ref[:, span]


def call(kernel, out, in_specs, scratch=()):
    return pl.pallas_call(
        kernel,
        out_shape=out,
        in_specs=in_specs,
        out_specs=[VMEM] * len(out),
        scratch_shapes=list(scratch),
        compiler_params=pltpu.CompilerParams(vmem_limit_bytes=16 * 2**20),
    )


def far(*arrays):
    return [pltpu.with_memory_space_constraint(array, pltpu.HBM) for array in arrays]


def struct(shape, dtype):
    return jax.ShapeDtypeStruct(shape, dtype)


def shards(right_side, iterate_in, diagonal, block_values, block_cols, couple_left, couple_right, send_rows,
           local_inverse, coarse_basis, coarse_diag, coarse_up):
    groups, members = lax.axis_size("grp"), lax.axis_size("sub")
    total = groups * members
    rows, cases = right_side.shape
    margin = send_rows.shape[2]
    extended = local_inverse.shape[1]
    modes = coarse_basis.shape[2]
    width = 3 * modes + cases
    pairs = [(i, i ^ 1) for i in range(total)]
    others = [(i, i + 1 if i % 2 else i - 1) for i in range(1, total - 1)]
    right_side, iterate_in = right_side.T, iterate_in.T
    basis = jnp.swapaxes(coarse_basis, 1, 2)
    block_cols = jnp.transpose(block_cols, (2, 0, 1))

    halo = struct((cases, margin), BF16)
    full = struct((cases, rows), F32)
    semaphores = pltpu.SemaphoreType.DMA
    to_pair, to_other, basis_pair, basis_other, start, send_rows, basis, loads, diag, operator = call(
        load_kernel,
        [
            struct((cases + modes, margin), BF16),
            halo,
            struct((modes, 2 * margin), BF16),
            struct((modes, 2 * margin), BF16),
            full,
            struct(send_rows.shape, send_rows.dtype),
            struct(basis.shape, BF16),
            full,
            struct(diagonal.shape, F32),
            struct((rows, rows + 2 * margin), BF16),
        ],
        [HBM] * 10,
        [
            pltpu.VMEM(coarse_up.shape, F32),
            pltpu.SMEM(block_cols.shape, block_cols.dtype),
            pltpu.VMEM(block_values.shape, BF16),
            semaphores((10,)),
        ],
    )(*far(
        iterate_in, send_rows, coarse_up, basis, right_side, diagonal, block_values, block_cols, couple_left, couple_right
    ))
    first_pair = lax.ppermute(to_pair, AXES, pairs)
    (partial,) = call(own_kernel, [full], [VMEM] * 4)(start, loads, diag, operator)
    known, message = call(offer_kernel, [full, struct((3 * cases + margin, margin), BF16)], [VMEM] * 5)(
        partial, operator, send_rows, first_pair, to_other
    )
    first_other = lax.ppermute(message, AXES, others)
    inverse, factor, plain = call(
        inverse_kernel,
        [struct(local_inverse.shape, BF16), struct((modes, 4 * modes), F32), struct((modes, 4 * modes), F32)],
        [VMEM] + [HBM] * 3,
        [pltpu.VMEM((2, modes, modes), F32), semaphores((3,))],
    )(first_pair, *far(local_inverse, coarse_diag, coarse_up))
    residual, rounded, to_pair, other_halo = call(
        residual_kernel, [full, struct((cases, rows), BF16), halo, halo], [VMEM] * 6
    )(known, operator, send_rows, to_other, first_other, plain)
    pair_halo = lax.ppermute(to_pair, AXES, pairs)
    local, coarse = call(own_local_kernel, [struct((cases, extended), F32), struct((modes, cases), F32)], [VMEM] * 4)(
        rounded, inverse, basis, other_halo
    )
    chips = members // 2
    local, message = call(
        local_kernel, [struct((cases, extended), F32), struct((modes, width), F32)], [VMEM] * 7
    )(local, coarse, inverse, basis, factor, plain, pair_halo)
    returned = struct((cases + modes, 2 * margin), BF16)
    to_pair, to_other = call(return_kernel, [returned, returned], [VMEM] * 4)(local, basis_pair, basis_other, send_rows)
    from_other = lax.ppermute(to_other, AXES, others)
    from_pair = lax.ppermute(to_pair, AXES, pairs)

    def partners(value, stride, count):
        swaps = [[(i, i ^ (stride * d)) for i in range(total)] for d in range(1, count)]
        return [value] + [lax.ppermute(value, AXES, swap) for swap in swaps]

    same = partners(message, 2, chips)
    opposite = [lax.ppermute(same[0], AXES, pairs)]
    opposite += [lax.ppermute(value, AXES, pairs) for value in same[1:]]
    block = pltpu.VMEM((members, modes, width), F32)
    solved, reduced = call(
        group_kernel,
        [struct((members, modes, width), F32), struct((3 * modes, width), F32)],
        [VMEM] * members,
        [block],
    )(*same, *opposite)
    reduced = partners(reduced, members, groups)
    maps, place = call(
        compose_kernel,
        [struct((3, modes, width), F32), struct((rows, 2 * margin), BF16)],
        [VMEM] * 2,
        [pltpu.VMEM((members + 1, modes, width), F32)],
    )(solved, send_rows)
    direction, image, sums = call(
        solve_kernel,
        [full, full, struct((total, 2, cases), F32)],
        [VMEM] * (groups + 9),
        [pltpu.VMEM((groups, 3 * modes, width), F32), pltpu.VMEM((groups + 1, modes, width), F32)],
    )(*reduced, maps, local, basis, place, from_pair, from_other, residual, diag, operator)
    sums = lax.all_to_all(sums, AXES, 0, 0, tiled=True)
    iterate, residual = call(finish_kernel, [full, full], [VMEM] * 5)(start, direction, residual, image, sums)
    return iterate.T, residual.T


def solution(mesh):
    def spec(rank):
        return P(AXES, *([None] * (rank - 1)))

    return jax.shard_map(
        shards,
        mesh=mesh,
        in_specs=tuple(spec(rank) for rank in (2, 2, 1, 5, 3, 2, 2, 3, 3, 3, 3, 3)),
        out_specs=(spec(2), spec(2)),
        check_vma=False,
    )
```
